256 devices in a mesh: ctx: 32 (over x, z), tp: 8 (over y, core).
Axes of the slice: x: 4, y: 4, z: 8, core: 2. Of those that a mesh axis runs over, the one named last changes fastest.
Arguments:
- tokens: int32 [8192], P('ctx'), may hold values from 0 to 3
- rc_map: int32 [4], replicated, may hold values from 0 to 3, each once
- embedding: bfloat16 [4, 2048], replicated, may hold values from -6 to 6
- norm_gain: float32 [2048], replicated, may hold values from 0.5 to 1.5
- w_values: bfloat16 [2048, 4096], P(None, 'tp'), may hold values from -0.125 to 0.125
- w_gates: bfloat16 [2048, 4096], P(None, 'tp'), may hold values from -0.125 to 0.125
- w_states: bfloat16 [2048, 256], replicated, may hold values from -0.125 to 0.125
- w_steps: bfloat16 [2048, 32], P(None, 'tp'), may hold values from -0.125 to 0.125
- conv_values: float32 [4, 4096], P(None, 'tp'), may hold values from -0.5 to 0.5
- conv_states: float32 [4, 256], replicated, may hold values from -0.5 to 0.5
- step_bias: float32 [32], P('tp'), may hold values from -1 to 1
- log_rate: float32 [32], P('tp'), as said below
- skip_gain: float32 [32], P('tp'), may hold values from 0.5 to 1.5
- head_gain: float32 [4096], P('tp'), may hold values from 0.5 to 1.5
- cotangent: bfloat16 [8192, 4096], P('ctx', 'tp'), may hold values from -6 to 6
Outputs:
- encoded: bfloat16 [8192, 4096], P('ctx', 'tp')
- grad_log_rate: float32 [32], replicated
- grad_step_bias: float32 [32], replicated
- grad_conv_states: float32 [4, 256], replicated
The draws below stay inside these ranges and needn't reach their ends.
Inputs may be any that keep to these rules, and one draw needn't show every extreme that they name: `rc_map`: a permutation of the four ids. exp(log_rate) lies between 0.3 / 8192 and 0.1.
All inputs are finite; a program needn't handle non-finite values.
Results may differ from the reference program's by a relative error of at most 0.001.
The reference program's roundings to bfloat16 on the way (of `normed`) count: a program that leaves them out, or rounds other values in their place, can miss the bound.
Values sent between devices are 32-bit elements; how exact they have to be, the bound alone decides.
A program may use at most 128 MiB of HBM per device.

```python
import math
import jax
import jax.numpy as jnp
from jax import lax

D = 2048
H = 32
HEAD = 128
STATE = 128
GROUP = 256
CONV = 4
DI = 4096
TOKENS = 8192


def draw_log_rate(key, part):
    key_kind, key_slow, key_fast = jax.random.split(jax.random.fold_in(key, 11), 3)
    slow_share = 0.5
    slow_mask = jax.random.uniform(key_kind, (H,)) < slow_share
    slow_logs = jax.random.uniform(key_slow, (H,), minval=jnp.log(0.3), maxval=jnp.log(2.0)) - jnp.log(1.0 * TOKENS)
    fast_logs = jax.random.uniform(key_fast, (H,), minval=jnp.log(0.03), maxval=jnp.log(0.1))
    return jnp.where(slow_mask, slow_logs, fast_logs).astype(jnp.float32)


def set_ends(drawn, own_key, low, high):
    dims = drawn.shape
    index_at = [jax.random.randint(jax.random.fold_in(own_key, axis), (), 0, dims[axis]) for axis in range(len(dims))]
    drawn = drawn.at[tuple(index_at)].set(low)
    longest = dims.index(max(dims))
    index_at[longest] = (index_at[longest] + 1) % dims[longest]
    return drawn.at[tuple(index_at)].set(high)


def levels(key, dims, pieces, smallest, largest):
    gain = 1.0
    for dim, parts in pieces:
        steps = jax.random.uniform(jax.random.fold_in(jax.random.fold_in(key, 6), dim), (parts,), jnp.float32, smallest / len(pieces), largest / len(pieces))
        gain = gain * jnp.repeat(jnp.exp(steps), dims[dim] // parts).reshape((-1,) + (1,) * (len(dims) - 1 - dim))
    return gain


def normal_values(rng, shape, spread, most, shards=(), kind=jnp.bfloat16):
    entries = jax.random.normal(rng, shape, jnp.float32) * spread
    if len(shards) > 0:
        entries = levels(rng, shape, shards, -0.22, 0.18) * entries
    return jnp.clip(entries, min=-most, max=most).astype(kind)


def setup_inputs(seed: int = 0) -> dict:
    splits = jax.random.split(jax.random.key(seed), 16)
    tokens = set_ends(jax.random.randint(splits[0], (TOKENS,), 0, 4), jax.random.fold_in(splits[0], 1), 0, 3).astype(jnp.int32)
    rc_map = jax.random.permutation(splits[1], 4).astype(jnp.int32)
    embedding = normal_values(splits[2], (4, D), 1.0, 6.0)
    norm_gain = jnp.clip(1.0 + 0.1 * jax.random.normal(splits[3], (D,), jnp.float32), 0.5, 1.5)
    w_values = normal_values(splits[4], (D, DI), D ** -0.5, 0.125, ((1, 8),))
    w_gates = normal_values(splits[5], (D, DI), D ** -0.5, 0.125, ((1, 8),))
    w_states = normal_values(splits[6], (D, 2 * STATE), D ** -0.5, 0.125)
    w_steps = normal_values(splits[7], (D, H), D ** -0.5, 0.125, ((1, 8),))
    conv_values = jnp.clip(jax.random.uniform(splits[8], (CONV, DI), jnp.float32, -0.5, 0.5) * levels(splits[8], (CONV, DI), ((1, 8),), -0.4, 0.0), -0.5, 0.5)
    conv_states = jnp.clip(jax.random.uniform(splits[9], (CONV, 2 * STATE), jnp.float32, -0.5, 0.5), -0.5, 0.5)
    step_bias = jnp.clip(jax.random.uniform(splits[10], (H,), jnp.float32, -1.0, 1.0) * levels(splits[10], (H,), ((0, 8),), -0.4, 0.0), -1.0, 1.0)
    log_rate = draw_log_rate(jax.random.fold_in(splits[15], 71), 0)
    skip_gain = jnp.clip(0.5 + 1.0 * jax.random.uniform(splits[12], (H,), jnp.float32) ** levels(splits[12], (H,), ((0, 8),), -0.2, 0.2), 0.5, 1.5)
    head_gain = jnp.clip(1.0 + 0.1 * jax.random.normal(splits[13], (DI,), jnp.float32), 0.5, 1.5)
    cotangent = normal_values(splits[14], (TOKENS, DI), 1.0, 6.0, ((0, 32), (1, 8)))
    return {"tokens": tokens, "rc_map": rc_map, "embedding": embedding, "norm_gain": norm_gain, "w_values": w_values, "w_gates": w_gates, "w_states": w_states, "w_steps": w_steps, "conv_values": conv_values, "conv_states": conv_states, "step_bias": step_bias, "log_rate": log_rate, "skip_gain": skip_gain, "head_gain": head_gain, "cotangent": cotangent}


epsilon = 1e-05
highest = lax.Precision.HIGHEST

def lookup(token_ids, lookup_table):
    onehot = (token_ids[:, None] == jnp.arange(4, dtype=jnp.int32)[None, :]).astype(jnp.float32)
    return jnp.dot(onehot, lookup_table, precision=highest, preferred_element_type=jnp.float32)

def group_step(carry_state, inputs):
    values, keys_b, queries_c, steps_dt, log_decay = inputs
    cumulative = jnp.cumsum(log_decay, axis=0)
    length = log_decay.shape[0]
    causal = (jnp.arange(length)[:, None] >= jnp.arange(length)[None, :])[:, :, None]
    differences = cumulative[:, None, :] - cumulative[None, :, :]
    decays = jnp.where(causal, jnp.exp(jnp.where(causal, differences, 0.0)), 0.0)
    scores = jnp.dot(queries_c, keys_b.T, precision=highest)
    mixing = scores[:, :, None] * decays * steps_dt[None, :, :]
    within = jnp.einsum('tsh,shp->thp', mixing, values, precision=highest)
    carried = jnp.exp(cumulative)[:, :, None] * jnp.einsum('tn,hnp->thp', queries_c, carry_state, precision=highest)
    end_weights = jnp.exp(cumulative[-1][None, :] - cumulative) * steps_dt
    fresh_state = jnp.einsum('sh,sn,shp->hnp', end_weights, keys_b, values, precision=highest)
    new_state = jnp.exp(cumulative[-1])[:, None, None] * carry_state + fresh_state
    return (new_state, within + carried)

def gate_norm(outputs, gate_rows, head_gain):
    own_count, head_count, head_size = outputs.shape
    gated_rows = outputs * jax.nn.silu(gate_rows).reshape(own_count, head_count, head_size)
    scaled = gated_rows * lax.rsqrt(lax.optimization_barrier(jnp.mean(gated_rows * gated_rows, axis=2, keepdims=True)) + epsilon)
    return scaled.reshape(own_count, head_count * head_size) * head_gain

def strand_output(rate_in, bias_in, conv_in, token_ids, tables, conv_values, skip_gain, head_gain):
    table_vs, table_z, table_dt = tables
    own_count = token_ids.shape[0]
    projected = lookup(token_ids, table_vs)
    padded = jnp.concatenate([jnp.zeros((CONV - 1, projected.shape[1]), jnp.float32), projected], axis=0)
    conv_weights = jnp.concatenate([conv_values, conv_in], axis=1)
    summed = sum((conv_weights[shift_tap] * padded[shift_tap:shift_tap + own_count] for shift_tap in range(CONV)))
    activated = jax.nn.silu(summed)
    inner_width = conv_values.shape[1]
    head_count = inner_width // HEAD
    values = activated[:, :inner_width].reshape(own_count, head_count, HEAD)
    keys_b = activated[:, inner_width:inner_width + STATE]
    queries_c = activated[:, inner_width + STATE:]
    steps_dt = jax.nn.softplus(lookup(token_ids, table_dt) + bias_in)
    log_decay = -jnp.exp(rate_in) * steps_dt
    blocks = own_count // GROUP

    def to_blocks(member):
        return member.reshape((blocks, GROUP) + member.shape[1:])
    zero_state = jnp.zeros((head_count, STATE, HEAD), jnp.float32)
    grouped = tuple((to_blocks(member) for member in (values, keys_b, queries_c, steps_dt, log_decay)))
    _, rows_out = lax.scan(jax.checkpoint(group_step), zero_state, grouped)
    outputs = rows_out.reshape(own_count, head_count, HEAD) + skip_gain[None, :, None] * values
    return gate_norm(outputs, lookup(token_ids, table_z), head_gain)

def reference(tokens, rc_map, embedding, norm_gain, w_values, w_gates, w_states, w_steps, conv_values, conv_states, step_bias, log_rate, skip_gain, head_gain, cotangent):
    embedded = embedding.astype(jnp.float32)
    normed = (embedded * lax.rsqrt(lax.optimization_barrier(jnp.mean(embedded * embedded, axis=1, keepdims=True)) + epsilon) * norm_gain).astype(jnp.bfloat16)
    table_vs = jnp.concatenate([jnp.dot(normed, w_values, preferred_element_type=jnp.float32), jnp.dot(normed, w_states, preferred_element_type=jnp.float32)], axis=1)
    table_z = jnp.dot(normed, w_gates, preferred_element_type=jnp.float32)
    table_dt = jnp.dot(normed, w_steps, preferred_element_type=jnp.float32)
    tables = (table_vs, table_z, table_dt)
    rc_tokens = lax.optimization_barrier(jnp.sum(jnp.where(tokens[:, None] == jnp.arange(4, dtype=jnp.int32)[None, :], rc_map[None, :], 0), axis=1)).astype(jnp.int32)

    def both_strands(rate_in, bias_in, conv_in):
        forward_rows = strand_output(rate_in, bias_in, conv_in, tokens, tables, conv_values, skip_gain, head_gain)
        reverse_rows = strand_output(rate_in, bias_in, conv_in, rc_tokens[::-1], tables, conv_values, skip_gain, head_gain)
        return forward_rows + reverse_rows[::-1]
    summed, pullback = jax.vjp(both_strands, log_rate, step_bias, conv_states)
    loss_scale = 1.0 / math.sqrt(TOKENS * HEAD)
    grads = pullback(cotangent.astype(jnp.float32) * loss_scale)
    return (summed.astype(jnp.bfloat16), grads[0], grads[1], grads[2])
```

```python
import math

import jax
import jax.numpy as jnp
from jax import lax
from jax.experimental import pallas as pl
from jax.experimental.pallas import tpu as pltpu
from jax.sharding import PartitionSpec as P

F32 = jnp.float32
BF16 = jnp.bfloat16
HEAD = 128
CONV = 4
EPS = 1e-05
MESH = pl.DeviceIdType.MESH
VM = pl.BlockSpec(memory_space=pltpu.VMEM)
SM = pl.BlockSpec(memory_space=pltpu.SMEM)


def split(v):
    hi = v.astype(BF16)
    return hi, (v - hi.astype(F32)).astype(BF16)


def dot(a, b, ca=1, cb=0):
    return lax.dot_general(a, b, (((ca,), (cb,)), ((), ())), preferred_element_type=F32)


def mm(a, b, ca=1, cb=0):
    return dot(a[0], b[0], ca, cb) + (dot(a[0], b[1], ca, cb) + dot(a[1], b[0], ca, cb))


def iota(shape, dim):
    return lax.broadcasted_iota(jnp.int32, shape, dim)


def back_one(v, fill):
    rolled = pltpu.roll(v, 1, 1)
    wrapped = pltpu.roll(rolled, 1, 0)
    moved = jnp.where(iota(v.shape, 1) == 0, wrapped, rolled)
    first = (iota(v.shape, 0) == 0) & (iota(v.shape, 1) == 0)
    return jnp.where(first, fill, moved)


def ahead_one(v, fill):
    rows, lanes = v.shape
    rolled = pltpu.roll(v, lanes - 1, 1)
    wrapped = pltpu.roll(rolled, rows - 1, 0)
    moved = jnp.where(iota(v.shape, 1) == lanes - 1, wrapped, rolled)
    last = (iota(v.shape, 0) == rows - 1) & (iota(v.shape, 1) == lanes - 1)
    return jnp.where(last, fill, moved)


def softplus(v):
    return jnp.maximum(v, 0.0) + jnp.log1p(jnp.exp(-jnp.abs(v)))


def mixer_kernel(
    place, rc, bias, log_rate, skip, tok_ref, emb_ref, ng_ref, wv_ref, wg_ref, ws_ref, wst_ref,
    cv_ref, cs_ref, hg_ref, cot_ref, enc_ref, pay_ref, fwd_ref, rev_ref, kmer_ref, rows_ref,
    *, loss_scale,
):
    me, slot = place()
    chunks = tok_ref.shape[0]
    blocks = chunks // 2
    inner = cv_ref.shape[1]
    heads = inner // HEAD
    own = cot_ref.shape[0]

    e = emb_ref[...].astype(F32)
    scale = lax.rsqrt(jnp.mean(e * e, axis=1, keepdims=True) + EPS)
    normed = (e * scale * ng_ref[...]).astype(BF16)
    normed = jnp.concatenate([normed, jnp.zeros((12, e.shape[1]), BF16)], axis=0)
    table_v = dot(normed, wv_ref[...])[0:4]
    table_s = dot(normed, ws_ref[...])[0:4]
    table_z = dot(normed, wg_ref[...])[0:4]
    table_d = dot(normed, wst_ref[...])[0:4]
    lane_h = iota((1, heads), 1)
    bias_row = jnp.zeros((1, heads), F32)
    rate_row = jnp.zeros((1, heads), F32)
    for h in range(heads):
        bias_row = jnp.where(lane_h == h, bias[h], bias_row)
        rate_row = jnp.where(lane_h == h, log_rate[h], rate_row)
    rate_row = jnp.exp(rate_row)
    pre_step = table_d + bias_row
    step_t = softplus(pre_step)
    sig_t = 1.0 / (1.0 + jnp.exp(-pre_step))
    gate_t = table_z / (1.0 + jnp.exp(-table_z))
    table_vs = jnp.concatenate([table_v, table_s], axis=1)
    taps = jnp.concatenate([cv_ref[...], cs_ref[...]], axis=1)
    tail = jnp.concatenate(
        [gate_t, step_t, sig_t, jnp.zeros((4, 128 - 2 * heads), F32)], axis=1
    )
    parts = []
    for k in range(CONV):
        rest = tail if k == CONV - 1 else jnp.zeros_like(tail)
        parts.append(jnp.concatenate([table_vs * taps[k : k + 1], rest], axis=1))
    per_tap = jnp.concatenate(parts, axis=0)
    p_hi = per_tap.astype(BF16)
    p_rest = per_tap - p_hi.astype(F32)
    p_mid = p_rest.astype(BF16)
    p_low = (p_rest - p_mid.astype(F32)).astype(BF16)
    per_tap3 = jnp.concatenate([p_hi, p_mid, p_low], axis=0)

    tok = tok_ref[...].astype(F32)
    comp = jnp.zeros_like(tok)
    for a in range(4):
        comp = jnp.where(tok == a, rc[a].astype(F32), comp)
    f_shift, r_shift = [tok], [comp]
    for _ in range(CONV - 1):
        f_shift.append(back_one(f_shift[-1], -1.0))
        r_shift.append(ahead_one(r_shift[-1], -1.0))
    for d in range(CONV):
        fwd_ref[d] = f_shift[d]
        rev_ref[d] = r_shift[d]

    row = iota(tok.shape, 0)
    position = row * 128 + iota(tok.shape, 1)
    before = row < 2 * me
    outside = before | (row >= 2 * me + 2)
    kmer_f = f_shift[0] + 4.0 * f_shift[1] + 16.0 * f_shift[2] + 64.0 * f_shift[3]
    kmer_r = r_shift[0] + 4.0 * r_shift[1] + 16.0 * r_shift[2] + 64.0 * r_shift[3]
    kmer = jnp.where(before, kmer_f, kmer_r)
    edge = (before & (position < CONV - 1)) | (position >= chunks * 128 - (CONV - 1))
    kmer_ref[...] = jnp.where(edge & outside, -1.0, kmer)
    mixed = jnp.where(outside, jnp.where(before, tok, comp), -1.0)
    tri = (iota((128, 128), 0) <= iota((128, 128), 1)).astype(BF16)
    ones = jnp.ones((128, 128), BF16)
    strict = (iota((chunks, chunks), 1) < iota((chunks, chunks), 0)).astype(BF16)
    counts = []
    for a in range(4):
        hit = (mixed == a).astype(F32)
        hit16 = hit.astype(BF16)
        within = dot(hit16, tri)
        offset = dot(strict, dot(hit16, ones).astype(BF16))
        total_f = jnp.sum(jnp.where(before, hit, 0.0), keepdims=True)
        inclusive = within + offset - total_f
        counts.append(jnp.where(before, -inclusive, inclusive - hit))
    for h in range(heads):
        steps_sum = sum(counts[a] * step_t[a : a + 1, h : h + 1] for a in range(4))
        sig_sum = sum(counts[a] * sig_t[a : a + 1, h : h + 1] for a in range(4))
        exponent = -(rate_row[:, h : h + 1] * steps_sum)
        decay = jnp.where(outside, jnp.exp(exponent), 0.0)
        for q, value in enumerate((decay, decay * exponent, decay * sig_sum)):
            base = (q * heads + h) * chunks
            rows_ref[base : base + chunks, :] = value
    for q in range(3 * heads, 16):
        rows_ref[q * chunks : (q + 1) * chunks, :] = jnp.zeros((chunks, 128), F32)

    kmer_id = iota((256, 128), 0).astype(F32)

    def load_rows(chunk):
        return rows_ref[pl.ds(chunk, 16, stride=chunks), :]

    def one_hot(chunk):
        return (jnp.broadcast_to(kmer_ref[pl.ds(chunk, 1), :], (256, 128)) == kmer_id).astype(F32)

    def add_block(i, acc):
        weights = jnp.concatenate([load_rows(2 * i), load_rows(2 * i + 1)], axis=1)
        w_f = split(jnp.where(i < me, weights, 0.0))
        w_r = split(jnp.where(i > me, weights, 0.0))
        stacked = jnp.concatenate([w_f[0], w_f[1], w_r[0], w_r[1]], axis=0)
        hits = jnp.concatenate([one_hot(2 * i), one_hot(2 * i + 1)], axis=1).astype(BF16)
        return acc + dot(hits, stacked, 1, 1)

    acc = lax.fori_loop(0, blocks, add_block, jnp.zeros((256, 64), F32), unroll=4)
    lane = iota((16, 128), 1)
    e_f = split(jnp.where(lane < CONV - 1, load_rows(0), 0.0))
    e_r = split(jnp.where(lane >= 128 - (CONV - 1), load_rows(chunks - 1), 0.0))
    edge_rows = jnp.concatenate(
        [e_f[0], e_f[1], e_r[0], e_r[1]], axis=0
    )
    pick_row = iota((16, 128), 0)
    pick = (lane == jnp.where(pick_row < 8, pick_row, pick_row + 112)).astype(BF16)
    acc = jnp.concatenate([acc, dot(pick, edge_rows, 1, 1)], axis=0)
    sources_f = acc[:, 0:16] + acc[:, 16:32]
    sources_r = acc[:, 32:48] + acc[:, 48:64]

    def local_row(ref, d):
        pair = ref[d, pl.ds(2 * me, 2), :]
        return jnp.concatenate([pair[0:1], pair[1:2]], axis=1)

    hits_t = []
    for k in range(CONV):
        d = CONV - 1 - k
        lanes1 = iota((1, 128), 1)
        ends = jnp.where(
            lanes1 < 64, fwd_ref[d, 0:1, :], rev_ref[d, chunks - 1 : chunks, :]
        )
        line = jnp.concatenate([local_row(fwd_ref, d), local_row(rev_ref, d), ends], axis=1)
        hits_t.append(
            (jnp.broadcast_to(line, (4, line.shape[1])) == iota((4, line.shape[1]), 0).astype(F32))
        )
    hits_t = jnp.concatenate([h.astype(F32) for h in hits_t], axis=0)
    hits3_t = jnp.concatenate([hits_t, hits_t, hits_t], axis=0).astype(BF16)
    local_sum = dot(hits3_t, per_tap3, 0, 0)
    column = iota((256, 48), 1) % 16
    digit = lax.shift_right_logical(iota((256, 48), 0), 2 * (3 - column // 4)) & 3
    kmer_hits = (digit == column % 4).astype(F32).astype(BF16)
    kmer_sum = dot(kmer_hits, per_tap3)
    ends_sum = jnp.concatenate([local_sum[512:520], local_sum[632:640]], axis=0)
    kmer_sum = jnp.concatenate([kmer_sum, ends_sum], axis=0)

    def silu(v):
        return v / (1.0 + jnp.exp(-v))

    def silu_slope(v):
        s = 1.0 / (1.0 + jnp.exp(-v))
        return s + v * s * (1.0 - s)

    width = inner + 2 * HEAD
    kx = silu(kmer_sum[:, :inner])
    kb = silu(kmer_sum[:, inner : inner + HEAD])
    k_steps = kmer_sum[:, width + inner : width + inner + 128]
    kx_s = [split(kx[:, h * HEAD : (h + 1) * HEAD]) for h in range(heads)]
    kb_s = split(kb)

    tri_in = (iota((own, own), 0) <= iota((own, own), 1)).astype(BF16)
    tri_out = (iota((own, own), 0) >= iota((own, own), 1)).astype(BF16)
    pad4 = jnp.zeros((12, own), BF16)
    hits_f = hits_t[12:16, 0:own].astype(BF16)
    hits_r = hits_t[12:16, own : 2 * own].astype(BF16)
    n_f = dot(jnp.concatenate([hits_f, pad4], axis=0), tri_in)
    n_r = dot(jnp.concatenate([hits_r, pad4], axis=0), tri_out)
    cum_rows, sig_rows, step_rows, own_sig = [], [], [], []
    for counted, hit in ((n_f, hits_t[12:16, 0:own]), (n_r, hits_t[12:16, own : 2 * own])):
        for h in range(heads):
            steps_sum = sum(counted[a : a + 1] * step_t[a : a + 1, h : h + 1] for a in range(4))
            cum_rows.append(-(rate_row[:, h : h + 1] * steps_sum))
            sig_rows.append(
                sum(counted[a : a + 1] * sig_t[a : a + 1, h : h + 1] for a in range(4))
            )
            step_rows.append(sum(hit[a : a + 1] * step_t[a : a + 1, h : h + 1] for a in range(4)))
            own_sig.append(sum(hit[a : a + 1] * sig_t[a : a + 1, h : h + 1] for a in range(4)))
    stack = jnp.concatenate(
        cum_rows + sig_rows + [jnp.zeros((128 - 4 * heads, own), F32)], axis=0
    )
    columns = jnp.transpose(stack)

    cot = cot_ref[...].astype(F32) * loss_scale
    gain = hg_ref[...]
    encoded = jnp.zeros((own, inner), F32)
    d_kb = jnp.zeros(kb.shape, F32)
    rate_grads = [jnp.zeros((1, 1), F32)] * heads
    bias_grads = [jnp.zeros((1, 1), F32)] * heads
    tap_sums = jnp.zeros((16, 2 * HEAD), F32)

    def total(v):
        return jnp.sum(v, keepdims=True)

    for strand in range(2):
        summed = local_sum[strand * own : (strand + 1) * own]
        sources = (sources_f, sources_r)[strand]
        x = silu(summed[:, :inner])
        states = silu(summed[:, inner:width])
        gates = summed[:, width : width + inner]
        b_s = split(states[:, :HEAD])
        c = states[:, HEAD:]
        c_s = split(c)
        scores = mm(c_s, b_s, 1, 1)
        if strand == 0:
            causal = iota((own, own), 0) >= iota((own, own), 1)
        else:
            causal = iota((own, own), 0) <= iota((own, own), 1)
        d_scores = jnp.zeros((own, own), F32)
        d_c = jnp.zeros((own, HEAD), F32)
        for h in range(heads):
            n = strand * heads + h
            part = slice(h * HEAD, (h + 1) * HEAD)
            w0 = k_steps[:, h : h + 1] * sources[:, h : h + 1]
            w1 = k_steps[:, h : h + 1] * sources[:, heads + h : heads + h + 1]
            rate = rate_row[:, h : h + 1]
            w2 = (
                k_steps[:, heads + h : heads + h + 1] * sources[:, h : h + 1]
                - rate * k_steps[:, h : h + 1] * sources[:, 2 * heads + h : 2 * heads + h + 1]
            )
            start_s = split(mm(kb_s, split(kx[:, part] * w0), 0, 0))
            cum_c = columns[:, n : n + 1]
            sig_c = columns[:, 2 * heads + n : 2 * heads + n + 1]
            cum_r, sig_r, step_r = cum_rows[n], sig_rows[n], step_rows[n]
            decays = jnp.where(causal, jnp.exp(cum_c - cum_r), 0.0) * step_r
            x_h = x[:, part]
            x_s = split(x_h)
            grow = jnp.exp(cum_c)
            from_start = grow * mm(c_s, start_s)
            y = mm(split(scores * decays), x_s) + from_start + skip[h] * x_h
            gate = gates[:, part]
            gated = y * gate
            inv = lax.rsqrt(jnp.mean(gated * gated, axis=1, keepdims=True) + EPS)
            normal = gated * inv
            out = normal * gain[:, part]
            enc_part = encoded[:, part] + out
            if strand == 0:
                rows_ref[h * own : (h + 1) * own, :] = out
            else:
                enc_ref[:, part] = (rows_ref[h * own : (h + 1) * own, :] + out).astype(BF16)
            d_normal = cot[:, part] * gain[:, part]
            d_y = inv * (d_normal - normal * jnp.mean(normal * d_normal, axis=1, keepdims=True))
            d_y = d_y * gate
            d_y_s = split(d_y)
            mixed_grad = mm(d_y_s, x_s, 1, 1) * decays
            d_scores = d_scores + mixed_grad
            weighted = mixed_grad * scores
            row_sum = jnp.sum(weighted, axis=1, keepdims=True) + jnp.sum(
                d_y * from_start, axis=1, keepdims=True
            )
            col_sum = jnp.sum(weighted, axis=0, keepdims=True)
            grown_s = split(d_y * grow)
            d_c = d_c + mm(grown_s, start_s, 1, 1)
            d_start_s = split(mm(c_s, grown_s, 0, 0))
            pulled = mm(kx_s[h], d_start_s, 1, 1)
            d_kb = d_kb + pulled * w0
            d_w0 = jnp.sum(pulled * kb, axis=1, keepdims=True)
            rate_grads[h] = (
                rate_grads[h] + total(row_sum * cum_c) - total(col_sum * cum_r) + total(d_w0 * w1)
            )
            bias_grads[h] = (
                bias_grads[h]
                + rate * (total(col_sum * sig_r) - total(row_sum * sig_c))
                + total(jnp.where(step_r > 0.0, col_sum * own_sig[n] / step_r, 0.0))
                + total(d_w0 * w2)
            )
        d_scores_s = split(d_scores)
        d_c = d_c + mm(d_scores_s, b_s)
        d_b = mm(d_scores_s, c_s, 0, 0)
        d_sum = jnp.concatenate([d_b, d_c], axis=1) * silu_slope(summed[:, inner:width])
        d_sum_s = split(d_sum)
        hits = hits_t[:, strand * own : (strand + 1) * own].astype(BF16)
        tap_sums = tap_sums + dot(hits, d_sum_s[0]) + dot(hits, d_sum_s[1])
    d_kb = d_kb * silu_slope(kmer_sum[:, inner : inner + HEAD])
    d_kb_s = split(d_kb)
    end_hits = hits_t[:, 2 * own : 2 * own + 128]
    pick_s = pick
    b_sums = dot(kmer_hits[:, 0:16], d_kb_s[0][0:256], 0, 0) + dot(
        kmer_hits[:, 0:16], d_kb_s[1][0:256], 0, 0
    )
    end_pick = dot(end_hits.astype(BF16), pick_s, 1, 1).astype(BF16)
    b_sums = b_sums + dot(end_pick, d_kb_s[0][256:272]) + dot(end_pick, d_kb_s[1][256:272])
    tap_sums = tap_sums + jnp.concatenate([b_sums, jnp.zeros_like(b_sums)], axis=1)
    conv_rows = []
    for k in range(CONV):
        conv_rows.append(
            jnp.sum(tap_sums[4 * k : 4 * k + 4] * table_s, axis=0, keepdims=True)
        )
    lane8 = iota((8, 128), 1)
    row8 = iota((8, 128), 0)
    last = jnp.zeros((8, 128), F32)
    head_total = 8 * heads
    for h in range(heads):
        at = slot * heads + h
        last = jnp.where((row8 == 0) & (lane8 == at), rate_grads[h], last)
        last = jnp.where((row8 == 0) & (lane8 == head_total + at), bias_grads[h], last)
    conv = jnp.concatenate(conv_rows, axis=0)
    pay_ref[...] = jnp.concatenate([conv[:, :128], conv[:, 128:], last], axis=0)


def mixer(args, place, loss_scale, interpret=False):
    (tokens, rc_map, embedding, norm_gain, w_values, w_gates, w_states, w_steps, conv_values,
     conv_states, step_bias, log_rate, skip_gain, head_gain, cotangent) = args
    own, inner = cotangent.shape
    chunks = tokens.shape[0]

    def body(*refs):
        mixer_kernel(place, *refs, loss_scale=loss_scale)

    return pl.pallas_call(
        body,
        out_shape=(
            jax.ShapeDtypeStruct((own, inner), BF16),
            jax.ShapeDtypeStruct((16, 128), F32),
        ),
        in_specs=[SM] * 4 + [VM] * 11,
        out_specs=(VM, VM),
        scratch_shapes=[
            pltpu.VMEM((CONV, chunks, 128), F32),
            pltpu.VMEM((CONV, chunks, 128), F32),
            pltpu.VMEM((chunks, 128), F32),
            pltpu.VMEM((16 * chunks, 128), F32),
        ],
        compiler_params=pltpu.CompilerParams(vmem_limit_bytes=56 * 1024 * 1024),
        interpret=interpret,
        name="mixer",
    )(
        rc_map, step_bias, log_rate, skip_gain, tokens, embedding,
        norm_gain.reshape(1, -1), w_values, w_gates, w_states, w_steps, conv_values, conv_states,
        head_gain.reshape(1, -1), cotangent,
    )


def gather_kernel(tok_ref, out_ref, held, send_sem, recv_sem):
    count = held.shape[0]
    me = lax.axis_index("ctx")
    barrier = pltpu.get_barrier_semaphore()

    def greet(k, carry):
        peer = lax.rem(me + k, count)
        pl.semaphore_signal(barrier, inc=1, device_id={"ctx": peer}, device_id_type=MESH)
        return carry

    lax.fori_loop(1, count, greet, 0)
    pl.semaphore_wait(barrier, count - 1)

    def copy(k, source):
        peer = lax.rem(me + k, count)
        return pltpu.make_async_remote_copy(
            src_ref=tok_ref,
            dst_ref=held.at[source],
            send_sem=send_sem.at[k],
            recv_sem=recv_sem.at[source],
            device_id={"ctx": peer},
            device_id_type=MESH,
        )

    def send(k, carry):
        copy(k, me).start()
        return carry

    lax.fori_loop(1, count, send, 0)
    held[me] = tok_ref[...]

    def finish(k, carry):
        source = lax.rem(me + k, count)
        copy(k, source).wait_recv()
        copy(k, me).wait_send()
        return carry

    lax.fori_loop(1, count, finish, 0)
    out_ref[...] = held[...]


def gather(tokens, count):
    held = (count,) + tokens.shape
    return pl.pallas_call(
        gather_kernel,
        out_shape=jax.ShapeDtypeStruct(held, jnp.int32),
        in_specs=[VM],
        out_specs=VM,
        scratch_shapes=[
            pltpu.VMEM(held, jnp.int32),
            pltpu.SemaphoreType.DMA((count,)),
            pltpu.SemaphoreType.DMA((count,)),
        ],
        compiler_params=pltpu.CompilerParams(collective_id=0, has_side_effects=True),
        name="gather_tokens",
    )(tokens)


def reduce_kernel(x_size, z_size, pay_ref, rate_ref, bias_ref, conv_ref,
                  a_slots, b_slots, c_slots, sent, send_sem, recv_sem):
    ctx = lax.axis_index("ctx")
    tp = lax.axis_index("tp")
    x, z = ctx // z_size, lax.rem(ctx, z_size)
    stages = (
        (a_slots, tp, 8, lambda i: {"tp": i}),
        (b_slots, x, x_size, lambda i: {"ctx": i * z_size + z}),
        (c_slots, z, z_size, lambda i: {"ctx": x * z_size + i}),
    )
    barrier = pltpu.get_barrier_semaphore()
    peers = 0
    for slots, mine, size, device in stages:
        for k in range(1, size):
            pl.semaphore_signal(
                barrier, inc=1, device_id=device(lax.rem(mine + k, size)), device_id_type=MESH
            )
            peers += 1
    pl.semaphore_wait(barrier, peers)
    base = 0
    source = pay_ref
    for number, (slots, mine, size, device) in enumerate(stages):

        def copy(k, place):
            return pltpu.make_async_remote_copy(
                src_ref=source,
                dst_ref=slots.at[place],
                send_sem=send_sem.at[base + k],
                recv_sem=recv_sem.at[base + place],
                device_id=device(lax.rem(mine + k, size)),
                device_id_type=MESH,
            )

        for k in range(1, size):
            copy(k, mine).start()
        slots[mine] = source[...]
        for k in range(1, size):
            copy(k, lax.rem(mine + k, size)).wait_recv()
        summed = slots[0]
        for i in range(1, size):
            summed = summed + slots[i]
        for k in range(1, size):
            copy(k, mine).wait_send()
        if number < 2:
            sent[number] = summed
            source = sent.at[number]
        base += size
    heads = rate_ref.shape[1]
    rate_ref[...] = summed[8:9, 0:heads]
    bias_ref[...] = summed[8:9, heads : 2 * heads]
    conv_ref[...] = jnp.concatenate([summed[0:4], summed[4:8]], axis=1)


def reduce_all(pay, x_size, z_size, heads):
    def body(*refs):
        reduce_kernel(x_size, z_size, *refs)

    shape = pay.shape
    total = 8 + x_size + z_size
    return pl.pallas_call(
        body,
        out_shape=(
            jax.ShapeDtypeStruct((1, heads), F32),
            jax.ShapeDtypeStruct((1, heads), F32),
            jax.ShapeDtypeStruct((4, 256), F32),
        ),
        in_specs=[VM],
        out_specs=(VM, VM, VM),
        scratch_shapes=[
            pltpu.VMEM((8,) + shape, F32),
            pltpu.VMEM((x_size,) + shape, F32),
            pltpu.VMEM((z_size,) + shape, F32),
            pltpu.VMEM((2,) + shape, F32),
            pltpu.SemaphoreType.DMA((total,)),
            pltpu.SemaphoreType.DMA((total,)),
        ],
        compiler_params=pltpu.CompilerParams(collective_id=1, has_side_effects=True),
        name="reduce_grads",
    )(pay)


def solution(mesh):
    count = mesh.shape["ctx"]
    z_size = 8
    x_size = count // z_size

    def on_device(*args):
        tokens = args[0]
        own, inner = args[-1].shape
        everyone = gather(tokens.reshape(2, 128), count).reshape(2 * count, 128)
        loss_scale = 1.0 / math.sqrt(own * count * HEAD)

        def place():
            return lax.axis_index("ctx"), lax.axis_index("tp")

        encoded, pay = mixer((everyone,) + args[1:], place, loss_scale)
        heads = args[11].shape[0] * mesh.shape["tp"]
        rate, bias, conv = reduce_all(pay, x_size, z_size, heads)
        return encoded, rate.reshape(-1), bias.reshape(-1), conv

    tp = P("tp")
    cols = P(None, "tp")
    in_specs = (
        P("ctx"), P(), P(), P(), cols, cols, P(), cols, cols, P(), tp, tp, tp, tp, P("ctx", "tp"),
    )
    return jax.shard_map(
        on_device, mesh=mesh, in_specs=in_specs,
        out_specs=(P("ctx", "tp"), P(), P(), P()), check_vma=False,
    )
```

```python
import math

import jax
import jax.numpy as jnp
from jax import lax
from jax.experimental import pallas as pl
from jax.experimental.pallas import tpu as pltpu
from jax.sharding import PartitionSpec as P

F32 = jnp.float32
BF16 = jnp.bfloat16
HEAD = 128
CONV = 4
EPS = 1e-05
MESH = pl.DeviceIdType.MESH
VM = pl.BlockSpec(memory_space=pltpu.VMEM)
SM = pl.BlockSpec(memory_space=pltpu.SMEM)


def split(v):
    hi = v.astype(BF16)
    return hi, (v - hi.astype(F32)).astype(BF16)


def dot(a, b, ca=1, cb=0):
    return lax.dot_general(a, b, (((ca,), (cb,)), ((), ())), preferred_element_type=F32)


def mm(a, b, ca=1, cb=0):
    return dot(a[0], b[0], ca, cb) + (dot(a[0], b[1], ca, cb) + dot(a[1], b[0], ca, cb))


def iota(shape, dim):
    return lax.broadcasted_iota(jnp.int32, shape, dim)


def back_one(v, fill):
    rolled = pltpu.roll(v, 1, 1)
    wrapped = pltpu.roll(rolled, 1, 0)
    moved = jnp.where(iota(v.shape, 1) == 0, wrapped, rolled)
    first = (iota(v.shape, 0) == 0) & (iota(v.shape, 1) == 0)
    return jnp.where(first, fill, moved)


def ahead_one(v, fill):
    rows, lanes = v.shape
    rolled = pltpu.roll(v, lanes - 1, 1)
    wrapped = pltpu.roll(rolled, rows - 1, 0)
    moved = jnp.where(iota(v.shape, 1) == lanes - 1, wrapped, rolled)
    last = (iota(v.shape, 0) == rows - 1) & (iota(v.shape, 1) == lanes - 1)
    return jnp.where(last, fill, moved)


def softplus(v):
    return jnp.maximum(v, 0.0) + jnp.log1p(jnp.exp(-jnp.abs(v)))


class Links:
    def __init__(self, refs, z_size):
        (self.held, self.slots, self.sent, self.tok_send, self.tok_recv, self.sum_send,
         self.sum_recv) = refs
        self.z_size = z_size
        self.count = self.held.shape[0]
        self.ctx = lax.axis_index("ctx")
        self.tp = lax.axis_index("tp")
        self.tp_size = 8

    def greet(self):
        barrier = pltpu.get_barrier_semaphore()

        def along_ctx(k, carry):
            peer = lax.rem(self.ctx + k, self.count)
            pl.semaphore_signal(barrier, inc=1, device_id={"ctx": peer}, device_id_type=MESH)
            return carry

        def along_tp(k, carry):
            peer = lax.rem(self.tp + k, self.tp_size)
            pl.semaphore_signal(barrier, inc=1, device_id={"tp": peer}, device_id_type=MESH)
            return carry

        lax.fori_loop(1, self.count, along_ctx, 0)
        lax.fori_loop(1, self.tp_size, along_tp, 0)

    def met(self):
        pl.semaphore_wait(pltpu.get_barrier_semaphore(), self.count + self.tp_size - 2)

    def token_copy(self, tok_ref, k, source):
        return pltpu.make_async_remote_copy(
            src_ref=tok_ref,
            dst_ref=self.held.at[source],
            send_sem=self.tok_send.at[k],
            recv_sem=self.tok_recv.at[source],
            device_id={"ctx": lax.rem(self.ctx + k, self.count)},
            device_id_type=MESH,
        )

    def send_tokens(self, tok_ref):
        def send(k, carry):
            self.token_copy(tok_ref, k, self.ctx).start()
            return carry

        lax.fori_loop(1, self.count, send, 0)
        self.held[self.ctx] = tok_ref[...]

    def take_tokens(self, tok_ref):
        def take(k, carry):
            self.token_copy(tok_ref, k, lax.rem(self.ctx + k, self.count)).wait_recv()
            return carry

        lax.fori_loop(1, self.count, take, 0)

    def drain_tokens(self, tok_ref):
        def drain(k, carry):
            self.token_copy(tok_ref, k, self.ctx).wait_send()
            return carry

        lax.fori_loop(1, self.count, drain, 0)

    def reduce(self, value):
        x, z = self.ctx // self.z_size, lax.rem(self.ctx, self.z_size)
        x_size = self.count // self.z_size
        stages = (
            (self.tp, self.tp_size, lambda i: {"tp": i}),
            (x, x_size, lambda i: {"ctx": i * self.z_size + z}),
            (z, self.z_size, lambda i: {"ctx": x * self.z_size + i}),
        )
        base = 0
        for number, (mine, size, device) in enumerate(stages):
            self.sent[number] = value

            def copy(k, place):
                return pltpu.make_async_remote_copy(
                    src_ref=self.sent.at[number],
                    dst_ref=self.slots.at[base + place],
                    send_sem=self.sum_send.at[base + k],
                    recv_sem=self.sum_recv.at[base + place],
                    device_id=device(lax.rem(mine + k, size)),
                    device_id_type=MESH,
                )

            for k in range(1, size):
                copy(k, mine).start()
            self.slots[base + mine] = value
            for k in range(1, size):
                copy(k, lax.rem(mine + k, size)).wait_recv()
            value = self.slots[base]
            for i in range(1, size):
                value = value + self.slots[base + i]
            for k in range(1, size):
                copy(k, mine).wait_send()
            base += size
        return value


def layer_kernel(
    place, links, rc, bias, log_rate, skip, tok_ref, emb_ref, ng_ref, cv_ref, cs_ref, hg_ref,
    ws_hbm, wst_hbm, wv_hbm, wg_hbm, cot_hbm, enc_ref, pay_ref, held, fwd_ref, rev_ref, kmer_ref,
    rows_ref, decay_ref, ws_ref, wst_ref, wv_ref, wg_ref, cot_ref, load_sem,
    *, loss_scale,
):
    me, slot = place()
    blocks = held.shape[0]
    chunks = 2 * blocks
    inner = cv_ref.shape[1]
    heads = inner // HEAD
    own = cot_ref.shape[0]
    loads = [
        pltpu.make_async_copy(source, target, load_sem.at[n])
        for n, (source, target) in enumerate((
            (ws_hbm, ws_ref), (wst_hbm, wst_ref), (wv_hbm, wv_ref), (wg_hbm, wg_ref),
            (cot_hbm, cot_ref),
        ))
    ]
    for load in loads:
        load.start()
    if links is not None:
        links.greet()

    e = emb_ref[...].astype(F32)
    scale = lax.rsqrt(jnp.mean(e * e, axis=1, keepdims=True) + EPS)
    normed = (e * scale * ng_ref[...]).astype(BF16)
    normed = jnp.concatenate([normed, jnp.zeros((12, e.shape[1]), BF16)], axis=0)
    loads[0].wait()
    table_s = dot(normed, ws_ref[...])[0:4]
    loads[1].wait()
    table_d = dot(normed, wst_ref[...], 1, 1)[0:4]
    loads[2].wait()
    table_v = dot(normed, wv_ref[...])[0:4]
    if links is not None:
        links.met()
        links.send_tokens(tok_ref)
    loads[3].wait()
    table_z = dot(normed, wg_ref[...])[0:4]
    lane_h = iota((1, heads), 1)
    bias_row = jnp.zeros((1, heads), F32)
    rate_row = jnp.zeros((1, heads), F32)
    for h in range(heads):
        bias_row = jnp.where(lane_h == h, bias[h], bias_row)
        rate_row = jnp.where(lane_h == h, log_rate[h], rate_row)
    rate_row = jnp.exp(rate_row)
    pre_step = table_d + bias_row
    step_t = softplus(pre_step)
    sig_t = 1.0 / (1.0 + jnp.exp(-pre_step))
    gate_t = table_z / (1.0 + jnp.exp(-table_z))
    table_vs = jnp.concatenate([table_v, table_s], axis=1)
    taps = jnp.concatenate([cv_ref[...], cs_ref[...]], axis=1)
    tail = jnp.concatenate(
        [gate_t, step_t, sig_t, jnp.zeros((4, 128 - 2 * heads), F32)], axis=1
    )
    parts = []
    for k in range(CONV):
        rest = tail if k == CONV - 1 else jnp.zeros_like(tail)
        parts.append(jnp.concatenate([table_vs * taps[k : k + 1], rest], axis=1))
    per_tap = jnp.concatenate(parts, axis=0)
    p_hi = per_tap.astype(BF16)
    p_rest = per_tap - p_hi.astype(F32)
    p_mid = p_rest.astype(BF16)
    p_low = (p_rest - p_mid.astype(F32)).astype(BF16)
    per_tap3 = jnp.concatenate([p_hi, p_mid, p_low], axis=0)

    column = iota((256, 48), 1) % 16
    digit = lax.shift_right_logical(iota((256, 48), 0), 2 * (3 - column // 4)) & 3
    kmer_hits = (digit == column % 4).astype(F32).astype(BF16)
    kmer_full = dot(kmer_hits, per_tap3)

    width = inner + 2 * HEAD
    tri_in = (iota((own, own), 0) <= iota((own, own), 1)).astype(BF16)
    tri_out = (iota((own, own), 0) >= iota((own, own), 1)).astype(BF16)
    pad4 = jnp.zeros((12, own), BF16)
    mine = tok_ref[...].astype(F32)
    mine = jnp.concatenate([mine[0:1], mine[1:2]], axis=1)
    mine_rc = jnp.zeros_like(mine)
    for a in range(4):
        mine_rc = jnp.where(mine == a, rc[a].astype(F32), mine_rc)
    letters = iota((4, own), 0).astype(F32)
    own_f = (jnp.broadcast_to(mine, (4, own)) == letters).astype(F32)
    own_r = (jnp.broadcast_to(mine_rc, (4, own)) == letters).astype(F32)
    n_f = dot(jnp.concatenate([own_f.astype(BF16), pad4], axis=0), tri_in)
    n_r = dot(jnp.concatenate([own_r.astype(BF16), pad4], axis=0), tri_out)
    cum_rows, sig_rows, step_rows, own_sig = [], [], [], []
    for counted, hit in ((n_f, own_f), (n_r, own_r)):
        for h in range(heads):
            steps_sum = sum(counted[a : a + 1] * step_t[a : a + 1, h : h + 1] for a in range(4))
            cum_rows.append(-(rate_row[:, h : h + 1] * steps_sum))
            sig_rows.append(
                sum(counted[a : a + 1] * sig_t[a : a + 1, h : h + 1] for a in range(4))
            )
            step_rows.append(sum(hit[a : a + 1] * step_t[a : a + 1, h : h + 1] for a in range(4)))
            own_sig.append(sum(hit[a : a + 1] * sig_t[a : a + 1, h : h + 1] for a in range(4)))
    stack = jnp.concatenate(
        cum_rows + sig_rows + [jnp.zeros((128 - 4 * heads, own), F32)], axis=0
    )
    columns = jnp.transpose(stack)
    for n in range(2 * heads):
        if n < heads:
            causal = iota((own, own), 0) >= iota((own, own), 1)
        else:
            causal = iota((own, own), 0) <= iota((own, own), 1)
        decay_ref[n] = (
            jnp.where(causal, jnp.exp(columns[:, n : n + 1] - cum_rows[n]), 0.0) * step_rows[n]
        )
    loads[4].wait()
    gain = hg_ref[...]
    cot_ref32 = cot_ref[...].astype(F32) * loss_scale

    if links is not None:
        links.take_tokens(tok_ref)
    for r in range(blocks):
        kmer_ref[2 * r : 2 * r + 2, :] = held[r].astype(F32)

    tok = kmer_ref[...]
    comp = jnp.zeros_like(tok)
    for a in range(4):
        comp = jnp.where(tok == a, rc[a].astype(F32), comp)
    f_shift, r_shift = [tok], [comp]
    for _ in range(CONV - 1):
        f_shift.append(back_one(f_shift[-1], -1.0))
        r_shift.append(ahead_one(r_shift[-1], -1.0))
    for d in range(CONV):
        fwd_ref[d] = f_shift[d]
        rev_ref[d] = r_shift[d]

    row = iota(tok.shape, 0)
    position = row * 128 + iota(tok.shape, 1)
    before = row < 2 * me
    outside = before | (row >= 2 * me + 2)
    kmer_f = f_shift[0] + 4.0 * f_shift[1] + 16.0 * f_shift[2] + 64.0 * f_shift[3]
    kmer_r = r_shift[0] + 4.0 * r_shift[1] + 16.0 * r_shift[2] + 64.0 * r_shift[3]
    kmer = jnp.where(before, kmer_f, kmer_r)
    edge = (before & (position < CONV - 1)) | (position >= chunks * 128 - (CONV - 1))
    kmer_ref[...] = jnp.where(edge & outside, -1.0, kmer)
    mixed = jnp.where(outside, jnp.where(before, tok, comp), -1.0)
    tri = (iota((128, 128), 0) <= iota((128, 128), 1)).astype(BF16)
    ones = jnp.ones((128, 128), BF16)
    strict = (iota((chunks, chunks), 1) < iota((chunks, chunks), 0)).astype(BF16)
    counts = []
    for a in range(4):
        hit = (mixed == a).astype(F32)
        hit16 = hit.astype(BF16)
        within = dot(hit16, tri)
        offset = dot(strict, dot(hit16, ones).astype(BF16))
        total_f = jnp.sum(jnp.where(before, hit, 0.0), keepdims=True)
        inclusive = within + offset - total_f
        counts.append(jnp.where(before, -inclusive, inclusive - hit))
    for h in range(heads):
        steps_sum = sum(counts[a] * step_t[a : a + 1, h : h + 1] for a in range(4))
        sig_sum = sum(counts[a] * sig_t[a : a + 1, h : h + 1] for a in range(4))
        exponent = -(rate_row[:, h : h + 1] * steps_sum)
        decay = jnp.where(outside, jnp.exp(exponent), 0.0)
        for q, value in enumerate((decay, decay * exponent, decay * sig_sum)):
            base = (q * heads + h) * chunks
            rows_ref[base : base + chunks, :] = value
    for q in range(3 * heads, 16):
        rows_ref[q * chunks : (q + 1) * chunks, :] = jnp.zeros((chunks, 128), F32)

    kmer_id = iota((256, 128), 0).astype(F32)

    def load_rows(chunk):
        return rows_ref[pl.ds(chunk, 16, stride=chunks), :]

    def one_hot(chunk):
        return (jnp.broadcast_to(kmer_ref[pl.ds(chunk, 1), :], (256, 128)) == kmer_id).astype(F32)

    def add_block(i, acc):
        weights = jnp.concatenate([load_rows(2 * i), load_rows(2 * i + 1)], axis=1)
        w_f = split(jnp.where(i < me, weights, 0.0))
        w_r = split(jnp.where(i > me, weights, 0.0))
        stacked = jnp.concatenate([w_f[0], w_f[1], w_r[0], w_r[1]], axis=0)
        hits = jnp.concatenate([one_hot(2 * i), one_hot(2 * i + 1)], axis=1).astype(BF16)
        return acc + dot(hits, stacked, 1, 1)

    acc = lax.fori_loop(0, blocks, add_block, jnp.zeros((256, 64), F32), unroll=4)
    lane = iota((16, 128), 1)
    e_f = split(jnp.where(lane < CONV - 1, load_rows(0), 0.0))
    e_r = split(jnp.where(lane >= 128 - (CONV - 1), load_rows(chunks - 1), 0.0))
    edge_rows = jnp.concatenate(
        [e_f[0], e_f[1], e_r[0], e_r[1]], axis=0
    )
    pick_row = iota((16, 128), 0)
    pick = (lane == jnp.where(pick_row < 8, pick_row, pick_row + 112)).astype(BF16)
    acc = jnp.concatenate([acc, dot(pick, edge_rows, 1, 1)], axis=0)
    sources_f = acc[:, 0:16] + acc[:, 16:32]
    sources_r = acc[:, 32:48] + acc[:, 48:64]

    def local_row(ref, d):
        pair = ref[d, pl.ds(2 * me, 2), :]
        return jnp.concatenate([pair[0:1], pair[1:2]], axis=1)

    hits_t = []
    for k in range(CONV):
        d = CONV - 1 - k
        lanes1 = iota((1, 128), 1)
        ends = jnp.where(
            lanes1 < 64, fwd_ref[d, 0:1, :], rev_ref[d, chunks - 1 : chunks, :]
        )
        line = jnp.concatenate([local_row(fwd_ref, d), local_row(rev_ref, d), ends], axis=1)
        hits_t.append(
            (jnp.broadcast_to(line, (4, line.shape[1])) == iota((4, line.shape[1]), 0).astype(F32))
        )
    hits_t = jnp.concatenate([h.astype(F32) for h in hits_t], axis=0)
    hits3_t = jnp.concatenate([hits_t, hits_t, hits_t], axis=0).astype(BF16)
    local_sum = dot(hits3_t, per_tap3, 0, 0)
    ends_sum = jnp.concatenate([local_sum[512:520], local_sum[632:640]], axis=0)
    kmer_sum = jnp.concatenate([kmer_full, ends_sum], axis=0)

    def silu(v):
        return v / (1.0 + jnp.exp(-v))

    def silu_slope(v):
        s = 1.0 / (1.0 + jnp.exp(-v))
        return s + v * s * (1.0 - s)

    kx = silu(kmer_sum[:, :inner])
    kb = silu(kmer_sum[:, inner : inner + HEAD])
    k_steps = kmer_sum[:, width + inner : width + inner + 128]
    kx_s = [split(kx[:, h * HEAD : (h + 1) * HEAD]) for h in range(heads)]
    kb_s = split(kb)

    cot = cot_ref32
    d_kb = jnp.zeros(kb.shape, F32)
    rate_grads = [jnp.zeros((1, 1), F32)] * heads
    bias_grads = [jnp.zeros((1, 1), F32)] * heads
    tap_sums = jnp.zeros((16, 2 * HEAD), F32)

    def total(v):
        return jnp.sum(v, keepdims=True)

    for strand in range(2):
        summed = local_sum[strand * own : (strand + 1) * own]
        sources = (sources_f, sources_r)[strand]
        x = silu(summed[:, :inner])
        states = silu(summed[:, inner:width])
        gates = summed[:, width : width + inner]
        b_s = split(states[:, :HEAD])
        c = states[:, HEAD:]
        c_s = split(c)
        scores = mm(c_s, b_s, 1, 1)
        d_scores = jnp.zeros((own, own), F32)
        d_c = jnp.zeros((own, HEAD), F32)
        for h in range(heads):
            n = strand * heads + h
            part = slice(h * HEAD, (h + 1) * HEAD)
            w0 = k_steps[:, h : h + 1] * sources[:, h : h + 1]
            w1 = k_steps[:, h : h + 1] * sources[:, heads + h : heads + h + 1]
            rate = rate_row[:, h : h + 1]
            w2 = (
                k_steps[:, heads + h : heads + h + 1] * sources[:, h : h + 1]
                - rate * k_steps[:, h : h + 1] * sources[:, 2 * heads + h : 2 * heads + h + 1]
            )
            start_s = split(mm(kb_s, split(kx[:, part] * w0), 0, 0))
            cum_c = columns[:, n : n + 1]
            sig_c = columns[:, 2 * heads + n : 2 * heads + n + 1]
            cum_r, sig_r, step_r = cum_rows[n], sig_rows[n], step_rows[n]
            decays = decay_ref[n]
            x_h = x[:, part]
            x_s = split(x_h)
            grow = jnp.exp(cum_c)
            from_start = grow * mm(c_s, start_s)
            y = mm(split(scores * decays), x_s) + from_start + skip[h] * x_h
            gate = gates[:, part]
            gated = y * gate
            inv = lax.rsqrt(jnp.mean(gated * gated, axis=1, keepdims=True) + EPS)
            normal = gated * inv
            out = normal * gain[:, part]
            if strand == 0:
                rows_ref[h * own : (h + 1) * own, :] = out
            else:
                enc_ref[:, part] = (rows_ref[h * own : (h + 1) * own, :] + out).astype(BF16)
            d_normal = cot[:, part] * gain[:, part]
            d_y = inv * (d_normal - normal * jnp.mean(normal * d_normal, axis=1, keepdims=True))
            d_y = d_y * gate
            d_y_s = split(d_y)
            mixed_grad = mm(d_y_s, x_s, 1, 1) * decays
            d_scores = d_scores + mixed_grad
            weighted = mixed_grad * scores
            row_sum = jnp.sum(weighted, axis=1, keepdims=True) + jnp.sum(
                d_y * from_start, axis=1, keepdims=True
            )
            col_sum = jnp.sum(weighted, axis=0, keepdims=True)
            grown_s = split(d_y * grow)
            d_c = d_c + mm(grown_s, start_s, 1, 1)
            d_start_s = split(mm(c_s, grown_s, 0, 0))
            pulled = mm(kx_s[h], d_start_s, 1, 1)
            d_kb = d_kb + pulled * w0
            d_w0 = jnp.sum(pulled * kb, axis=1, keepdims=True)
            rate_grads[h] = (
                rate_grads[h] + total(row_sum * cum_c) - total(col_sum * cum_r) + total(d_w0 * w1)
            )
            bias_grads[h] = (
                bias_grads[h]
                + rate * (total(col_sum * sig_r) - total(row_sum * sig_c))
                + total(jnp.where(step_r > 0.0, col_sum * own_sig[n] / step_r, 0.0))
                + total(d_w0 * w2)
            )
        d_scores_s = split(d_scores)
        d_c = d_c + mm(d_scores_s, b_s)
        d_b = mm(d_scores_s, c_s, 0, 0)
        d_sum = jnp.concatenate([d_b, d_c], axis=1) * silu_slope(summed[:, inner:width])
        d_sum_s = split(d_sum)
        hits = hits_t[:, strand * own : (strand + 1) * own].astype(BF16)
        tap_sums = tap_sums + dot(hits, d_sum_s[0]) + dot(hits, d_sum_s[1])
    d_kb = d_kb * silu_slope(kmer_sum[:, inner : inner + HEAD])
    d_kb_s = split(d_kb)
    end_hits = hits_t[:, 2 * own : 2 * own + 128]
    pick_s = pick
    b_sums = dot(kmer_hits[:, 0:16], d_kb_s[0][0:256], 0, 0) + dot(
        kmer_hits[:, 0:16], d_kb_s[1][0:256], 0, 0
    )
    end_pick = dot(end_hits.astype(BF16), pick_s, 1, 1).astype(BF16)
    b_sums = b_sums + dot(end_pick, d_kb_s[0][256:272]) + dot(end_pick, d_kb_s[1][256:272])
    tap_sums = tap_sums + jnp.concatenate([b_sums, jnp.zeros_like(b_sums)], axis=1)
    conv_rows = []
    for k in range(CONV):
        conv_rows.append(
            jnp.sum(tap_sums[4 * k : 4 * k + 4] * table_s, axis=0, keepdims=True)
        )
    lane8 = iota((8, 128), 1)
    row8 = iota((8, 128), 0)
    last = jnp.zeros((8, 128), F32)
    head_total = 8 * heads
    for h in range(heads):
        at = slot * heads + h
        last = jnp.where((row8 == 0) & (lane8 == at), rate_grads[h], last)
        last = jnp.where((row8 == 0) & (lane8 == head_total + at), bias_grads[h], last)
    conv = jnp.concatenate(conv_rows, axis=0)
    value = jnp.concatenate([conv[:, :128], conv[:, 128:], last], axis=0)
    if links is not None:
        links.drain_tokens(tok_ref)
        value = links.reduce(value)
    pay_ref[...] = value


def layer(args, place, loss_scale, z_size, everyone=None):
    (tokens, rc_map, embedding, norm_gain, w_values, w_gates, w_states, w_steps, conv_values,
     conv_states, step_bias, log_rate, skip_gain, head_gain, cotangent) = args
    own, inner = cotangent.shape
    blocks = everyone.shape[0] if everyone is not None else 4 * z_size
    chunks = 2 * blocks
    hbm = pl.BlockSpec(memory_space=pl.ANY)

    scratch = [
        pltpu.VMEM((CONV, chunks, 128), F32),
        pltpu.VMEM((CONV, chunks, 128), F32),
        pltpu.VMEM((chunks, 128), F32),
        pltpu.VMEM((16 * chunks, 128), F32),
        pltpu.VMEM((8, own, own), F32),
        pltpu.VMEM(w_states.shape, BF16),
        pltpu.VMEM(w_steps.shape[::-1], BF16),
        pltpu.VMEM(w_values.shape, BF16),
        pltpu.VMEM(w_gates.shape, BF16),
        pltpu.VMEM(cotangent.shape, BF16),
        pltpu.SemaphoreType.DMA((5,)),
    ]
    stages = 8 + blocks // z_size + z_size
    remote = [
        pltpu.VMEM((blocks, 2, 128), jnp.int32),
        pltpu.VMEM((stages, 16, 128), F32),
        pltpu.VMEM((3, 16, 128), F32),
        pltpu.SemaphoreType.DMA((blocks,)),
        pltpu.SemaphoreType.DMA((blocks,)),
        pltpu.SemaphoreType.DMA((stages,)),
        pltpu.SemaphoreType.DMA((stages,)),
    ]
    small = [
        rc_map, step_bias, log_rate, skip_gain, tokens, embedding, norm_gain.reshape(1, -1),
        conv_values, conv_states, head_gain.reshape(1, -1),
    ]
    large = [w_states, w_steps.T, w_values, w_gates, cotangent]
    shapes = (
        jax.ShapeDtypeStruct((own, inner), BF16),
        jax.ShapeDtypeStruct((16, 128), F32),
    )
    if everyone is not None:

        def body(*refs):
            held = refs[10]
            layer_kernel(
                place, None, *refs[:10], *refs[11:18], held, *refs[18:], loss_scale=loss_scale
            )

        return pl.pallas_call(
            body, out_shape=shapes, in_specs=[SM] * 4 + [VM] * 7 + [hbm] * 5, out_specs=(VM, VM),
            scratch_shapes=scratch, interpret=True,
        )(*small, everyone, *large)

    def body(*refs):
        links = Links(refs[17:24], z_size)
        layer_kernel(place, links, *refs[:17], refs[17], *refs[24:], loss_scale=loss_scale)

    return pl.pallas_call(
        body,
        out_shape=shapes,
        in_specs=[SM] * 4 + [VM] * 6 + [hbm] * 5,
        out_specs=(VM, VM),
        scratch_shapes=remote + scratch,
        compiler_params=pltpu.CompilerParams(
            vmem_limit_bytes=60 * 1024 * 1024, collective_id=0, has_side_effects=True
        ),
        name="layer",
    )(*small, *large)


def emit_kernel(enc_ref, pay_ref, out_ref, rate_ref, bias_ref, conv_ref):
    heads = rate_ref.shape[1]
    out_ref[...] = enc_ref[...]
    rate_ref[...] = pay_ref[8:9, 0:heads]
    bias_ref[...] = pay_ref[8:9, heads : 2 * heads]
    conv_ref[...] = jnp.concatenate([pay_ref[0:4, :], pay_ref[4:8, :]], axis=1)


def emit(encoded, pay, heads):
    return pl.pallas_call(
        emit_kernel,
        out_shape=(
            jax.ShapeDtypeStruct(encoded.shape, BF16),
            jax.ShapeDtypeStruct((1, heads), F32),
            jax.ShapeDtypeStruct((1, heads), F32),
            jax.ShapeDtypeStruct((4, 256), F32),
        ),
        in_specs=[VM] * 2,
        out_specs=(VM,) * 4,
        name="emit",
    )(encoded, pay)


def solution(mesh):
    count = mesh.shape["ctx"]
    z_size = count // 4

    def on_device(*args):
        own = args[-1].shape[0]
        loss_scale = 1.0 / math.sqrt(own * count * HEAD)

        def place():
            return lax.axis_index("ctx"), lax.axis_index("tp")

        heads = args[11].shape[0] * mesh.shape["tp"]
        encoded, pay = layer((args[0].reshape(2, 128),) + args[1:], place, loss_scale, z_size)
        encoded, rate, bias, conv = emit(encoded, pay, heads)
        return encoded, rate.reshape(-1), bias.reshape(-1), conv

    tp = P("tp")
    cols = P(None, "tp")
    in_specs = (
        P("ctx"), P(), P(), P(), cols, cols, P(), cols, cols, P(), tp, tp, tp, tp, P("ctx", "tp"),
    )
    return jax.shard_map(
        on_device, mesh=mesh, in_specs=in_specs,
        out_specs=(P("ctx", "tp"), P(), P(), P()), check_vma=False,
    )
```

```python
import math

import jax
import jax.numpy as jnp
from jax import lax
from jax.experimental import pallas as pl
from jax.experimental.pallas import tpu as pltpu
from jax.sharding import PartitionSpec as P

F32 = jnp.float32
BF16 = jnp.bfloat16
HEAD = 128
CONV = 4
EPS = 1e-05
MESH = pl.DeviceIdType.MESH
VM = pl.BlockSpec(memory_space=pltpu.VMEM)
SM = pl.BlockSpec(memory_space=pltpu.SMEM)


def split(v):
    hi = v.astype(BF16)
    return hi, (v - hi.astype(F32)).astype(BF16)


def dot(a, b, ca=1, cb=0):
    return lax.dot_general(a, b, (((ca,), (cb,)), ((), ())), preferred_element_type=F32)


def lhs3(v):
    hi, lo = v
    return jnp.concatenate([hi, lo, hi], axis=1)


def rhs3(v, axis=0):
    hi, lo = v
    return jnp.concatenate([hi, hi, lo], axis=axis)


def silu(v):
    return v / (1.0 + jnp.exp(-v))


def silu_slope(v):
    s = 1.0 / (1.0 + jnp.exp(-v))
    return s + v * s * (1.0 - s)


def fold(v):
    return v[:, :128] + v[:, 128:]


def iota(shape, dim):
    return lax.broadcasted_iota(jnp.int32, shape, dim)


def back_one(v, fill):
    rolled = pltpu.roll(v, 1, 1)
    wrapped = pltpu.roll(rolled, 1, 0)
    moved = jnp.where(iota(v.shape, 1) == 0, wrapped, rolled)
    first = (iota(v.shape, 0) == 0) & (iota(v.shape, 1) == 0)
    return jnp.where(first, fill, moved)


def ahead_one(v, fill):
    rows, lanes = v.shape
    rolled = pltpu.roll(v, lanes - 1, 1)
    wrapped = pltpu.roll(rolled, rows - 1, 0)
    moved = jnp.where(iota(v.shape, 1) == lanes - 1, wrapped, rolled)
    last = (iota(v.shape, 0) == rows - 1) & (iota(v.shape, 1) == lanes - 1)
    return jnp.where(last, fill, moved)


def softplus(v):
    return jnp.maximum(v, 0.0) + jnp.log1p(jnp.exp(-jnp.abs(v)))


class Links:
    def __init__(self, refs, z_size):
        (self.held, self.slots, self.sent, self.tok_send, self.tok_recv, self.sum_send,
         self.sum_recv) = refs
        self.z_size = z_size
        self.count = self.held.shape[0]
        self.ctx = lax.axis_index("ctx")
        self.tp = lax.axis_index("tp")
        self.tp_size = 8
        self.x_size = self.count // z_size
        self.x, self.z = self.ctx // z_size, lax.rem(self.ctx, z_size)

    def greet(self):
        barrier = pltpu.get_barrier_semaphore()

        def along_ctx(k, carry):
            peer = lax.rem(self.ctx + k, self.count)
            pl.semaphore_signal(barrier, inc=1, device_id={"ctx": peer}, device_id_type=MESH)
            return carry

        def along_plane(k, carry):
            peer = lax.rem(self.tp + 1 + k // self.x_size, self.tp_size)
            row = lax.rem(k, self.x_size)
            where = {"ctx": row * self.z_size + self.z, "tp": peer}
            pl.semaphore_signal(barrier, inc=1, device_id=where, device_id_type=MESH)
            return carry

        lax.fori_loop(1, self.count, along_ctx, 0)
        lax.fori_loop(0, (self.tp_size - 1) * self.x_size, along_plane, 0)

    def met(self):
        pl.semaphore_wait(pltpu.get_barrier_semaphore(), self.count - 1 + (self.tp_size - 1) * self.x_size)

    def token_copy(self, tok_ref, k, source):
        return pltpu.make_async_remote_copy(
            src_ref=tok_ref,
            dst_ref=self.held.at[source],
            send_sem=self.tok_send.at[k],
            recv_sem=self.tok_recv.at[source],
            device_id={"ctx": lax.rem(self.ctx + k, self.count)},
            device_id_type=MESH,
        )

    def send_tokens(self, tok_ref):
        def send(k, carry):
            self.token_copy(tok_ref, k, self.ctx).start()
            return carry

        lax.fori_loop(1, self.count, send, 0)
        self.held[self.ctx] = tok_ref[...]

    def take_one(self, tok_ref, k):
        self.token_copy(tok_ref, k, lax.rem(self.ctx + k, self.count)).wait_recv()

    def take_neighbours(self, tok_ref):
        self.take_one(tok_ref, 1)
        self.take_one(tok_ref, self.count - 1)

    def take_others(self, tok_ref):
        def take(k, carry):
            self.take_one(tok_ref, k)
            return carry

        lax.fori_loop(2, self.count - 1, take, 0)

    def drain_tokens(self, tok_ref):
        def drain(k, carry):
            self.token_copy(tok_ref, k, self.ctx).wait_send()
            return carry

        lax.fori_loop(1, self.count, drain, 0)

    def reduce(self, value):
        plane = self.x_size * self.tp_size
        stages = (
            (
                self.x * self.tp_size + self.tp,
                plane,
                lambda i: {
                    "ctx": (i // self.tp_size) * self.z_size + self.z,
                    "tp": lax.rem(i, self.tp_size),
                },
            ),
            (self.z, self.z_size, lambda i: {"ctx": self.x * self.z_size + i}),
        )
        base = 0
        for number, (mine, size, device) in enumerate(stages):
            self.sent[number] = value

            def copy(k, place):
                return pltpu.make_async_remote_copy(
                    src_ref=self.sent.at[number],
                    dst_ref=self.slots.at[base + place],
                    send_sem=self.sum_send.at[base + k],
                    recv_sem=self.sum_recv.at[base + place],
                    device_id=device(lax.rem(mine + k, size)),
                    device_id_type=MESH,
                )

            def start(k, carry):
                copy(k, mine).start()
                return carry

            def take(k, carry):
                copy(k, lax.rem(mine + k, size)).wait_recv()
                return carry

            def drain(k, carry):
                copy(k, mine).wait_send()
                return carry

            lax.fori_loop(1, size, start, 0)
            self.slots[base + mine] = value
            lax.fori_loop(1, size, take, 0)
            value = self.slots[base]
            for i in range(1, size):
                value = value + self.slots[base + i]
            lax.fori_loop(1, size, drain, 0)
            base += size
        return value


def layer_kernel(
    place, links, rc, bias, log_rate, skip, tok_ref, emb_ref, ng_ref, cv_ref, cs_ref, hg_ref,
    ws_hbm, wst_hbm, wv_hbm, wg_hbm, cot_hbm, enc_ref, pay_ref, held, fwd_ref, rev_ref, kmer_ref,
    rows_ref, decay_ref, ws_ref, wst_ref, wv_ref, wg_ref, cot_ref, load_sem,
    xh_ref, xl_ref, y_ref, gate_ref, grow_ref, dg_ref, score_ref, gh_ref, gl_ref,
    *, loss_scale,
):
    me, slot = place()
    blocks = held.shape[0]
    chunks = 2 * blocks
    inner = cv_ref.shape[1]
    heads = inner // HEAD
    own = cot_ref.shape[0]
    width = inner + 2 * HEAD
    loads = [
        pltpu.make_async_copy(source, target, load_sem.at[n])
        for n, (source, target) in enumerate((
            (ws_hbm, ws_ref), (wst_hbm, wst_ref), (wv_hbm, wv_ref), (wg_hbm, wg_ref),
            (cot_hbm, cot_ref),
        ))
    ]
    for load in loads:
        load.start()
    if links is not None:
        links.greet()

    e = emb_ref[...].astype(F32)
    scale = lax.rsqrt(jnp.mean(e * e, axis=1, keepdims=True) + EPS)
    normed = (e * scale * ng_ref[...]).astype(BF16)
    normed = jnp.concatenate([normed, jnp.zeros((12, e.shape[1]), BF16)], axis=0)
    loads[0].wait()
    table_s = dot(normed, ws_ref[...])[0:4]
    loads[1].wait()
    table_d = dot(normed, wst_ref[...], 1, 1)[0:4]
    loads[2].wait()
    table_v = dot(normed, wv_ref[...])[0:4]
    if links is not None:
        links.met()
        links.send_tokens(tok_ref)
    loads[3].wait()
    table_z = dot(normed, wg_ref[...])[0:4]
    lane_h = iota((1, heads), 1)
    bias_row = jnp.zeros((1, heads), F32)
    rate_row = jnp.zeros((1, heads), F32)
    for h in range(heads):
        bias_row = jnp.where(lane_h == h, bias[h], bias_row)
        rate_row = jnp.where(lane_h == h, log_rate[h], rate_row)
    rate_row = jnp.exp(rate_row)
    pre_step = table_d + bias_row
    step_t = softplus(pre_step)
    sig_t = 1.0 / (1.0 + jnp.exp(-pre_step))
    ratio_t = jnp.where(step_t > 0.0, sig_t / step_t, 1.0)
    gate_t = silu(table_z)
    table_vs = jnp.concatenate([table_v, table_s], axis=1)
    taps = jnp.concatenate([cv_ref[...], cs_ref[...]], axis=1)
    none2 = jnp.zeros((4, 2 * heads), F32)
    rest = jnp.zeros((4, 128 - 3 * heads), F32)
    tail = jnp.concatenate(
        [
            gate_t,
            step_t, step_t, -rate_row * step_t, rest,
            none2, sig_t, rest,
            none2, ratio_t, rest,
        ],
        axis=1,
    )
    parts = []
    for k in range(CONV):
        last = tail if k == CONV - 1 else jnp.zeros_like(tail)
        parts.append(jnp.concatenate([table_vs * taps[k : k + 1], last], axis=1))
    per_tap = jnp.concatenate(parts, axis=0)
    p_hi = per_tap.astype(BF16)
    p_rest = per_tap - p_hi.astype(F32)
    p_mid = p_rest.astype(BF16)
    p_low = (p_rest - p_mid.astype(F32)).astype(BF16)
    per_tap3 = jnp.concatenate([p_hi, p_mid, p_low], axis=0)
    place_cols = width + inner

    column = iota((256, 48), 1) % 16
    digit = lax.shift_right_logical(iota((256, 48), 0), 2 * (3 - column // 4)) & 3
    kmer_hits = (digit == column % 4).astype(F32).astype(BF16)
    kmer_sum = dot(kmer_hits, per_tap3[:, : inner + HEAD])
    kmer_tail = dot(kmer_hits, per_tap3[:, place_cols:])
    kx = silu(kmer_sum[:, :inner])
    kb = silu(kmer_sum[:, inner:])
    kb_slope = silu_slope(kmer_sum[:, inner:])

    tri_in = (iota((own, own), 0) <= iota((own, own), 1)).astype(BF16)
    tri_out = (iota((own, own), 0) >= iota((own, own), 1)).astype(BF16)
    pad4 = jnp.zeros((12, own), BF16)

    def complement(v):
        out = jnp.full(v.shape, -1.0, F32)
        for a in range(4):
            out = jnp.where(v == a, rc[a].astype(F32), out)
        return out

    pair = tok_ref[...].astype(F32)
    mine = jnp.concatenate([pair[0:1], pair[1:2]], axis=1)
    mine_rc = complement(mine)
    letters = iota((4, own), 0).astype(F32)
    own_f = (jnp.broadcast_to(mine, (4, own)) == letters).astype(F32)
    own_r = (jnp.broadcast_to(mine_rc, (4, own)) == letters).astype(F32)
    n_f = dot(jnp.concatenate([own_f.astype(BF16), pad4], axis=0), tri_in)
    n_r = dot(jnp.concatenate([own_r.astype(BF16), pad4], axis=0), tri_out)

    def blend(weights, table, h):
        return sum(weights[a : a + 1] * table[a : a + 1, h : h + 1] for a in range(4))

    cum_rows, sig_rows, step_rows, ratio_rows = [], [], [], []
    for counted, hit in ((n_f, own_f), (n_r, own_r)):
        for h in range(heads):
            cum_rows.append(-(rate_row[:, h : h + 1] * blend(counted, step_t, h)))
            sig_rows.append(blend(counted, sig_t, h))
            step_rows.append(blend(hit, step_t, h))
            ratio_rows.append(blend(hit, ratio_t, h))
    cum8 = jnp.concatenate(cum_rows, axis=0)
    both = split(jnp.concatenate([cum8] + sig_rows, axis=0))
    side = jnp.concatenate([both[0], both[1]], axis=0)
    side = jnp.concatenate([side, side], axis=1)
    columns = jnp.transpose(
        jnp.concatenate([cum8, jnp.zeros((128 - 2 * heads, own), F32)], axis=0)
    )
    for n in range(2 * heads):
        if n < heads:
            causal = iota((own, own), 0) >= iota((own, own), 1)
        else:
            causal = iota((own, own), 0) <= iota((own, own), 1)
        cum_c = jnp.broadcast_to(columns[:, n : n + 1], (own, 128))
        for half in range(own // 128):
            at = slice(half * 128, half * 128 + 128)
            decay_ref[n, :, at] = (
                jnp.where(causal[:, at], jnp.exp(cum_c - cum_rows[n][:, at]), 0.0)
                * step_rows[n][:, at]
            )
        part = slice((n % heads) * HEAD, (n % heads + 1) * HEAD)
        grow_ref[n // heads, :, part] = jnp.exp(cum_c)
    loads[4].wait()
    gain = hg_ref[...]
    dg_ref[...] = cot_ref[...].astype(F32) * (gain * loss_scale)

    if links is not None:
        links.take_neighbours(tok_ref)
    earlier = held[lax.rem(me + blocks - 1, blocks)].astype(F32)[1:2]
    later = held[lax.rem(me + 1, blocks)].astype(F32)[0:1]
    earlier = jnp.where(me > 0, earlier, -1.0)
    later = jnp.where(me < blocks - 1, later, -1.0)
    line = jnp.concatenate([earlier, mine, later], axis=1)
    line = jnp.broadcast_to(line, (8, line.shape[1]))
    line_rc = complement(line)
    letters8 = iota((8, own), 0).astype(F32)
    f_hits, r_hits = [], []
    for k in range(CONV):
        d = CONV - 1 - k
        f_line = pltpu.roll(line, d, 1) if d else line
        r_line = pltpu.roll(line_rc, line.shape[1] - d, 1) if d else line_rc
        f_hits.append((f_line[:, 128 : 128 + own] == letters8)[0:4].astype(F32))
        r_hits.append((r_line[:, 128 : 128 + own] == letters8)[0:4].astype(F32))
    hits_t = [jnp.concatenate(f_hits, axis=0), jnp.concatenate(r_hits, axis=0)]
    slopes, c_parts, ct_parts, b_parts = [], [], [], []
    for strand in range(2):
        hits = jnp.concatenate([hits_t[strand]] * 3, axis=0).astype(BF16)
        summed = dot(hits, per_tap3[:, :place_cols], 0, 0)
        gate_ref[strand] = summed[:, width:]
        states = silu(summed[:, inner:width])
        slopes.append(silu_slope(summed[:, inner:width]))
        b_s = split(states[:, :HEAD])
        c_s = split(states[:, HEAD:])
        b_parts.append(b_s)
        c_parts.append(c_s)
        ct_parts.append(split(jnp.transpose(states[:, HEAD:])))
        scores = dot(lhs3(c_s), rhs3(b_s, 1), 1, 1)
        score_ref[strand] = scores
        for h in range(heads):
            part = slice(h * HEAD, (h + 1) * HEAD)
            x_h = silu(summed[:, part])
            x_s = split(x_h)
            xh_ref[strand, :, part] = x_s[0]
            xl_ref[strand, :, part] = x_s[1]
            mixing = split(scores * decay_ref[strand * heads + h])
            y_ref[strand, :, part] = dot(lhs3(mixing), rhs3(x_s)) + skip[h] * x_h

    if links is not None:
        links.take_others(tok_ref)
    for r in range(blocks):
        kmer_ref[2 * r : 2 * r + 2, :] = held[r].astype(F32)
    tok = kmer_ref[...]
    comp = complement(tok)
    f_shift, r_shift = [tok], [comp]
    for _ in range(CONV - 1):
        f_shift.append(back_one(f_shift[-1], -1.0))
        r_shift.append(ahead_one(r_shift[-1], -1.0))

    row = iota(tok.shape, 0)
    position = row * 128 + iota(tok.shape, 1)
    before = row < 2 * me
    outside = before | (row >= 2 * me + 2)
    kmer_f = f_shift[0] + 4.0 * f_shift[1] + 16.0 * f_shift[2] + 64.0 * f_shift[3]
    kmer_r = r_shift[0] + 4.0 * r_shift[1] + 16.0 * r_shift[2] + 64.0 * r_shift[3]
    kmer = jnp.where(before, kmer_f, kmer_r)
    edge = (before & (position < CONV - 1)) | (position >= chunks * 128 - (CONV - 1))
    kmer_ref[...] = jnp.where(edge & outside, -1.0, kmer)
    mixed = jnp.where(outside, jnp.where(before, tok, comp), -1.0)
    tri = (iota((128, 128), 0) <= iota((128, 128), 1)).astype(BF16)
    ones = jnp.ones((128, 128), BF16)
    strict = (iota((chunks, chunks), 1) < iota((chunks, chunks), 0)).astype(BF16)
    counts = []
    for a in range(4):
        hit = (mixed == a).astype(F32)
        hit16 = hit.astype(BF16)
        within = dot(hit16, tri)
        offset = dot(strict, dot(hit16, ones).astype(BF16))
        total_f = jnp.sum(jnp.where(before, hit, 0.0), keepdims=True)
        inclusive = within + offset - total_f
        counts.append(jnp.where(before, -inclusive, inclusive - hit))
    for h in range(heads):
        steps_sum = sum(counts[a] * step_t[a : a + 1, h : h + 1] for a in range(4))
        sig_sum = sum(counts[a] * sig_t[a : a + 1, h : h + 1] for a in range(4))
        exponent = -(rate_row[:, h : h + 1] * steps_sum)
        decay = jnp.where(outside, jnp.exp(exponent), 0.0)
        for q, value in enumerate((decay, decay * exponent, decay * sig_sum)):
            base = (q * heads + h) * chunks
            rows_ref[base : base + chunks, :] = value
    for q in range(3 * heads, 16):
        rows_ref[q * chunks : (q + 1) * chunks, :] = jnp.zeros((chunks, 128), F32)

    kmer_id = iota((256, 128), 0).astype(F32)
    idle = jnp.zeros((64, 256), BF16)

    def load_rows(chunk):
        return rows_ref[pl.ds(chunk, 16, stride=chunks), :]

    def one_hot(chunk):
        return (jnp.broadcast_to(kmer_ref[pl.ds(chunk, 1), :], (256, 128)) == kmer_id).astype(F32)

    def add_block(i, acc):
        weights = jnp.concatenate([load_rows(2 * i), load_rows(2 * i + 1)], axis=1)
        w_f = split(jnp.where(i < me, weights, 0.0))
        w_r = split(jnp.where(i > me, weights, 0.0))
        stacked = jnp.concatenate([w_f[0], w_f[1], w_r[0], w_r[1], idle], axis=0)
        hits = jnp.concatenate([one_hot(2 * i), one_hot(2 * i + 1)], axis=1).astype(BF16)
        return acc + dot(hits, stacked, 1, 1)

    acc = lax.fori_loop(0, blocks, add_block, jnp.zeros((256, 128), F32), unroll=4)
    lane = iota((16, 128), 1)
    e_f = split(jnp.where(lane < CONV - 1, load_rows(0), 0.0))
    e_r = split(jnp.where(lane >= 128 - (CONV - 1), load_rows(chunks - 1), 0.0))
    edge_rows = jnp.concatenate(
        [e_f[0], e_f[1], e_r[0], e_r[1], jnp.zeros((64, 128), BF16)], axis=0
    )
    pick_row = iota((16, 128), 0)
    pick = (lane == jnp.where(pick_row < 8, pick_row, pick_row + 112)).astype(BF16)
    acc = jnp.concatenate([acc, dot(pick, edge_rows, 1, 1)], axis=0)

    end_hits = []
    for k in range(CONV):
        d = CONV - 1 - k
        ends = jnp.where(
            iota((1, 128), 1) < 64, f_shift[d][0:1, :], r_shift[d][chunks - 1 : chunks, :]
        )
        end_hits.append(
            (jnp.broadcast_to(ends, (4, 128)) == iota((4, 128), 0).astype(F32)).astype(F32)
        )
    end_hits = jnp.concatenate(end_hits, axis=0).astype(BF16)
    end_pick = dot(end_hits, pick, 1, 1)
    end3 = jnp.concatenate([end_pick] * 3, axis=0).astype(BF16)
    end_sum = dot(end3, per_tap3, 0, 0)
    kx = jnp.concatenate([kx, silu(end_sum[:, :inner])], axis=0)
    kb = jnp.concatenate([kb, silu(end_sum[:, inner : inner + HEAD])], axis=0)
    kb_slope = jnp.concatenate([kb_slope, silu_slope(end_sum[:, inner : inner + HEAD])], axis=0)
    k_tail = jnp.concatenate([kmer_tail, end_sum[:, place_cols:]], axis=0)
    table_rows = kx.shape[0]

    joined = acc + pltpu.roll(acc, 128 - 16, 1)
    lanes = iota((1, 128), 1)
    lane_rate = jnp.zeros((1, 128), F32)
    for h in range(heads):
        lane_rate = jnp.where(lanes == 2 * heads + h, -rate_row[:, h : h + 1], lane_rate)
    lane_one = jnp.where((lanes >= heads) & (lanes < 2 * heads), 1.0, lane_rate)
    weights, ratios, kxw_parts = [], [], []
    for strand in range(2):
        source = joined if strand == 0 else pltpu.roll(joined, 128 - 32, 1)
        w = k_tail[:, 0:128] * source
        e4, e8 = pltpu.roll(source, heads, 1), pltpu.roll(source, 2 * heads, 1)
        decay = jnp.where((lanes >= heads) & (lanes < 2 * heads), e4, e8)
        kept = (decay > 0.0) & (lanes >= heads) & (lanes < 3 * heads)
        ratio = jnp.where(
            kept, lane_one * source / jnp.where(kept, decay, 1.0) + k_tail[:, 256:384], 0.0
        )
        ratio = jnp.concatenate(
            [ratio, jnp.zeros((384 - table_rows, 128), F32)], axis=0
        )
        ratio = split(jnp.transpose(ratio)[0:16, :table_rows])
        ratios.append(jnp.concatenate([ratio[0], ratio[1]], axis=0))
        kxw_parts.append(
            split(
                jnp.concatenate(
                    [
                        kx[:, h * HEAD : (h + 1) * HEAD]
                        * jnp.broadcast_to(w[:, h : h + 1], (table_rows, HEAD))
                        for h in range(heads)
                    ],
                    axis=1,
                )
            )
        )
    kb_t = jnp.concatenate([kb, jnp.zeros((384 - table_rows, HEAD), F32)], axis=0)
    kb_t = split(jnp.transpose(kb_t)[:, :table_rows])

    d_kb = jnp.zeros(kb.shape, F32)
    rate_grads = [jnp.zeros((1, 128), F32)] * heads
    bias_grads = [jnp.zeros((1, 128), F32)] * heads
    tap_sums = jnp.zeros((16, 2 * HEAD), F32)
    for strand in range(2):
        kxw = kxw_parts[strand]
        c_s, ct_s, b_s = c_parts[strand], ct_parts[strand], b_parts[strand]
        start = (
            dot(kb_t[0], kxw[0]) + (dot(kb_t[0], kxw[1]) + dot(kb_t[1], kxw[0]))
        )
        start_s = split(start)
        carried = dot(lhs3(c_s), rhs3(start_s))
        scores = score_ref[strand]
        d_scores = jnp.zeros((own, own), F32)
        for h in range(heads):
            n = strand * heads + h
            part = slice(h * HEAD, (h + 1) * HEAD)
            grow = grow_ref[strand, :, part]
            from_start = grow * carried[:, part]
            gate = gate_ref[strand, :, part]
            gated = (y_ref[strand, :, part] + from_start) * gate
            inv = lax.rsqrt(jnp.mean(gated * gated, axis=1, keepdims=True) + EPS)
            normal = gated * inv
            out = normal * gain[:, part]
            if strand == 0:
                y_ref[0, :, part] = out
            else:
                enc_ref[:, part] = (y_ref[0, :, part] + out).astype(BF16)
            d_normal = dg_ref[:, part]
            d_y = d_normal - normal * jnp.mean(normal * d_normal, axis=1, keepdims=True)
            d_y = (d_y * inv) * gate
            x_s = (xh_ref[strand, :, part], xl_ref[strand, :, part])
            mixed_grad = dot(lhs3(split(d_y)), rhs3(x_s, 1), 1, 1) * decay_ref[n]
            d_scores = d_scores + mixed_grad
            weighted = mixed_grad * scores
            wsum = split(fold(weighted) + d_y * from_start)
            moved = dot(side, jnp.concatenate([wsum[0], wsum[1]], axis=0))
            col_sum = jnp.sum(weighted, axis=0, keepdims=True)
            grown = split(d_y * grow)
            gh_ref[:, part] = grown[0]
            gl_ref[:, part] = grown[1]
            rate = rate_row[:, h : h + 1]
            rows = 2 * heads
            rate_grads[h] = (
                rate_grads[h]
                + (moved[n : n + 1] + moved[2 * rows + n : 2 * rows + n + 1])
                - fold(col_sum * cum_rows[n])
            )
            bias_grads[h] = (
                bias_grads[h]
                + fold(col_sum * (rate * sig_rows[n] + ratio_rows[n]))
                - rate * (moved[rows + n : rows + n + 1] + moved[3 * rows + n : 3 * rows + n + 1])
            )
        grown = (gh_ref[...], gl_ref[...])
        d_start = split(dot(lhs3(ct_s), rhs3(grown)))
        for h in range(heads):
            part = slice(h * HEAD, (h + 1) * HEAD)
            d_start_h = (d_start[0][:, part], d_start[1][:, part])
            pulled = dot(
                lhs3((kxw[0][:, part], kxw[1][:, part])), rhs3(d_start_h, 1), 1, 1
            )
            d_kb = d_kb + pulled
            t = split(pulled * kb)
            slope = dot(ratios[strand], t[0]) + dot(ratios[strand], t[1])
            slope = slope[0:16] + slope[16:32]
            rate_grads[h] = rate_grads[h] + slope[heads + h : heads + h + 1]
            bias_grads[h] = bias_grads[h] + slope[2 * heads + h : 2 * heads + h + 1]
        d_scores_s = split(d_scores)
        d_c = dot(lhs3(d_scores_s), rhs3(b_s)) + dot(lhs3(grown), rhs3(start_s, 1), 1, 1)
        d_b = dot(lhs3(split(jnp.transpose(d_scores))), rhs3(c_s))
        d_sum = split(jnp.concatenate([d_b, d_c], axis=1) * slopes[strand])
        hits = hits_t[strand].astype(BF16)
        tap_sums = tap_sums + dot(
            jnp.concatenate([hits, hits], axis=1), jnp.concatenate([d_sum[0], d_sum[1]], axis=0)
        )
    d_kb = split(d_kb * kb_slope)
    b_sums = dot(kmer_hits[:, 0:16], d_kb[0][0:256], 0, 0)
    b_sums = b_sums + dot(kmer_hits[:, 0:16], d_kb[1][0:256], 0, 0)
    end_pick = end_pick.astype(BF16)
    b_sums = b_sums + dot(end_pick, d_kb[0][256:]) + dot(end_pick, d_kb[1][256:])
    tap_sums = tap_sums + jnp.concatenate([b_sums, jnp.zeros_like(b_sums)], axis=1)
    conv_rows = []
    for k in range(CONV):
        conv_rows.append(
            jnp.sum(tap_sums[4 * k : 4 * k + 4] * table_s, axis=0, keepdims=True)
        )
    sums = jnp.sum(jnp.concatenate(rate_grads + bias_grads, axis=0), axis=1, keepdims=True)
    lane8 = iota((8, 128), 1)
    row8 = iota((8, 128), 0)
    last = jnp.zeros((8, 128), F32)
    head_total = 8 * heads
    for h in range(heads):
        at = slot * heads + h
        last = jnp.where((row8 == 0) & (lane8 == at), sums[h : h + 1], last)
        last = jnp.where(
            (row8 == 0) & (lane8 == head_total + at), sums[heads + h : heads + h + 1], last
        )
    conv = jnp.concatenate(conv_rows, axis=0)
    value = jnp.concatenate([conv[:, :128], conv[:, 128:], last], axis=0)
    if links is not None:
        links.drain_tokens(tok_ref)
        value = links.reduce(value)
    pay_ref[...] = value


def layer(args, place, loss_scale, z_size, everyone=None, interpret=False):
    (tokens, rc_map, embedding, norm_gain, w_values, w_gates, w_states, w_steps, conv_values,
     conv_states, step_bias, log_rate, skip_gain, head_gain, cotangent) = args
    own, inner = cotangent.shape
    blocks = everyone.shape[0] if everyone is not None else 4 * z_size
    chunks = 2 * blocks
    hbm = pl.BlockSpec(memory_space=pl.ANY)

    scratch = [
        pltpu.VMEM((CONV, chunks, 128), F32),
        pltpu.VMEM((CONV, chunks, 128), F32),
        pltpu.VMEM((chunks, 128), F32),
        pltpu.VMEM((16 * chunks, 128), F32),
        pltpu.VMEM((8, own, own), F32),
        pltpu.VMEM(w_states.shape, BF16),
        pltpu.VMEM(w_steps.shape[::-1], BF16),
        pltpu.VMEM(w_values.shape, BF16),
        pltpu.VMEM(w_gates.shape, BF16),
        pltpu.VMEM(cotangent.shape, BF16),
        pltpu.SemaphoreType.DMA((5,)),
        pltpu.VMEM((2, own, inner), BF16),
        pltpu.VMEM((2, own, inner), BF16),
        pltpu.VMEM((2, own, inner), F32),
        pltpu.VMEM((2, own, inner), F32),
        pltpu.VMEM((2, own, inner), F32),
        pltpu.VMEM((own, inner), F32),
        pltpu.VMEM((2, own, own), F32),
        pltpu.VMEM((own, inner), BF16),
        pltpu.VMEM((own, inner), BF16),
    ]
    stages = 8 * (blocks // z_size) + z_size
    remote = [
        pltpu.VMEM((blocks, 2, 128), jnp.int32),
        pltpu.VMEM((stages, 16, 128), F32),
        pltpu.VMEM((3, 16, 128), F32),
        pltpu.SemaphoreType.DMA((blocks,)),
        pltpu.SemaphoreType.DMA((blocks,)),
        pltpu.SemaphoreType.DMA((stages,)),
        pltpu.SemaphoreType.DMA((stages,)),
    ]
    small = [
        rc_map, step_bias, log_rate, skip_gain, tokens, embedding, norm_gain.reshape(1, -1),
        conv_values, conv_states, head_gain.reshape(1, -1),
    ]
    large = [w_states, w_steps.T, w_values, w_gates, cotangent]
    shapes = (
        jax.ShapeDtypeStruct((own, inner), BF16),
        jax.ShapeDtypeStruct((16, 128), F32),
    )
    if everyone is not None:

        def body(*refs):
            held = refs[10]
            layer_kernel(
                place, None, *refs[:10], *refs[11:18], held, *refs[18:], loss_scale=loss_scale
            )

        return pl.pallas_call(
            body, out_shape=shapes, in_specs=[SM] * 4 + [VM] * 7 + [hbm] * 5, out_specs=(VM, VM),
            scratch_shapes=scratch, interpret=interpret,
        )(*small, everyone, *large)

    def body(*refs):
        links = Links(refs[17:24], z_size)
        layer_kernel(place, links, *refs[:17], refs[17], *refs[24:], loss_scale=loss_scale)

    return pl.pallas_call(
        body,
        out_shape=shapes,
        in_specs=[SM] * 4 + [VM] * 6 + [hbm] * 5,
        out_specs=(VM, VM),
        scratch_shapes=remote + scratch,
        compiler_params=pltpu.CompilerParams(
            vmem_limit_bytes=60 * 1024 * 1024, collective_id=0, has_side_effects=True
        ),
        name="layer",
    )(*small, *large)


def emit_kernel(enc_ref, pay_ref, out_ref, rate_ref, bias_ref, conv_ref):
    heads = rate_ref.shape[1]
    out_ref[...] = enc_ref[...]
    rate_ref[...] = pay_ref[8:9, 0:heads]
    bias_ref[...] = pay_ref[8:9, heads : 2 * heads]
    conv_ref[...] = jnp.concatenate([pay_ref[0:4, :], pay_ref[4:8, :]], axis=1)


def emit(encoded, pay, heads):
    return pl.pallas_call(
        emit_kernel,
        out_shape=(
            jax.ShapeDtypeStruct(encoded.shape, BF16),
            jax.ShapeDtypeStruct((1, heads), F32),
            jax.ShapeDtypeStruct((1, heads), F32),
            jax.ShapeDtypeStruct((4, 256), F32),
        ),
        in_specs=[VM] * 2,
        out_specs=(VM,) * 4,
        name="emit",
    )(encoded, pay)


def solution(mesh):
    count = mesh.shape["ctx"]
    z_size = count // 4

    def on_device(*args):
        own = args[-1].shape[0]
        loss_scale = 1.0 / math.sqrt(own * count * HEAD)

        def place():
            return lax.axis_index("ctx"), lax.axis_index("tp")

        heads = args[11].shape[0] * mesh.shape["tp"]
        encoded, pay = layer((args[0].reshape(2, 128),) + args[1:], place, loss_scale, z_size)
        encoded, rate, bias, conv = emit(encoded, pay, heads)
        return encoded, rate.reshape(-1), bias.reshape(-1), conv

    tp = P("tp")
    cols = P(None, "tp")
    in_specs = (
        P("ctx"), P(), P(), P(), cols, cols, P(), cols, cols, P(), tp, tp, tp, tp, P("ctx", "tp"),
    )
    return jax.shard_map(
        on_device, mesh=mesh, in_specs=in_specs,
        out_specs=(P("ctx", "tp"), P(), P(), P()), check_vma=False,
    )
```

```python
import math

import jax
import jax.numpy as jnp
from jax import lax
from jax.experimental import pallas as pl
from jax.experimental.pallas import tpu as pltpu
from jax.sharding import PartitionSpec as P

F32 = jnp.float32
BF16 = jnp.bfloat16
HEAD = 128
CONV = 4
EPS = 1e-05
MESH = pl.DeviceIdType.MESH
VM = pl.BlockSpec(memory_space=pltpu.VMEM)


def split(v):
    hi = v.astype(BF16)
    return hi, (v - hi.astype(F32)).astype(BF16)


def dot(a, b, ca=1, cb=0):
    return lax.dot_general(a, b, (((ca,), (cb,)), ((), ())), preferred_element_type=F32)


def lhs3(v):
    hi, lo = v
    return jnp.concatenate([hi, lo, hi], axis=1)


def rhs3(v, axis=0):
    hi, lo = v
    return jnp.concatenate([hi, hi, lo], axis=axis)


def silu(v):
    return v / (1.0 + jnp.exp(-v))


def silu_slope(v):
    s = 1.0 / (1.0 + jnp.exp(-v))
    return s + v * s * (1.0 - s)


def fold(v):
    return v[:, :128] + v[:, 128:]


def iota(shape, dim):
    return lax.broadcasted_iota(jnp.int32, shape, dim)


def back_one(v, fill):
    rolled = pltpu.roll(v, 1, 1)
    wrapped = pltpu.roll(rolled, 1, 0)
    moved = jnp.where(iota(v.shape, 1) == 0, wrapped, rolled)
    first = (iota(v.shape, 0) == 0) & (iota(v.shape, 1) == 0)
    return jnp.where(first, fill, moved)


def ahead_one(v, fill):
    rows, lanes = v.shape
    rolled = pltpu.roll(v, lanes - 1, 1)
    wrapped = pltpu.roll(rolled, rows - 1, 0)
    moved = jnp.where(iota(v.shape, 1) == lanes - 1, wrapped, rolled)
    last = (iota(v.shape, 0) == rows - 1) & (iota(v.shape, 1) == lanes - 1)
    return jnp.where(last, fill, moved)


def softplus(v):
    return jnp.maximum(v, 0.0) + jnp.log1p(jnp.exp(-jnp.abs(v)))


SIZES = {"x": 4, "z": 8, "y": 4, "c": 2}


def offsets(axes):
    steps = [()]
    for axis in axes:
        steps = [step + (d,) for step in steps for d in range(SIZES[axis])]

    def hops(step):
        return sum(min(d, SIZES[axis] - d) for axis, d in zip(axes, step) if axis != "c")

    return sorted(steps[1:], key=lambda step: -hops(step))


class Links:
    def __init__(self, refs):
        (self.held, self.slots, self.sent, self.tok_send, self.tok_recv, self.sum_send,
         self.sum_recv) = refs
        ctx, tp = lax.axis_index("ctx"), lax.axis_index("tp")
        self.ctx = ctx
        self.here = {
            "x": ctx // SIZES["z"], "z": lax.rem(ctx, SIZES["z"]),
            "y": tp // SIZES["c"], "c": lax.rem(tp, SIZES["c"]),
        }
        self.drains = []

    def moved(self, axes, step):
        there = dict(self.here)
        for axis, d in zip(axes, step):
            if d:
                there[axis] = lax.rem(there[axis] + d, SIZES[axis])
        return there

    def device(self, there):
        return {
            "ctx": there["x"] * SIZES["z"] + there["z"], "tp": there["y"] * SIZES["c"] + there["c"]
        }

    def greet(self):
        barrier = pltpu.get_barrier_semaphore()
        self.greeted = 0
        plane = [step for step in offsets("xy") if step[1]]
        for axes, steps in (("xz", offsets("xz")), ("xy", plane), ("c", offsets("c"))):
            for step in steps:
                device = self.device(self.moved(axes, step))
                pl.semaphore_signal(barrier, inc=1, device_id=device, device_id_type=MESH)
                self.greeted += 1

    def met(self):
        pl.semaphore_wait(pltpu.get_barrier_semaphore(), self.greeted)

    def send_tokens(self, tok_ref):
        for k, step in enumerate(offsets("xz")):
            copy = pltpu.make_async_remote_copy(
                src_ref=tok_ref,
                dst_ref=self.held.at[self.ctx],
                send_sem=self.tok_send.at[k],
                recv_sem=self.tok_recv.at[self.ctx],
                device_id=self.device(self.moved("xz", step)),
                device_id_type=MESH,
            )
            copy.start()
            self.drains.append(copy)
        self.held[self.ctx] = tok_ref[...]

    def take_one(self, tok_ref, source):
        pltpu.make_async_remote_copy(
            src_ref=tok_ref,
            dst_ref=self.held.at[source],
            send_sem=self.tok_send.at[0],
            recv_sem=self.tok_recv.at[source],
            device_id={"ctx": source},
            device_id_type=MESH,
        ).wait_recv()

    def take_tokens(self, tok_ref, steps):
        count = self.held.shape[0]
        for k in steps:
            self.take_one(tok_ref, lax.rem(self.ctx + k, count))

    def reduce(self, value):
        base = 0
        for number, axes in enumerate(("c", "xy", "z")):
            self.sent[number] = value
            steps = offsets(axes)

            def slot(there):
                place = 0
                for axis in axes:
                    place = place * SIZES[axis] + there[axis]
                return base + place

            def copy(k, there, place):
                return pltpu.make_async_remote_copy(
                    src_ref=self.sent.at[number],
                    dst_ref=self.slots.at[place],
                    send_sem=self.sum_send.at[base + k],
                    recv_sem=self.sum_recv.at[place],
                    device_id=self.device(there),
                    device_id_type=MESH,
                )

            for k, step in enumerate(steps):
                sending = copy(k, self.moved(axes, step), slot(self.here))
                sending.start()
                self.drains.append(sending)
            self.slots[slot(self.here)] = value
            for step in reversed(steps):
                there = self.moved(axes, step)
                copy(0, there, slot(there)).wait_recv()
            value = self.slots[base]
            for i in range(1, len(steps) + 1):
                value = value + self.slots[base + i]
            base += len(steps) + 1
        return value

    def drain(self):
        for copy in self.drains:
            copy.wait_send()


def layer_kernel(
    place, links, sources, enc_hbm, pay_ref, held, stores, kmer_ref, last_ref, rows_ref, decay_ref, load_sem,
    xh_ref, xl_ref, y_ref, gate_ref, grow_ref, dg_ref, score_ref, gh_ref, gl_ref, car_ref, enc_ref,
    *, loss_scale,
):
    if links is not None:
        links.greet()
    loads = [
        pltpu.make_async_copy(source, store, load_sem.at[n])
        for n, (source, store) in enumerate(zip(sources, stores))
    ]
    for load in loads:
        load.start()
    (tok_ref, rc, bias, log_rate, skip, emb_ref, ng_ref, cv_ref, cs_ref, hg_ref, ws_ref, wst_ref,
     wv_ref, wg_ref, cot_ref) = stores
    me, slot = place()
    blocks = held.shape[0]
    chunks = 2 * blocks
    inner = cv_ref.shape[1]
    heads = inner // HEAD
    own = cot_ref.shape[0]
    width = inner + 2 * HEAD
    for load in loads[:10]:
        load.wait()
    e = emb_ref[...].astype(F32)
    scale = lax.rsqrt(jnp.mean(e * e, axis=1, keepdims=True) + EPS)
    normed = (e * scale * ng_ref[...]).astype(BF16)
    normed = jnp.concatenate([normed, jnp.zeros((12, e.shape[1]), BF16)], axis=0)
    loads[10].wait()
    table_s = dot(normed, ws_ref[...])[0:4]
    loads[11].wait()
    table_d = dot(normed, wst_ref[...], 1, 1)[0:4]
    loads[12].wait()
    table_v = dot(normed, wv_ref[...])[0:4]
    if links is not None:
        links.met()
        links.send_tokens(tok_ref)
    loads[13].wait()
    table_z = dot(normed, wg_ref[...])[0:4]
    lane_h = iota((1, heads), 1)
    bias_row = jnp.zeros((1, heads), F32)
    rate_row = jnp.zeros((1, heads), F32)
    for h in range(heads):
        bias_row = jnp.where(lane_h == h, bias[h], bias_row)
        rate_row = jnp.where(lane_h == h, log_rate[h], rate_row)
    rate_row = jnp.exp(rate_row)
    pre_step = table_d + bias_row
    step_t = softplus(pre_step)
    sig_t = 1.0 / (1.0 + jnp.exp(-pre_step))
    ratio_t = jnp.where(step_t > 0.0, sig_t / step_t, 1.0)
    gate_t = silu(table_z)
    table_vs = jnp.concatenate([table_v, table_s], axis=1)
    taps = jnp.concatenate([cv_ref[...], cs_ref[...]], axis=1)
    none2 = jnp.zeros((4, 2 * heads), F32)
    rest = jnp.zeros((4, 128 - 3 * heads), F32)
    tail = jnp.concatenate(
        [
            gate_t,
            step_t, step_t, -rate_row * step_t, rest,
            none2, sig_t, rest,
            none2, ratio_t, rest,
        ],
        axis=1,
    )
    parts = []
    for k in range(CONV):
        last = tail if k == CONV - 1 else jnp.zeros_like(tail)
        parts.append(jnp.concatenate([table_vs * taps[k : k + 1], last], axis=1))
    per_tap = jnp.concatenate(parts, axis=0)
    p_hi = per_tap.astype(BF16)
    p_rest = per_tap - p_hi.astype(F32)
    p_mid = p_rest.astype(BF16)
    p_low = (p_rest - p_mid.astype(F32)).astype(BF16)
    per_tap3 = jnp.concatenate([p_hi, p_mid, p_low], axis=0)
    place_cols = width + inner

    column = iota((256, 48), 1) % 16
    index, tap = iota((256, 48), 0), column // 4
    digit = lax.shift_right_logical(index & 63, jnp.maximum(2 * (2 - tap), 0)) & 3
    digit = jnp.where(tap == 3, lax.shift_right_logical(index, 6), digit)
    kmer_hits = (digit == column % 4).astype(F32).astype(BF16)
    kmer_sum = dot(kmer_hits, per_tap3[:, : inner + HEAD])
    kmer_tail = dot(kmer_hits, per_tap3[:, place_cols:])
    kx = silu(kmer_sum[:, :inner])
    kb = silu(kmer_sum[:, inner:])
    kb_slope = silu_slope(kmer_sum[:, inner:])

    tri_in = (iota((own, own), 0) <= iota((own, own), 1)).astype(BF16)
    tri_out = (iota((own, own), 0) >= iota((own, own), 1)).astype(BF16)
    pad4 = jnp.zeros((12, own), BF16)

    def complement(v):
        out = jnp.full(v.shape, -1.0, F32)
        for a in range(4):
            out = jnp.where(v == a, rc[a].astype(F32), out)
        return out

    pair = tok_ref[...].astype(F32)
    mine = jnp.concatenate([pair[0:1], pair[1:2]], axis=1)
    mine_rc = complement(mine)
    letters = iota((4, own), 0).astype(F32)
    own_f = (jnp.broadcast_to(mine, (4, own)) == letters).astype(F32)
    own_r = (jnp.broadcast_to(mine_rc, (4, own)) == letters).astype(F32)
    n_f = dot(jnp.concatenate([own_f.astype(BF16), pad4], axis=0), tri_in)
    n_r = dot(jnp.concatenate([own_r.astype(BF16), pad4], axis=0), tri_out)

    def blend(weights, table, h):
        return sum(weights[a : a + 1] * table[a : a + 1, h : h + 1] for a in range(4))

    cum_rows, sig_rows, step_rows, ratio_rows = [], [], [], []
    for counted, hit in ((n_f, own_f), (n_r, own_r)):
        for h in range(heads):
            cum_rows.append(-(rate_row[:, h : h + 1] * blend(counted, step_t, h)))
            sig_rows.append(blend(counted, sig_t, h))
            step_rows.append(blend(hit, step_t, h))
            ratio_rows.append(blend(hit, ratio_t, h))
    cum8 = jnp.concatenate(cum_rows, axis=0)
    both = split(jnp.concatenate([cum8] + sig_rows, axis=0))
    side = jnp.concatenate([both[0], both[1]], axis=0)
    side = jnp.concatenate([side, side], axis=1)
    columns = jnp.transpose(
        jnp.concatenate([cum8, jnp.zeros((128 - 2 * heads, own), F32)], axis=0)
    )
    for n in range(2 * heads):
        if n < heads:
            causal = iota((own, own), 0) >= iota((own, own), 1)
        else:
            causal = iota((own, own), 0) <= iota((own, own), 1)
        cum_c = jnp.broadcast_to(columns[:, n : n + 1], (own, 128))
        for half in range(own // 128):
            at = slice(half * 128, half * 128 + 128)
            decay_ref[n, :, at] = (
                jnp.where(causal[:, at], jnp.exp(cum_c - cum_rows[n][:, at]), 0.0)
                * step_rows[n][:, at]
            )
        part = slice((n % heads) * HEAD, (n % heads + 1) * HEAD)
        grow_ref[n // heads, :, part] = jnp.exp(cum_c)
    loads[14].wait()
    gain = hg_ref[...]
    dg_ref[...] = cot_ref[...].astype(F32) * (gain * loss_scale)

    if links is not None:
        links.take_tokens(tok_ref, (1, blocks - 1))
    earlier = held[lax.rem(me + blocks - 1, blocks)].astype(F32)[1:2]
    later = held[lax.rem(me + 1, blocks)].astype(F32)[0:1]
    earlier = jnp.where(me > 0, earlier, -1.0)
    later = jnp.where(me < blocks - 1, later, -1.0)
    line = jnp.concatenate([earlier, mine, later], axis=1)
    line = jnp.broadcast_to(line, (8, line.shape[1]))
    line_rc = complement(line)
    letters8 = iota((8, own), 0).astype(F32)
    f_hits, r_hits = [], []
    for k in range(CONV):
        d = CONV - 1 - k
        f_line = pltpu.roll(line, d, 1) if d else line
        r_line = pltpu.roll(line_rc, line.shape[1] - d, 1) if d else line_rc
        f_hits.append((f_line[:, 128 : 128 + own] == letters8)[0:4].astype(F32))
        r_hits.append((r_line[:, 128 : 128 + own] == letters8)[0:4].astype(F32))
    hits_t = [jnp.concatenate(f_hits, axis=0), jnp.concatenate(r_hits, axis=0)]
    slopes, c_parts, ct_parts, b_parts = [], [], [], []
    for strand in range(2):
        hits = jnp.concatenate([hits_t[strand]] * 3, axis=0).astype(BF16)
        summed = dot(hits, per_tap3[:, :place_cols], 0, 0)
        gate_ref[strand] = summed[:, width:]
        states = silu(summed[:, inner:width])
        slopes.append(silu_slope(summed[:, inner:width]))
        b_s = split(states[:, :HEAD])
        c_s = split(states[:, HEAD:])
        b_parts.append(b_s)
        c_parts.append(c_s)
        ct_parts.append(split(jnp.transpose(states[:, HEAD:])))
        scores = dot(lhs3(c_s), rhs3(b_s, 1), 1, 1)
        score_ref[strand] = scores
        for h in range(heads):
            part = slice(h * HEAD, (h + 1) * HEAD)
            x_h = silu(summed[:, part])
            x_s = split(x_h)
            xh_ref[strand, :, part] = x_s[0]
            xl_ref[strand, :, part] = x_s[1]
            mixing = split(scores * decay_ref[strand * heads + h])
            y_ref[strand, :, part] = dot(lhs3(mixing), rhs3(x_s)) + skip[h] * x_h

    if links is not None:
        links.take_tokens(tok_ref, range(2, blocks - 1))
    for r in range(blocks):
        kmer_ref[2 * r : 2 * r + 2, :] = held[r].astype(F32)
    tok = kmer_ref[...]
    comp = complement(tok)
    f_shift, r_shift = [tok], [comp]
    for _ in range(CONV - 1):
        f_shift.append(back_one(f_shift[-1], -1.0))
        r_shift.append(ahead_one(r_shift[-1], -1.0))

    row = iota(tok.shape, 0)
    position = row * 128 + iota(tok.shape, 1)
    before = row < 2 * me
    outside = before | (row >= 2 * me + 2)
    kmer_f = f_shift[1] + 4.0 * f_shift[2] + 16.0 * f_shift[3]
    kmer_r = r_shift[1] + 4.0 * r_shift[2] + 16.0 * r_shift[3]
    kmer = jnp.where(before, kmer_f, kmer_r)
    edge = (before & (position < CONV - 1)) | (position >= chunks * 128 - (CONV - 1))
    kmer_ref[...] = jnp.where(edge & outside, -1.0, kmer)
    mixed = jnp.where(outside, jnp.where(before, tok, comp), -1.0)
    last_ref[...] = mixed
    tri = (iota((128, 128), 0) <= iota((128, 128), 1)).astype(BF16)
    ones = jnp.ones((128, 128), BF16)
    strict = (iota((chunks, chunks), 1) < iota((chunks, chunks), 0)).astype(BF16)
    counts = []
    for a in range(4):
        hit = (mixed == a).astype(F32)
        hit16 = hit.astype(BF16)
        within = dot(hit16, tri)
        offset = dot(strict, dot(hit16, ones).astype(BF16))
        total_f = jnp.sum(jnp.where(before, hit, 0.0), keepdims=True)
        inclusive = within + offset - total_f
        counts.append(jnp.where(before, -inclusive, inclusive - hit))
    for h in range(heads):
        steps_sum = sum(counts[a] * step_t[a : a + 1, h : h + 1] for a in range(4))
        sig_sum = sum(counts[a] * sig_t[a : a + 1, h : h + 1] for a in range(4))
        exponent = -(rate_row[:, h : h + 1] * steps_sum)
        decay = jnp.where(outside, jnp.exp(exponent), 0.0)
        for q, value in enumerate((decay, decay * exponent, decay * sig_sum)):
            base = (q * heads + h) * chunks
            rows_ref[base : base + chunks, :] = value
    for q in range(3 * heads, 16):
        rows_ref[q * chunks : (q + 1) * chunks, :] = jnp.zeros((chunks, 128), F32)

    first_id = iota((64, 128), 0).astype(F32).astype(BF16)
    one16, zero16 = jnp.ones((64, 128), BF16), jnp.zeros((64, 128), BF16)
    nothing = jnp.zeros((32, 128), BF16)

    def load_rows(chunk):
        return rows_ref[pl.ds(chunk, 16, stride=chunks), :]

    acc_f = jnp.zeros((64, 128), F32)
    acc_r = jnp.zeros((64, 128), F32)
    for block in range(blocks):
        hits, weights = [], []
        for chunk in (2 * block, 2 * block + 1):
            w = jnp.concatenate(split(load_rows(chunk)), axis=0)
            final = jnp.broadcast_to(last_ref[chunk : chunk + 1, :], (32, 128)).astype(BF16)
            weights.append(
                jnp.concatenate([jnp.where(final == a, w, nothing) for a in range(4)], axis=0)
            )
            ids = jnp.broadcast_to(kmer_ref[chunk : chunk + 1, :], (64, 128)).astype(BF16)
            hits.append(jnp.where(ids == first_id, one16, zero16))
        found = dot(jnp.concatenate(hits, axis=1), jnp.concatenate(weights, axis=1), 1, 1)
        acc_f = acc_f + jnp.where(block < me, found, 0.0)
        acc_r = acc_r + jnp.where(block > me, found, 0.0)
    lane = iota((16, 128), 1)
    e_f = split(jnp.where(lane < CONV - 1, load_rows(0), 0.0))
    e_r = split(jnp.where(lane >= 128 - (CONV - 1), load_rows(chunks - 1), 0.0))
    pick_row = iota((16, 128), 0)
    pick = (lane == jnp.where(pick_row < 8, pick_row, pick_row + 112)).astype(BF16)

    def by_row(acc, ends):
        parts = [acc] + [pltpu.roll(acc, 128 - 32 * a, 1) for a in range(1, 4)]
        ends = jnp.concatenate([ends[0], ends[1], jnp.zeros((96, 128), BF16)], axis=0)
        joined = jnp.concatenate(parts + [dot(pick, ends, 1, 1)], axis=0)
        return joined + pltpu.roll(joined, 128 - 16, 1)

    joined = (by_row(acc_f, e_f), by_row(acc_r, e_r))

    end_hits = []
    for k in range(CONV):
        d = CONV - 1 - k
        ends = jnp.where(
            iota((1, 128), 1) < 64, f_shift[d][0:1, :], r_shift[d][chunks - 1 : chunks, :]
        )
        end_hits.append(
            (jnp.broadcast_to(ends, (4, 128)) == iota((4, 128), 0).astype(F32)).astype(F32)
        )
    end_hits = jnp.concatenate(end_hits, axis=0).astype(BF16)
    end_pick = dot(end_hits, pick, 1, 1)
    end3 = jnp.concatenate([end_pick] * 3, axis=0).astype(BF16)
    end_sum = dot(end3, per_tap3, 0, 0)
    kx = jnp.concatenate([kx, silu(end_sum[:, :inner])], axis=0)
    kb = jnp.concatenate([kb, silu(end_sum[:, inner : inner + HEAD])], axis=0)
    kb_slope = jnp.concatenate([kb_slope, silu_slope(end_sum[:, inner : inner + HEAD])], axis=0)
    k_tail = jnp.concatenate([kmer_tail, end_sum[:, place_cols:]], axis=0)
    table_rows = kx.shape[0]

    lanes = iota((1, 128), 1)
    lane_rate = jnp.zeros((1, 128), F32)
    for h in range(heads):
        lane_rate = jnp.where(lanes == 2 * heads + h, -rate_row[:, h : h + 1], lane_rate)
    lane_one = jnp.where((lanes >= heads) & (lanes < 2 * heads), 1.0, lane_rate)
    weights, ratios, kxw_parts = [], [], []
    for strand in range(2):
        source = joined[strand]
        w = k_tail[:, 0:128] * source
        e4, e8 = pltpu.roll(source, heads, 1), pltpu.roll(source, 2 * heads, 1)
        decay = jnp.where((lanes >= heads) & (lanes < 2 * heads), e4, e8)
        kept = (decay > 0.0) & (lanes >= heads) & (lanes < 3 * heads)
        ratio = jnp.where(
            kept, lane_one * source / jnp.where(kept, decay, 1.0) + k_tail[:, 256:384], 0.0
        )
        ratio = jnp.concatenate(
            [ratio, jnp.zeros((384 - table_rows, 128), F32)], axis=0
        )
        ratio = split(jnp.transpose(ratio)[0:16, :table_rows])
        ratios.append(jnp.concatenate([ratio[0], ratio[1]], axis=0))
        kxw_parts.append(
            split(
                jnp.concatenate(
                    [
                        kx[:, h * HEAD : (h + 1) * HEAD]
                        * jnp.broadcast_to(w[:, h : h + 1], (table_rows, HEAD))
                        for h in range(heads)
                    ],
                    axis=1,
                )
            )
        )
    kb_t = jnp.concatenate([kb, jnp.zeros((384 - table_rows, HEAD), F32)], axis=0)
    kb_t = split(jnp.transpose(kb_t)[:, :table_rows])

    d_kb = [jnp.zeros(kb.shape, F32)]
    rate_grads = [jnp.zeros((1, 128), F32)] * heads
    bias_grads = [jnp.zeros((1, 128), F32)] * heads
    tap_sums = [jnp.zeros((16, 2 * HEAD), F32)]
    starts, d_scores, d_starts = [], [None, None], [None, None]
    for strand in range(2):
        kxw = kxw_parts[strand]
        start = dot(kb_t[0], kxw[0]) + (dot(kb_t[0], kxw[1]) + dot(kb_t[1], kxw[0]))
        starts.append(split(start))
        car_ref[strand] = dot(lhs3(c_parts[strand]), rhs3(starts[strand]))

    def head_pass(strand, h):
        n = strand * heads + h
        part = slice(h * HEAD, (h + 1) * HEAD)
        grow = grow_ref[strand, :, part]
        from_start = grow * car_ref[strand, :, part]
        gate = gate_ref[strand, :, part]
        gated = (y_ref[strand, :, part] + from_start) * gate
        inv = lax.rsqrt(jnp.mean(gated * gated, axis=1, keepdims=True) + EPS)
        normal = gated * inv
        out = normal * gain[:, part]
        if strand == 0:
            y_ref[0, :, part] = out
        else:
            enc_ref[:, part] = (y_ref[0, :, part] + out).astype(BF16)
        d_normal = dg_ref[:, part]
        d_y = d_normal - normal * jnp.mean(normal * d_normal, axis=1, keepdims=True)
        d_y = (d_y * inv) * gate
        x_s = (xh_ref[strand, :, part], xl_ref[strand, :, part])
        mixed_grad = dot(lhs3(split(d_y)), rhs3(x_s, 1), 1, 1) * decay_ref[n]
        d_scores[strand] = mixed_grad if h == 0 else d_scores[strand] + mixed_grad
        weighted = mixed_grad * score_ref[strand]
        wsum = split(fold(weighted) + d_y * from_start)
        moved = dot(side, jnp.concatenate([wsum[0], wsum[1]], axis=0))
        col_sum = jnp.sum(weighted, axis=0, keepdims=True)
        grown = split(d_y * grow)
        gh_ref[strand, :, part] = grown[0]
        gl_ref[strand, :, part] = grown[1]
        rate = rate_row[:, h : h + 1]
        rows = 2 * heads
        rate_grads[h] = (
            rate_grads[h]
            + (moved[n : n + 1] + moved[2 * rows + n : 2 * rows + n + 1])
            - fold(col_sum * cum_rows[n])
        )
        bias_grads[h] = (
            bias_grads[h]
            + fold(col_sum * (rate * sig_rows[n] + ratio_rows[n]))
            - rate * (moved[rows + n : rows + n + 1] + moved[3 * rows + n : 3 * rows + n + 1])
        )

    def state_pass(strand):
        grown = (gh_ref[strand], gl_ref[strand])
        d_starts[strand] = split(dot(lhs3(ct_parts[strand]), rhs3(grown)))

    def table_pass(strand, h):
        part = slice(h * HEAD, (h + 1) * HEAD)
        d_start_h = (d_starts[strand][0][:, part], d_starts[strand][1][:, part])
        pulled = dot(
            lhs3((kxw_parts[strand][0][:, part], kxw_parts[strand][1][:, part])), rhs3(d_start_h, 1), 1, 1
        )
        d_kb[0] = d_kb[0] + pulled
        t = split(pulled * kb)
        slope = dot(ratios[strand], t[0]) + dot(ratios[strand], t[1])
        slope = slope[0:16] + slope[16:32]
        rate_grads[h] = rate_grads[h] + slope[heads + h : heads + h + 1]
        bias_grads[h] = bias_grads[h] + slope[2 * heads + h : 2 * heads + h + 1]

    def local_pass(strand):
        d_scores_s = split(d_scores[strand])
        d_c = dot(lhs3(d_scores_s), rhs3(b_parts[strand])) + dot(lhs3((gh_ref[strand], gl_ref[strand])), rhs3(starts[strand], 1), 1, 1)
        d_b = dot(lhs3(split(jnp.transpose(d_scores[strand]))), rhs3(c_parts[strand]))
        d_sum = split(jnp.concatenate([d_b, d_c], axis=1) * slopes[strand])
        hits = hits_t[strand].astype(BF16)
        tap_sums[0] = tap_sums[0] + dot(
            jnp.concatenate([hits, hits], axis=1), jnp.concatenate([d_sum[0], d_sum[1]], axis=0)
        )

    for h in range(heads):
        head_pass(0, h)
    state_pass(0)
    for h in range(heads):
        head_pass(1, h)
        table_pass(0, h)
    leave = pltpu.make_async_copy(enc_ref, enc_hbm, load_sem.at[len(loads)])
    leave.start()
    local_pass(0)
    state_pass(1)
    for h in range(heads):
        table_pass(1, h)
    local_pass(1)
    d_kb, tap_sums = d_kb[0], tap_sums[0]
    d_kb = split(d_kb * kb_slope)
    b_sums = dot(kmer_hits[:, 0:16], d_kb[0][0:256], 0, 0)
    b_sums = b_sums + dot(kmer_hits[:, 0:16], d_kb[1][0:256], 0, 0)
    end_pick = end_pick.astype(BF16)
    b_sums = b_sums + dot(end_pick, d_kb[0][256:]) + dot(end_pick, d_kb[1][256:])
    tap_sums = tap_sums + jnp.concatenate([b_sums, jnp.zeros_like(b_sums)], axis=1)
    conv_rows = []
    for k in range(CONV):
        conv_rows.append(
            jnp.sum(tap_sums[4 * k : 4 * k + 4] * table_s, axis=0, keepdims=True)
        )
    sums = jnp.sum(jnp.concatenate(rate_grads + bias_grads, axis=0), axis=1, keepdims=True)
    lane8 = iota((8, 128), 1)
    row8 = iota((8, 128), 0)
    last = jnp.zeros((8, 128), F32)
    head_total = 8 * heads
    for h in range(heads):
        at = slot * heads + h
        last = jnp.where((row8 == 0) & (lane8 == at), sums[h : h + 1], last)
        last = jnp.where(
            (row8 == 0) & (lane8 == head_total + at), sums[heads + h : heads + h + 1], last
        )
    conv = jnp.concatenate(conv_rows, axis=0)
    value = jnp.concatenate([conv[:, :128], conv[:, 128:], last[0:1]], axis=0)
    if links is not None:
        value = links.reduce(value)
    pay_ref[...] = value
    leave.wait()
    if links is not None:
        links.drain()


def layer(args, place, loss_scale, everyone=None, interpret=False):
    (tokens, rc_map, embedding, norm_gain, w_values, w_gates, w_states, w_steps, conv_values,
     conv_states, step_bias, log_rate, skip_gain, head_gain, cotangent) = args
    own, inner = cotangent.shape
    blocks = SIZES["x"] * SIZES["z"]
    chunks = 2 * blocks
    hbm = pl.BlockSpec(memory_space=pl.ANY)
    inputs = [
        tokens, rc_map, step_bias, log_rate, skip_gain, embedding, norm_gain.reshape(1, -1),
        conv_values, conv_states, head_gain.reshape(1, -1), w_states, w_steps.T, w_values, w_gates,
        cotangent,
    ]
    count = len(inputs)
    stores = [
        (pltpu.SMEM if 1 <= n <= 4 else pltpu.VMEM)(a.shape, a.dtype) for n, a in enumerate(inputs)
    ]
    scratch = [
        pltpu.VMEM((chunks, 128), F32),
        pltpu.VMEM((chunks, 128), F32),
        pltpu.VMEM((16 * chunks, 128), F32),
        pltpu.VMEM((8, own, own), F32),
        pltpu.SemaphoreType.DMA((count + 1,)),
        pltpu.VMEM((2, own, inner), BF16),
        pltpu.VMEM((2, own, inner), BF16),
        pltpu.VMEM((2, own, inner), F32),
        pltpu.VMEM((2, own, inner), F32),
        pltpu.VMEM((2, own, inner), F32),
        pltpu.VMEM((own, inner), F32),
        pltpu.VMEM((2, own, own), F32),
        pltpu.VMEM((2, own, inner), BF16),
        pltpu.VMEM((2, own, inner), BF16),
        pltpu.VMEM((2, own, inner), F32),
        pltpu.VMEM((own, inner), BF16),
    ]
    slots = SIZES["c"] + SIZES["x"] * SIZES["y"] + SIZES["z"]
    remote = [
        pltpu.VMEM((blocks, 2, 128), jnp.int32),
        pltpu.VMEM((slots, 9, 128), F32),
        pltpu.VMEM((3, 9, 128), F32),
        pltpu.SemaphoreType.DMA((blocks,)),
        pltpu.SemaphoreType.DMA((blocks,)),
        pltpu.SemaphoreType.DMA((slots,)),
        pltpu.SemaphoreType.DMA((slots,)),
    ]
    shapes = (
        jax.ShapeDtypeStruct((own, inner), BF16),
        jax.ShapeDtypeStruct((9, 128), F32),
    )
    alone = everyone is not None

    def body(*refs):
        refs = list(refs)
        sources, refs = refs[:count], refs[count:]
        if alone:
            links, held, refs = None, refs[0], refs[1:]
            out, refs = refs[:2], refs[2:]
        else:
            out, refs = refs[:2], refs[2:]
            links, held, refs = Links(refs[:7]), refs[0], refs[7:]
        layer_kernel(
            place, links, sources, *out, held, refs[:count], *refs[count:], loss_scale=loss_scale
        )

    if alone:
        params = pltpu.CompilerParams(vmem_limit_bytes=60 * 1024 * 1024)
    else:
        params = pltpu.CompilerParams(
            vmem_limit_bytes=60 * 1024 * 1024, collective_id=0, has_side_effects=True
        )
    return pl.pallas_call(
        body,
        out_shape=shapes,
        in_specs=[hbm] * count + [VM] * alone,
        out_specs=(hbm, VM),
        scratch_shapes=([] if alone else remote) + stores + scratch,
        compiler_params=params,
        interpret=interpret,
        name="layer",
    )(*inputs, *([everyone] if alone else []))


def emit_kernel(enc_ref, pay_ref, out_ref, rate_ref, bias_ref, conv_ref):
    heads = rate_ref.shape[1]
    out_ref[...] = enc_ref[...]
    rate_ref[...] = pay_ref[8:9, 0:heads]
    bias_ref[...] = pay_ref[8:9, heads : 2 * heads]
    conv_ref[...] = jnp.concatenate([pay_ref[0:4, :], pay_ref[4:8, :]], axis=1)


def emit(encoded, pay, heads):
    return pl.pallas_call(
        emit_kernel,
        out_shape=(
            jax.ShapeDtypeStruct(encoded.shape, BF16),
            jax.ShapeDtypeStruct((1, heads), F32),
            jax.ShapeDtypeStruct((1, heads), F32),
            jax.ShapeDtypeStruct((4, 256), F32),
        ),
        in_specs=[VM] * 2,
        out_specs=(VM,) * 4,
        name="emit",
    )(encoded, pay)


def solution(mesh):
    count = mesh.shape["ctx"]

    def on_device(*args):
        own = args[-1].shape[0]
        loss_scale = 1.0 / math.sqrt(own * count * HEAD)

        def place():
            return lax.axis_index("ctx"), lax.axis_index("tp")

        heads = args[11].shape[0] * mesh.shape["tp"]
        encoded, pay = layer((args[0].reshape(2, 128),) + args[1:], place, loss_scale)
        encoded, rate, bias, conv = emit(encoded, pay, heads)
        return encoded, rate.reshape(-1), bias.reshape(-1), conv

    tp = P("tp")
    cols = P(None, "tp")
    in_specs = (
        P("ctx"), P(), P(), P(), cols, cols, P(), cols, cols, P(), tp, tp, tp, tp, P("ctx", "tp"),
    )
    return jax.shard_map(
        on_device, mesh=mesh, in_specs=in_specs,
        out_specs=(P("ctx", "tp"), P(), P(), P()), check_vma=False,
    )
```

```python
import math

import jax
import jax.numpy as jnp
from jax import lax
from jax.experimental import pallas as pl
from jax.experimental.pallas import tpu as pltpu
from jax.sharding import PartitionSpec as P

F32 = jnp.float32
BF16 = jnp.bfloat16
HEAD = 128
CONV = 4
EPS = 1e-05
MESH = pl.DeviceIdType.MESH
VM = pl.BlockSpec(memory_space=pltpu.VMEM)


def split(v):
    hi = v.astype(BF16)
    return hi, (v - hi.astype(F32)).astype(BF16)


def dot(a, b, ca=1, cb=0):
    return lax.dot_general(a, b, (((ca,), (cb,)), ((), ())), preferred_element_type=F32)


def lhs3(v):
    hi, lo = v
    return jnp.concatenate([hi, lo, hi], axis=1)


def rhs3(v, axis=0):
    hi, lo = v
    return jnp.concatenate([hi, hi, lo], axis=axis)


def silu(v):
    return v / (1.0 + jnp.exp(-v))


def silu_slope(v):
    s = 1.0 / (1.0 + jnp.exp(-v))
    return s + v * s * (1.0 - s)


def fold(v):
    return v[:, :128] + v[:, 128:]


def iota(shape, dim):
    return lax.broadcasted_iota(jnp.int32, shape, dim)


def back_one(v, fill):
    rolled = pltpu.roll(v, 1, 1)
    wrapped = pltpu.roll(rolled, 1, 0)
    moved = jnp.where(iota(v.shape, 1) == 0, wrapped, rolled)
    first = (iota(v.shape, 0) == 0) & (iota(v.shape, 1) == 0)
    return jnp.where(first, fill, moved)


def ahead_one(v, fill):
    rows, lanes = v.shape
    rolled = pltpu.roll(v, lanes - 1, 1)
    wrapped = pltpu.roll(rolled, rows - 1, 0)
    moved = jnp.where(iota(v.shape, 1) == lanes - 1, wrapped, rolled)
    last = (iota(v.shape, 0) == rows - 1) & (iota(v.shape, 1) == lanes - 1)
    return jnp.where(last, fill, moved)


def softplus(v):
    return jnp.maximum(v, 0.0) + jnp.log1p(jnp.exp(-jnp.abs(v)))


SIZES = {"x": 4, "z": 8, "y": 4, "c": 2}


def offsets(axes):
    steps = [()]
    for axis in axes:
        steps = [step + (d,) for step in steps for d in range(SIZES[axis])]

    def hops(step):
        return sum(min(d, SIZES[axis] - d) for axis, d in zip(axes, step) if axis != "c")

    return sorted(steps[1:], key=lambda step: -hops(step))


class Links:
    def __init__(self, refs):
        (self.held, self.near, self.slots, self.sent, self.tok_send, self.tok_recv,
         self.sum_send, self.sum_recv) = refs
        ctx, tp = lax.axis_index("ctx"), lax.axis_index("tp")
        self.ctx = ctx
        self.here = {
            "x": ctx // SIZES["z"], "z": lax.rem(ctx, SIZES["z"]),
            "y": tp // SIZES["c"], "c": lax.rem(tp, SIZES["c"]),
        }
        self.drains = []

    def moved(self, axes, step):
        there = dict(self.here)
        for axis, d in zip(axes, step):
            if d:
                there[axis] = lax.rem(there[axis] + d, SIZES[axis])
        return there

    def device(self, there):
        return {
            "ctx": there["x"] * SIZES["z"] + there["z"], "tp": there["y"] * SIZES["c"] + there["c"]
        }

    def beside(self, d):
        count = SIZES["x"] * SIZES["z"]
        return {"ctx": lax.rem(self.ctx + d % count, count)}

    def greet(self):
        barrier = pltpu.get_barrier_semaphore()
        devices = [self.device(self.moved("z", step)) for step in offsets("z")]
        devices += [self.device(self.moved("x", step)) for step in offsets("x")]
        devices += [self.beside(1), self.beside(-1)]
        devices += [self.device(self.moved("xy", step)) for step in offsets("xy") if step[1]]
        devices += [self.device(self.moved("c", step)) for step in offsets("c")]
        for device in devices:
            pl.semaphore_signal(barrier, inc=1, device_id=device, device_id_type=MESH)
        self.greeted = len(devices)

    def met(self):
        pl.semaphore_wait(pltpu.get_barrier_semaphore(), self.greeted)

    def token_copy(self, source, target, number, arrives, device):
        return pltpu.make_async_remote_copy(
            src_ref=source, dst_ref=target, send_sem=self.tok_send.at[number],
            recv_sem=self.tok_recv.at[arrives], device_id=device, device_id_type=MESH,
        )

    def send(self, copy):
        copy.start()
        self.drains.append(copy)

    def send_tokens(self, tok_ref):
        x, z = self.here["x"], self.here["z"]
        own = self.held.at[z, x]
        for k, step in enumerate(offsets("x")):
            self.send(self.token_copy(tok_ref, own, k, x, self.device(self.moved("x", step))))
        for k, d in ((3, 1), (4, -1)):
            near = self.near.at[k - 3]
            self.send(self.token_copy(tok_ref, near, k, 9 + k, self.beside(d)))
        self.held[z, x] = tok_ref[...]

    def pass_tokens(self, tok_ref):
        x, z = self.here["x"], self.here["z"]
        for step in reversed(offsets("x")):
            there = self.moved("x", step)
            self.token_copy(
                tok_ref, self.held.at[z, there["x"]], 0, there["x"], self.device(there)
            ).wait_recv()
        row = self.held.at[z]
        for k, step in enumerate(offsets("z")):
            there = self.moved("z", step)
            self.send(self.token_copy(row, row, 5 + k, 4 + z, self.device(there)))

    def take_beside(self, tok_ref):
        for k, d in ((3, 1), (4, -1)):
            self.token_copy(tok_ref, self.near.at[k - 3], k, 9 + k, self.beside(d)).wait_recv()

    def take_tokens(self):
        for step in reversed(offsets("z")):
            there = self.moved("z", step)
            row = self.held.at[there["z"]]
            self.token_copy(row, row, 5, 4 + there["z"], self.device(there)).wait_recv()

    def reduce(self, value):
        base = 0
        for number, axes in enumerate(("c", "xy", "z")):
            self.sent[number] = value
            steps = offsets(axes)
            sending = []

            def slot(there):
                place = 0
                for axis in axes:
                    place = place * SIZES[axis] + there[axis]
                return base + place

            def copy(k, there, place):
                return pltpu.make_async_remote_copy(
                    src_ref=self.sent.at[number],
                    dst_ref=self.slots.at[place],
                    send_sem=self.sum_send.at[base + k],
                    recv_sem=self.sum_recv.at[place],
                    device_id=self.device(there),
                    device_id_type=MESH,
                )

            for k, step in enumerate(steps):
                sending.append(copy(k, self.moved(axes, step), slot(self.here)))
                sending[-1].start()
            self.drain()
            self.drains = sending
            self.slots[slot(self.here)] = value
            for step in reversed(steps):
                there = self.moved(axes, step)
                copy(0, there, slot(there)).wait_recv()
            value = self.slots[base]
            for i in range(1, len(steps) + 1):
                value = value + self.slots[base + i]
            base += len(steps) + 1
        return value

    def drain(self):
        for copy in self.drains:
            copy.wait_send()


def layer_kernel(
    place, links, sources, enc_hbm, pay_ref, held, stores, kmer_ref, last_ref, rows_ref, decay_ref, load_sem,
    xh_ref, xl_ref, y_ref, gate_ref, grow_ref, dg_ref, score_ref, gh_ref, gl_ref, car_ref, enc_ref, kxw_ref,
    *, loss_scale,
):
    if links is not None:
        links.greet()
    loads = [
        pltpu.make_async_copy(source, store, load_sem.at[n])
        for n, (source, store) in enumerate(zip(sources, stores))
    ]
    for load in loads:
        load.start()
    (tok_ref, rc, bias, log_rate, skip, emb_ref, ng_ref, cv_ref, cs_ref, hg_ref, ws_ref, wst_ref,
     wv_ref, wg_ref, cot_ref) = stores
    me, slot = place()
    blocks = SIZES["x"] * SIZES["z"]
    chunks = 2 * blocks
    inner = cv_ref.shape[1]
    heads = inner // HEAD
    own = cot_ref.shape[0]
    width = inner + 2 * HEAD
    for load in loads[:10]:
        load.wait()
    e = emb_ref[...].astype(F32)
    scale = lax.rsqrt(jnp.mean(e * e, axis=1, keepdims=True) + EPS)
    normed = (e * scale * ng_ref[...]).astype(BF16)
    normed = jnp.concatenate([normed, jnp.zeros((12, e.shape[1]), BF16)], axis=0)
    loads[10].wait()
    table_s = dot(normed, ws_ref[...])[0:4]
    loads[11].wait()
    table_d = dot(normed, wst_ref[...], 1, 1)[0:4]
    loads[12].wait()
    table_v = dot(normed, wv_ref[...])[0:4]
    if links is not None:
        links.met()
        links.send_tokens(tok_ref)
    loads[13].wait()
    table_z = dot(normed, wg_ref[...])[0:4]
    lane_h = iota((1, heads), 1)
    bias_row = jnp.zeros((1, heads), F32)
    rate_row = jnp.zeros((1, heads), F32)
    for h in range(heads):
        bias_row = jnp.where(lane_h == h, bias[h], bias_row)
        rate_row = jnp.where(lane_h == h, log_rate[h], rate_row)
    rate_row = jnp.exp(rate_row)
    pre_step = table_d + bias_row
    step_t = softplus(pre_step)
    sig_t = 1.0 / (1.0 + jnp.exp(-pre_step))
    ratio_t = jnp.where(step_t > 0.0, sig_t / step_t, 1.0)
    gate_t = silu(table_z)
    table_vs = jnp.concatenate([table_v, table_s], axis=1)
    taps = jnp.concatenate([cv_ref[...], cs_ref[...]], axis=1)
    none2 = jnp.zeros((4, 2 * heads), F32)
    rest = jnp.zeros((4, 128 - 3 * heads), F32)
    tail = jnp.concatenate(
        [
            gate_t,
            step_t, step_t, -rate_row * step_t, rest,
            none2, sig_t, rest,
            none2, ratio_t, rest,
        ],
        axis=1,
    )
    parts = []
    for k in range(CONV):
        last = tail if k == CONV - 1 else jnp.zeros_like(tail)
        parts.append(jnp.concatenate([table_vs * taps[k : k + 1], last], axis=1))
    per_tap = jnp.concatenate(parts, axis=0)
    p_hi = per_tap.astype(BF16)
    p_rest = per_tap - p_hi.astype(F32)
    p_mid = p_rest.astype(BF16)
    p_low = (p_rest - p_mid.astype(F32)).astype(BF16)
    per_tap3 = jnp.concatenate([p_hi, p_mid, p_low], axis=0)
    place_cols = width + inner

    column = iota((256, 48), 1) % 16
    index, tap = iota((256, 48), 0), column // 4
    digit = lax.shift_right_logical(index & 63, jnp.maximum(2 * (2 - tap), 0)) & 3
    digit = jnp.where(tap == 3, lax.shift_right_logical(index, 6), digit)
    kmer_hits = (digit == column % 4).astype(F32).astype(BF16)
    kmer_sum = dot(kmer_hits, per_tap3[:, : inner + HEAD])
    kmer_tail = dot(kmer_hits, per_tap3[:, place_cols:])
    kx = silu(kmer_sum[:, :inner])
    kb = silu(kmer_sum[:, inner:])
    kb_slope = silu_slope(kmer_sum[:, inner:])

    tri_in = (iota((own, own), 0) <= iota((own, own), 1)).astype(BF16)
    tri_out = (iota((own, own), 0) >= iota((own, own), 1)).astype(BF16)
    pad4 = jnp.zeros((12, own), BF16)

    def complement(v):
        out = jnp.full(v.shape, -1.0, F32)
        for a in range(4):
            out = jnp.where(v == a, rc[a].astype(F32), out)
        return out

    pair = tok_ref[...].astype(F32)
    mine = jnp.concatenate([pair[0:1], pair[1:2]], axis=1)
    mine_rc = complement(mine)
    letters = iota((4, own), 0).astype(F32)
    own_f = (jnp.broadcast_to(mine, (4, own)) == letters).astype(F32)
    own_r = (jnp.broadcast_to(mine_rc, (4, own)) == letters).astype(F32)
    n_f = dot(jnp.concatenate([own_f.astype(BF16), pad4], axis=0), tri_in)
    n_r = dot(jnp.concatenate([own_r.astype(BF16), pad4], axis=0), tri_out)

    def blend(weights, table, h):
        return sum(weights[a : a + 1] * table[a : a + 1, h : h + 1] for a in range(4))

    cum_rows, sig_rows, step_rows, ratio_rows = [], [], [], []
    for counted, hit in ((n_f, own_f), (n_r, own_r)):
        for h in range(heads):
            cum_rows.append(-(rate_row[:, h : h + 1] * blend(counted, step_t, h)))
            sig_rows.append(blend(counted, sig_t, h))
            step_rows.append(blend(hit, step_t, h))
            ratio_rows.append(blend(hit, ratio_t, h))
    cum8 = jnp.concatenate(cum_rows, axis=0)
    both = split(jnp.concatenate([cum8] + sig_rows, axis=0))
    side = jnp.concatenate([both[0], both[1]], axis=0)
    side = jnp.concatenate([side, side], axis=1)
    columns = jnp.transpose(
        jnp.concatenate([cum8, jnp.zeros((128 - 2 * heads, own), F32)], axis=0)
    )
    for n in range(2 * heads):
        if n < heads:
            causal = iota((own, own), 0) >= iota((own, own), 1)
        else:
            causal = iota((own, own), 0) <= iota((own, own), 1)
        cum_c = jnp.broadcast_to(columns[:, n : n + 1], (own, 128))
        for half in range(own // 128):
            at = slice(half * 128, half * 128 + 128)
            decay_ref[n, :, at] = (
                jnp.where(causal[:, at], jnp.exp(cum_c - cum_rows[n][:, at]), 0.0)
                * step_rows[n][:, at]
            )
        part = slice((n % heads) * HEAD, (n % heads + 1) * HEAD)
        grow_ref[n // heads, :, part] = jnp.exp(cum_c)
    loads[14].wait()
    gain = hg_ref[...]
    dg_ref[...] = cot_ref[...].astype(F32) * (gain * loss_scale)

    if links is not None:
        links.pass_tokens(tok_ref)
        links.take_beside(tok_ref)
        earlier, later = links.near[0], links.near[1]
    else:
        earlier, later = (
            held[lax.rem(there, SIZES["z"]), there // SIZES["z"]]
            for there in (lax.rem(me + blocks - 1, blocks), lax.rem(me + 1, blocks))
        )
    earlier, later = earlier.astype(F32)[1:2], later.astype(F32)[0:1]
    earlier = jnp.where(me > 0, earlier, -1.0)
    later = jnp.where(me < blocks - 1, later, -1.0)
    line = jnp.concatenate([earlier, mine, later], axis=1)
    line = jnp.broadcast_to(line, (8, line.shape[1]))
    line_rc = complement(line)
    letters8 = iota((8, own), 0).astype(F32)
    f_hits, r_hits = [], []
    for k in range(CONV):
        d = CONV - 1 - k
        f_line = pltpu.roll(line, d, 1) if d else line
        r_line = pltpu.roll(line_rc, line.shape[1] - d, 1) if d else line_rc
        f_hits.append((f_line[:, 128 : 128 + own] == letters8)[0:4].astype(F32))
        r_hits.append((r_line[:, 128 : 128 + own] == letters8)[0:4].astype(F32))
    hits_t = [jnp.concatenate(f_hits, axis=0), jnp.concatenate(r_hits, axis=0)]
    slopes, c_parts, ct_parts, b_parts = [], [], [], []
    for strand in range(2):
        hits = jnp.concatenate([hits_t[strand]] * 3, axis=0).astype(BF16)
        summed = dot(hits, per_tap3[:, :place_cols], 0, 0)
        gate_ref[strand] = summed[:, width:]
        states = silu(summed[:, inner:width])
        slopes.append(silu_slope(summed[:, inner:width]))
        b_s = split(states[:, :HEAD])
        c_s = split(states[:, HEAD:])
        b_parts.append(b_s)
        c_parts.append(c_s)
        ct_parts.append(split(jnp.transpose(states[:, HEAD:])))
        scores = dot(lhs3(c_s), rhs3(b_s, 1), 1, 1)
        score_ref[strand] = scores
        for h in range(heads):
            part = slice(h * HEAD, (h + 1) * HEAD)
            x_h = silu(summed[:, part])
            x_s = split(x_h)
            xh_ref[strand, :, part] = x_s[0]
            xl_ref[strand, :, part] = x_s[1]
            mixing = split(scores * decay_ref[strand * heads + h])
            y_ref[strand, :, part] = dot(lhs3(mixing), rhs3(x_s)) + skip[h] * x_h

    if links is not None:
        links.take_tokens()
    for r in range(blocks):
        kmer_ref[2 * r : 2 * r + 2, :] = held[r % SIZES["z"], r // SIZES["z"]].astype(F32)
    tok = kmer_ref[...]
    comp = complement(tok)
    f_shift, r_shift = [tok], [comp]
    for _ in range(CONV - 1):
        f_shift.append(back_one(f_shift[-1], -1.0))
        r_shift.append(ahead_one(r_shift[-1], -1.0))

    row = iota(tok.shape, 0)
    position = row * 128 + iota(tok.shape, 1)
    before = row < 2 * me
    outside = before | (row >= 2 * me + 2)
    kmer_f = f_shift[1] + 4.0 * f_shift[2] + 16.0 * f_shift[3]
    kmer_r = r_shift[1] + 4.0 * r_shift[2] + 16.0 * r_shift[3]
    kmer = jnp.where(before, kmer_f, kmer_r)
    edge = (before & (position < CONV - 1)) | (position >= chunks * 128 - (CONV - 1))
    kmer_ref[...] = jnp.where(edge & outside, -1.0, kmer)
    mixed = jnp.where(outside, jnp.where(before, tok, comp), -1.0)
    last_ref[...] = mixed
    tri = (iota((128, 128), 0) <= iota((128, 128), 1)).astype(BF16)
    ones = jnp.ones((128, 128), BF16)
    strict = (iota((chunks, chunks), 1) < iota((chunks, chunks), 0)).astype(BF16)
    counts = []
    for a in range(4):
        hit = (mixed == a).astype(F32)
        hit16 = hit.astype(BF16)
        within = dot(hit16, tri)
        offset = dot(strict, dot(hit16, ones).astype(BF16))
        total_f = jnp.sum(jnp.where(before, hit, 0.0), keepdims=True)
        inclusive = within + offset - total_f
        counts.append(jnp.where(before, -inclusive, inclusive - hit))
    for h in range(heads):
        steps_sum = sum(counts[a] * step_t[a : a + 1, h : h + 1] for a in range(4))
        sig_sum = sum(counts[a] * sig_t[a : a + 1, h : h + 1] for a in range(4))
        exponent = -(rate_row[:, h : h + 1] * steps_sum)
        decay = jnp.where(outside, jnp.exp(exponent), 0.0)
        for q, value in enumerate((decay, decay * exponent, decay * sig_sum)):
            base = (q * heads + h) * chunks
            rows_ref[base : base + chunks, :] = value
    for q in range(3 * heads, 16):
        rows_ref[q * chunks : (q + 1) * chunks, :] = jnp.zeros((chunks, 128), F32)

    first_id = iota((64, 128), 0).astype(F32).astype(BF16)
    one16, zero16 = jnp.ones((64, 128), BF16), jnp.zeros((64, 128), BF16)
    nothing = jnp.zeros((32, 128), BF16)

    def load_rows(chunk):
        return rows_ref[pl.ds(chunk, 16, stride=chunks), :]

    acc_f = jnp.zeros((64, 128), F32)
    acc_r = jnp.zeros((64, 128), F32)
    for block in range(blocks):
        hits, weights = [], []
        for chunk in (2 * block, 2 * block + 1):
            w = jnp.concatenate(split(load_rows(chunk)), axis=0)
            final = jnp.broadcast_to(last_ref[chunk : chunk + 1, :], (32, 128)).astype(BF16)
            weights.append(
                jnp.concatenate([jnp.where(final == a, w, nothing) for a in range(4)], axis=0)
            )
            ids = jnp.broadcast_to(kmer_ref[chunk : chunk + 1, :], (64, 128)).astype(BF16)
            hits.append(jnp.where(ids == first_id, one16, zero16))
        found = dot(jnp.concatenate(hits, axis=1), jnp.concatenate(weights, axis=1), 1, 1)
        acc_f = acc_f + jnp.where(block < me, found, 0.0)
        acc_r = acc_r + jnp.where(block > me, found, 0.0)
    lane = iota((16, 128), 1)
    e_f = split(jnp.where(lane < CONV - 1, load_rows(0), 0.0))
    e_r = split(jnp.where(lane >= 128 - (CONV - 1), load_rows(chunks - 1), 0.0))
    pick_row = iota((16, 128), 0)
    pick = (lane == jnp.where(pick_row < 8, pick_row, pick_row + 112)).astype(BF16)

    def by_row(acc, ends):
        parts = [acc] + [pltpu.roll(acc, 128 - 32 * a, 1) for a in range(1, 4)]
        ends = jnp.concatenate([ends[0], ends[1], jnp.zeros((96, 128), BF16)], axis=0)
        joined = jnp.concatenate(parts + [dot(pick, ends, 1, 1)], axis=0)
        return joined + pltpu.roll(joined, 128 - 16, 1)

    joined = (by_row(acc_f, e_f), by_row(acc_r, e_r))

    end_hits = []
    for k in range(CONV):
        d = CONV - 1 - k
        ends = jnp.where(
            iota((1, 128), 1) < 64, f_shift[d][0:1, :], r_shift[d][chunks - 1 : chunks, :]
        )
        end_hits.append(
            (jnp.broadcast_to(ends, (4, 128)) == iota((4, 128), 0).astype(F32)).astype(F32)
        )
    end_hits = jnp.concatenate(end_hits, axis=0).astype(BF16)
    end_pick = dot(end_hits, pick, 1, 1)
    end3 = jnp.concatenate([end_pick] * 3, axis=0).astype(BF16)
    end_sum = dot(end3, per_tap3, 0, 0)
    kx = jnp.concatenate([kx, silu(end_sum[:, :inner])], axis=0)
    kb = jnp.concatenate([kb, silu(end_sum[:, inner : inner + HEAD])], axis=0)
    kb_slope = jnp.concatenate([kb_slope, silu_slope(end_sum[:, inner : inner + HEAD])], axis=0)
    k_tail = jnp.concatenate([kmer_tail, end_sum[:, place_cols:]], axis=0)
    table_rows = kx.shape[0]

    lanes = iota((1, 128), 1)
    lane_rate = jnp.zeros((1, 128), F32)
    for h in range(heads):
        lane_rate = jnp.where(lanes == 2 * heads + h, -rate_row[:, h : h + 1], lane_rate)
    lane_one = jnp.where((lanes >= heads) & (lanes < 2 * heads), 1.0, lane_rate)
    weights, ratios, kxw_parts = [], [], []
    for strand in range(2):
        source = joined[strand]
        w = k_tail[:, 0:128] * source
        e4, e8 = pltpu.roll(source, heads, 1), pltpu.roll(source, 2 * heads, 1)
        decay = jnp.where((lanes >= heads) & (lanes < 2 * heads), e4, e8)
        kept = (decay > 0.0) & (lanes >= heads) & (lanes < 3 * heads)
        ratio = jnp.where(
            kept, lane_one * source / jnp.where(kept, decay, 1.0) + k_tail[:, 256:384], 0.0
        )
        ratio = jnp.concatenate(
            [ratio, jnp.zeros((384 - table_rows, 128), F32)], axis=0
        )
        ratio = split(jnp.transpose(ratio)[0:16, :table_rows])
        ratios.append(jnp.concatenate([ratio[0], ratio[1]], axis=0))
        for h in range(heads):
            part = slice(h * HEAD, (h + 1) * HEAD)
            kxw_ref[strand, :, part] = kx[:, part] * jnp.broadcast_to(
                w[:, h : h + 1], (table_rows, HEAD)
            )
        kxw_parts.append(split(kxw_ref[strand]))
    kb_t = jnp.concatenate([kb, jnp.zeros((384 - table_rows, HEAD), F32)], axis=0)
    kb_t = split(jnp.transpose(kb_t)[:, :table_rows])

    d_kb = [jnp.zeros(kb.shape, F32)]
    rate_grads = [jnp.zeros((1, 128), F32)] * heads
    bias_grads = [jnp.zeros((1, 128), F32)] * heads
    tap_sums = [jnp.zeros((16, 2 * HEAD), F32)]
    starts, d_scores, d_starts = [], [None, None], [None, None]
    for strand in range(2):
        kxw = kxw_parts[strand]
        start = dot(kb_t[0], kxw[0]) + (dot(kb_t[0], kxw[1]) + dot(kb_t[1], kxw[0]))
        starts.append(split(start))
        car_ref[strand] = dot(lhs3(c_parts[strand]), rhs3(starts[strand]))

    def head_pass(strand, h):
        n = strand * heads + h
        part = slice(h * HEAD, (h + 1) * HEAD)
        grow = grow_ref[strand, :, part]
        from_start = grow * car_ref[strand, :, part]
        gate = gate_ref[strand, :, part]
        gated = (y_ref[strand, :, part] + from_start) * gate
        inv = lax.rsqrt(jnp.mean(gated * gated, axis=1, keepdims=True) + EPS)
        normal = gated * inv
        out = normal * gain[:, part]
        if strand == 0:
            y_ref[0, :, part] = out
        else:
            enc_ref[:, part] = (y_ref[0, :, part] + out).astype(BF16)
        d_normal = dg_ref[:, part]
        d_y = d_normal - normal * jnp.mean(normal * d_normal, axis=1, keepdims=True)
        d_y = (d_y * inv) * gate
        x_s = (xh_ref[strand, :, part], xl_ref[strand, :, part])
        mixed_grad = dot(lhs3(split(d_y)), rhs3(x_s, 1), 1, 1) * decay_ref[n]
        d_scores[strand] = mixed_grad if h == 0 else d_scores[strand] + mixed_grad
        weighted = mixed_grad * score_ref[strand]
        wsum = split(fold(weighted) + d_y * from_start)
        moved = dot(side, jnp.concatenate([wsum[0], wsum[1]], axis=0))
        col_sum = jnp.sum(weighted, axis=0, keepdims=True)
        grown = split(d_y * grow)
        gh_ref[strand, :, part] = grown[0]
        gl_ref[strand, :, part] = grown[1]
        rate = rate_row[:, h : h + 1]
        rows = 2 * heads
        rate_grads[h] = (
            rate_grads[h]
            + (moved[n : n + 1] + moved[2 * rows + n : 2 * rows + n + 1])
            - fold(col_sum * cum_rows[n])
        )
        bias_grads[h] = (
            bias_grads[h]
            + fold(col_sum * (rate * sig_rows[n] + ratio_rows[n]))
            - rate * (moved[rows + n : rows + n + 1] + moved[3 * rows + n : 3 * rows + n + 1])
        )

    def state_pass(strand):
        grown = (gh_ref[strand], gl_ref[strand])
        d_starts[strand] = split(dot(lhs3(ct_parts[strand]), rhs3(grown)))

    def table_pass(strand):
        kxw, d_start = kxw_parts[strand], d_starts[strand]
        d_kb[0] = d_kb[0] + dot(lhs3(kxw), rhs3(d_start, 1), 1, 1)
        met = split(dot(lhs3(split(kb)), rhs3(d_start)) * kxw_ref[strand])
        slope = dot(ratios[strand], met[0]) + dot(ratios[strand], met[1])
        slope = slope[0:16] + slope[16:32]
        for h in range(heads):
            part = slice(h * HEAD, (h + 1) * HEAD)
            rate_grads[h] = rate_grads[h] + slope[heads + h : heads + h + 1, part]
            bias_grads[h] = bias_grads[h] + slope[2 * heads + h : 2 * heads + h + 1, part]

    def local_pass(strand):
        d_scores_s = split(d_scores[strand])
        d_c = dot(lhs3(d_scores_s), rhs3(b_parts[strand])) + dot(lhs3((gh_ref[strand], gl_ref[strand])), rhs3(starts[strand], 1), 1, 1)
        d_b = dot(lhs3(split(jnp.transpose(d_scores[strand]))), rhs3(c_parts[strand]))
        d_sum = split(jnp.concatenate([d_b, d_c], axis=1) * slopes[strand])
        hits = hits_t[strand].astype(BF16)
        tap_sums[0] = tap_sums[0] + dot(
            jnp.concatenate([hits, hits], axis=1), jnp.concatenate([d_sum[0], d_sum[1]], axis=0)
        )

    for h in range(heads):
        head_pass(0, h)
    state_pass(0)
    for h in range(heads):
        head_pass(1, h)
        if h == 0:
            table_pass(0)
    leave = pltpu.make_async_copy(enc_ref, enc_hbm, load_sem.at[len(loads)])
    leave.start()
    local_pass(0)
    state_pass(1)
    table_pass(1)
    local_pass(1)
    d_kb, tap_sums = d_kb[0], tap_sums[0]
    d_kb = split(d_kb * kb_slope)
    b_sums = dot(kmer_hits[:, 0:16], d_kb[0][0:256], 0, 0)
    b_sums = b_sums + dot(kmer_hits[:, 0:16], d_kb[1][0:256], 0, 0)
    end_pick = end_pick.astype(BF16)
    b_sums = b_sums + dot(end_pick, d_kb[0][256:]) + dot(end_pick, d_kb[1][256:])
    tap_sums = tap_sums + jnp.concatenate([b_sums, jnp.zeros_like(b_sums)], axis=1)
    conv_rows = []
    for k in range(CONV):
        conv_rows.append(
            jnp.sum(tap_sums[4 * k : 4 * k + 4] * table_s, axis=0, keepdims=True)
        )
    sums = jnp.sum(jnp.concatenate(rate_grads + bias_grads, axis=0), axis=1, keepdims=True)
    lane8 = iota((8, 128), 1)
    row8 = iota((8, 128), 0)
    last = jnp.zeros((8, 128), F32)
    head_total = 8 * heads
    for h in range(heads):
        at = slot * heads + h
        last = jnp.where((row8 == 0) & (lane8 == at), sums[h : h + 1], last)
        last = jnp.where(
            (row8 == 0) & (lane8 == head_total + at), sums[heads + h : heads + h + 1], last
        )
    conv = jnp.concatenate(conv_rows, axis=0)
    value = jnp.concatenate([conv[:, :128], conv[:, 128:], last[0:1]], axis=0)
    if links is not None:
        value = links.reduce(value)
    pay_ref[...] = value
    leave.wait()
    if links is not None:
        links.drain()


def layer(args, place, loss_scale, everyone=None, interpret=False):
    (tokens, rc_map, embedding, norm_gain, w_values, w_gates, w_states, w_steps, conv_values,
     conv_states, step_bias, log_rate, skip_gain, head_gain, cotangent) = args
    own, inner = cotangent.shape
    blocks = SIZES["x"] * SIZES["z"]
    chunks = 2 * blocks
    hbm = pl.BlockSpec(memory_space=pl.ANY)
    inputs = [
        tokens, rc_map, step_bias, log_rate, skip_gain, embedding, norm_gain.reshape(1, -1),
        conv_values, conv_states, head_gain.reshape(1, -1), w_states, w_steps.T, w_values, w_gates,
        cotangent,
    ]
    count = len(inputs)
    stores = [
        (pltpu.SMEM if 1 <= n <= 4 else pltpu.VMEM)(a.shape, a.dtype) for n, a in enumerate(inputs)
    ]
    scratch = [
        pltpu.VMEM((chunks, 128), F32),
        pltpu.VMEM((chunks, 128), F32),
        pltpu.VMEM((16 * chunks, 128), F32),
        pltpu.VMEM((8, own, own), F32),
        pltpu.SemaphoreType.DMA((count + 1,)),
        pltpu.VMEM((2, own, inner), BF16),
        pltpu.VMEM((2, own, inner), BF16),
        pltpu.VMEM((2, own, inner), F32),
        pltpu.VMEM((2, own, inner), F32),
        pltpu.VMEM((2, own, inner), F32),
        pltpu.VMEM((own, inner), F32),
        pltpu.VMEM((2, own, own), F32),
        pltpu.VMEM((2, own, inner), BF16),
        pltpu.VMEM((2, own, inner), BF16),
        pltpu.VMEM((2, own, inner), F32),
        pltpu.VMEM((own, inner), BF16),
        pltpu.VMEM((2, 256 + 16, inner), F32),
    ]
    slots = SIZES["c"] + SIZES["x"] * SIZES["y"] + SIZES["z"]
    remote = [
        pltpu.VMEM((SIZES["z"], SIZES["x"], 2, 128), jnp.int32),
        pltpu.VMEM((2, 2, 128), jnp.int32),
        pltpu.VMEM((slots, 9, 128), F32),
        pltpu.VMEM((3, 9, 128), F32),
        pltpu.SemaphoreType.DMA((12,)),
        pltpu.SemaphoreType.DMA((14,)),
        pltpu.SemaphoreType.DMA((slots,)),
        pltpu.SemaphoreType.DMA((slots,)),
    ]
    shapes = (
        jax.ShapeDtypeStruct((own, inner), BF16),
        jax.ShapeDtypeStruct((9, 128), F32),
    )
    alone = everyone is not None

    def body(*refs):
        refs = list(refs)
        sources, refs = refs[:count], refs[count:]
        if alone:
            links, held, refs = None, refs[0], refs[1:]
            out, refs = refs[:2], refs[2:]
        else:
            out, refs = refs[:2], refs[2:]
            links, held, refs = Links(refs[:8]), refs[0], refs[8:]
        layer_kernel(
            place, links, sources, *out, held, refs[:count], *refs[count:], loss_scale=loss_scale
        )

    if alone:
        params = pltpu.CompilerParams(vmem_limit_bytes=60 * 1024 * 1024)
    else:
        params = pltpu.CompilerParams(
            vmem_limit_bytes=60 * 1024 * 1024, collective_id=0, has_side_effects=True
        )
    return pl.pallas_call(
        body,
        out_shape=shapes,
        in_specs=[hbm] * count + [VM] * alone,
        out_specs=(hbm, VM),
        scratch_shapes=([] if alone else remote) + stores + scratch,
        compiler_params=params,
        interpret=interpret,
        name="layer",
    )(*inputs, *([everyone] if alone else []))


def emit_kernel(enc_ref, pay_ref, out_ref, rate_ref, bias_ref, conv_ref):
    heads = rate_ref.shape[1]
    out_ref[...] = enc_ref[...]
    rate_ref[...] = pay_ref[8:9, 0:heads]
    bias_ref[...] = pay_ref[8:9, heads : 2 * heads]
    conv_ref[...] = jnp.concatenate([pay_ref[0:4, :], pay_ref[4:8, :]], axis=1)


def emit(encoded, pay, heads):
    return pl.pallas_call(
        emit_kernel,
        out_shape=(
            jax.ShapeDtypeStruct(encoded.shape, BF16),
            jax.ShapeDtypeStruct((1, heads), F32),
            jax.ShapeDtypeStruct((1, heads), F32),
            jax.ShapeDtypeStruct((4, 256), F32),
        ),
        in_specs=[VM] * 2,
        out_specs=(VM,) * 4,
        name="emit",
    )(encoded, pay)


def solution(mesh):
    count = mesh.shape["ctx"]

    def on_device(*args):
        own = args[-1].shape[0]
        loss_scale = 1.0 / math.sqrt(own * count * HEAD)

        def place():
            return lax.axis_index("ctx"), lax.axis_index("tp")

        heads = args[11].shape[0] * mesh.shape["tp"]
        encoded, pay = layer((args[0].reshape(2, 128),) + args[1:], place, loss_scale)
        encoded, rate, bias, conv = emit(encoded, pay, heads)
        return encoded, rate.reshape(-1), bias.reshape(-1), conv

    tp = P("tp")
    cols = P(None, "tp")
    in_specs = (
        P("ctx"), P(), P(), P(), cols, cols, P(), cols, cols, P(), tp, tp, tp, tp, P("ctx", "tp"),
    )
    return jax.shard_map(
        on_device, mesh=mesh, in_specs=in_specs,
        out_specs=(P("ctx", "tp"), P(), P(), P()), check_vma=False,
    )
```

```python
import math

import jax
import jax.numpy as jnp
from jax import lax
from jax.experimental import pallas as pl
from jax.experimental.pallas import tpu as pltpu
from jax.sharding import PartitionSpec as P

F32 = jnp.float32
BF16 = jnp.bfloat16
HEAD = 128
CONV = 4
EPS = 1e-05
MESH = pl.DeviceIdType.MESH
VM = pl.BlockSpec(memory_space=pltpu.VMEM)


def split(v):
    hi = v.astype(BF16)
    return hi, (v - hi.astype(F32)).astype(BF16)


def dot(a, b, ca=1, cb=0):
    return lax.dot_general(a, b, (((ca,), (cb,)), ((), ())), preferred_element_type=F32)


def lhs3(v):
    hi, lo = v
    return jnp.concatenate([hi, lo, hi], axis=1)


def rhs3(v, axis=0):
    hi, lo = v
    return jnp.concatenate([hi, hi, lo], axis=axis)


def silu(v):
    return v / (1.0 + jnp.exp(-v))


def silu_slope(v):
    s = 1.0 / (1.0 + jnp.exp(-v))
    return s + v * s * (1.0 - s)


def fold(v):
    return v[:, :128] + v[:, 128:]


def iota(shape, dim):
    return lax.broadcasted_iota(jnp.int32, shape, dim)


def back_one(v, fill):
    rolled = pltpu.roll(v, 1, 1)
    wrapped = pltpu.roll(rolled, 1, 0)
    moved = jnp.where(iota(v.shape, 1) == 0, wrapped, rolled)
    first = (iota(v.shape, 0) == 0) & (iota(v.shape, 1) == 0)
    return jnp.where(first, fill, moved)


def ahead_one(v, fill):
    rows, lanes = v.shape
    rolled = pltpu.roll(v, lanes - 1, 1)
    wrapped = pltpu.roll(rolled, rows - 1, 0)
    moved = jnp.where(iota(v.shape, 1) == lanes - 1, wrapped, rolled)
    last = (iota(v.shape, 0) == rows - 1) & (iota(v.shape, 1) == lanes - 1)
    return jnp.where(last, fill, moved)


def softplus(v):
    return jnp.maximum(v, 0.0) + jnp.log1p(jnp.exp(-jnp.abs(v)))


SIZES = {"x": 4, "z": 8, "y": 4, "c": 2}


def offsets(axes):
    steps = [()]
    for axis in axes:
        steps = [step + (d,) for step in steps for d in range(SIZES[axis])]

    def hops(step):
        return sum(min(d, SIZES[axis] - d) for axis, d in zip(axes, step) if axis != "c")

    return sorted(steps[1:], key=lambda step: -hops(step))


class Links:
    def __init__(self, refs):
        (self.held, self.near, self.slots, self.sent, self.tok_send, self.tok_recv,
         self.sum_send, self.sum_recv) = refs
        ctx, tp = lax.axis_index("ctx"), lax.axis_index("tp")
        self.ctx = ctx
        self.here = {
            "x": ctx // SIZES["z"], "z": lax.rem(ctx, SIZES["z"]),
            "y": tp // SIZES["c"], "c": lax.rem(tp, SIZES["c"]),
        }
        self.drains = []

    def moved(self, axes, step):
        there = dict(self.here)
        for axis, d in zip(axes, step):
            if d:
                there[axis] = lax.rem(there[axis] + d, SIZES[axis])
        return there

    def device(self, there):
        return {
            "ctx": there["x"] * SIZES["z"] + there["z"], "tp": there["y"] * SIZES["c"] + there["c"]
        }

    def beside(self, d):
        count = SIZES["x"] * SIZES["z"]
        return {"ctx": lax.rem(self.ctx + d % count, count)}

    def greet(self):
        barrier = pltpu.get_barrier_semaphore()
        devices = [self.device(self.moved("z", step)) for step in offsets("z")]
        devices += [self.device(self.moved("x", step)) for step in offsets("x")]
        devices += [self.beside(1), self.beside(-1)]
        devices += [self.device(self.moved("xy", step)) for step in offsets("xy") if step[1]]
        devices += [self.device(self.moved("c", step)) for step in offsets("c")]
        for device in devices:
            pl.semaphore_signal(barrier, inc=1, device_id=device, device_id_type=MESH)
        self.greeted = len(devices)

    def met(self):
        pl.semaphore_wait(pltpu.get_barrier_semaphore(), self.greeted)

    def token_copy(self, source, target, number, arrives, device):
        return pltpu.make_async_remote_copy(
            src_ref=source, dst_ref=target, send_sem=self.tok_send.at[number],
            recv_sem=self.tok_recv.at[arrives], device_id=device, device_id_type=MESH,
        )

    def send(self, copy):
        copy.start()
        self.drains.append(copy)

    def send_tokens(self, tok_ref):
        x, z = self.here["x"], self.here["z"]
        own = self.held.at[z, x]
        for k, step in enumerate(offsets("x")):
            self.send(self.token_copy(tok_ref, own, k, x, self.device(self.moved("x", step))))
        for k, d in ((3, 1), (4, -1)):
            near = self.near.at[k - 3]
            self.send(self.token_copy(tok_ref, near, k, 9 + k, self.beside(d)))
        self.held[z, x] = tok_ref[...]

    def pass_tokens(self, tok_ref):
        x, z = self.here["x"], self.here["z"]
        for step in reversed(offsets("x")):
            there = self.moved("x", step)
            self.token_copy(
                tok_ref, self.held.at[z, there["x"]], 0, there["x"], self.device(there)
            ).wait_recv()
        row = self.held.at[z]
        for k, step in enumerate(offsets("z")):
            there = self.moved("z", step)
            self.send(self.token_copy(row, row, 5 + k, 4 + z, self.device(there)))

    def take_beside(self, tok_ref):
        for k, d in ((3, 1), (4, -1)):
            self.token_copy(tok_ref, self.near.at[k - 3], k, 9 + k, self.beside(d)).wait_recv()

    def take_tokens(self):
        for step in reversed(offsets("z")):
            there = self.moved("z", step)
            row = self.held.at[there["z"]]
            self.token_copy(row, row, 5, 4 + there["z"], self.device(there)).wait_recv()

    def reduce(self, value):
        base = 0
        for number, axes in enumerate(("c", "xy", "z")):
            self.sent[number] = value
            steps = offsets(axes)
            sending = []

            def slot(there):
                place = 0
                for axis in axes:
                    place = place * SIZES[axis] + there[axis]
                return base + place

            def copy(k, there, place):
                return pltpu.make_async_remote_copy(
                    src_ref=self.sent.at[number],
                    dst_ref=self.slots.at[place],
                    send_sem=self.sum_send.at[base + k],
                    recv_sem=self.sum_recv.at[place],
                    device_id=self.device(there),
                    device_id_type=MESH,
                )

            for k, step in enumerate(steps):
                sending.append(copy(k, self.moved(axes, step), slot(self.here)))
                sending[-1].start()
            self.drain()
            self.drains = sending
            self.slots[slot(self.here)] = value
            for step in reversed(steps):
                there = self.moved(axes, step)
                copy(0, there, slot(there)).wait_recv()
            value = self.slots[base]
            for i in range(1, len(steps) + 1):
                value = value + self.slots[base + i]
            base += len(steps) + 1
        return value

    def drain(self):
        for copy in self.drains:
            copy.wait_send()


def layer_kernel(
    place, links, sources, enc_ref, pay_ref, held, stores, kmer_ref, last_ref, rows_ref, decay_ref, load_sem,
    xh_ref, xl_ref, y_ref, gate_ref, grow_ref, dg_ref, score_ref, gh_ref, gl_ref, car_ref, kxw_ref,
    *, loss_scale,
):
    if links is not None:
        links.greet()
    loads = [
        pltpu.make_async_copy(source, store, load_sem.at[n])
        for n, (source, store) in enumerate(zip(sources, stores))
    ]
    for load in loads:
        load.start()
    (tok_ref, rc, bias, log_rate, skip, emb_ref, ng_ref, cv_ref, cs_ref, hg_ref, ws_ref, wst_ref,
     wv_ref, wg_ref, cot_ref) = stores
    me, slot = place()
    blocks = SIZES["x"] * SIZES["z"]
    chunks = 2 * blocks
    inner = cv_ref.shape[1]
    heads = inner // HEAD
    own = cot_ref.shape[0]
    width = inner + 2 * HEAD
    for load in loads[:10]:
        load.wait()
    e = emb_ref[...].astype(F32)
    scale = lax.rsqrt(jnp.mean(e * e, axis=1, keepdims=True) + EPS)
    normed = (e * scale * ng_ref[...]).astype(BF16)
    normed = jnp.concatenate([normed, jnp.zeros((12, e.shape[1]), BF16)], axis=0)
    loads[10].wait()
    table_s = dot(normed, ws_ref[...])[0:4]
    loads[11].wait()
    table_d = dot(normed, wst_ref[...], 1, 1)[0:4]
    loads[12].wait()
    table_v = dot(normed, wv_ref[...])[0:4]
    if links is not None:
        links.met()
        links.send_tokens(tok_ref)
    loads[13].wait()
    table_z = dot(normed, wg_ref[...])[0:4]
    lane_h = iota((1, heads), 1)
    bias_row = jnp.zeros((1, heads), F32)
    rate_row = jnp.zeros((1, heads), F32)
    for h in range(heads):
        bias_row = jnp.where(lane_h == h, bias[h], bias_row)
        rate_row = jnp.where(lane_h == h, log_rate[h], rate_row)
    rate_row = jnp.exp(rate_row)
    pre_step = table_d + bias_row
    step_t = softplus(pre_step)
    sig_t = 1.0 / (1.0 + jnp.exp(-pre_step))
    ratio_t = jnp.where(step_t > 0.0, sig_t / step_t, 1.0)
    gate_t = silu(table_z)
    table_vs = jnp.concatenate([table_v, table_s], axis=1)
    taps = jnp.concatenate([cv_ref[...], cs_ref[...]], axis=1)
    none2 = jnp.zeros((4, 2 * heads), F32)
    rest = jnp.zeros((4, 128 - 3 * heads), F32)
    tail = jnp.concatenate(
        [
            gate_t,
            step_t, step_t, -rate_row * step_t, rest,
            none2, sig_t, rest,
            none2, ratio_t, rest,
        ],
        axis=1,
    )
    parts = []
    for k in range(CONV):
        last = tail if k == CONV - 1 else jnp.zeros_like(tail)
        parts.append(jnp.concatenate([table_vs * taps[k : k + 1], last], axis=1))
    per_tap = jnp.concatenate(parts, axis=0)
    p_hi = per_tap.astype(BF16)
    p_rest = per_tap - p_hi.astype(F32)
    p_mid = p_rest.astype(BF16)
    p_low = (p_rest - p_mid.astype(F32)).astype(BF16)
    per_tap3 = jnp.concatenate([p_hi, p_mid, p_low], axis=0)
    place_cols = width + inner

    column = iota((256, 48), 1) % 16
    index, tap = iota((256, 48), 0), column // 4
    digit = lax.shift_right_logical(index & 63, jnp.maximum(2 * (2 - tap), 0)) & 3
    digit = jnp.where(tap == 3, lax.shift_right_logical(index, 6), digit)
    kmer_hits = (digit == column % 4).astype(F32).astype(BF16)
    kmer_sum = dot(kmer_hits, per_tap3[:, : inner + HEAD])
    kmer_tail = dot(kmer_hits, per_tap3[:, place_cols:])
    kx = silu(kmer_sum[:, :inner])
    kb = silu(kmer_sum[:, inner:])
    kb_slope = silu_slope(kmer_sum[:, inner:])

    tri_in = (iota((own, own), 0) <= iota((own, own), 1)).astype(BF16)
    tri_out = (iota((own, own), 0) >= iota((own, own), 1)).astype(BF16)
    pad4 = jnp.zeros((12, own), BF16)

    def complement(v):
        out = jnp.full(v.shape, -1.0, F32)
        for a in range(4):
            out = jnp.where(v == a, rc[a].astype(F32), out)
        return out

    pair = tok_ref[...].astype(F32)
    mine = jnp.concatenate([pair[0:1], pair[1:2]], axis=1)
    mine_rc = complement(mine)
    letters = iota((4, own), 0).astype(F32)
    own_f = (jnp.broadcast_to(mine, (4, own)) == letters).astype(F32)
    own_r = (jnp.broadcast_to(mine_rc, (4, own)) == letters).astype(F32)
    n_f = dot(jnp.concatenate([own_f.astype(BF16), pad4], axis=0), tri_in)
    n_r = dot(jnp.concatenate([own_r.astype(BF16), pad4], axis=0), tri_out)

    def blend(weights, table, h):
        return sum(weights[a : a + 1] * table[a : a + 1, h : h + 1] for a in range(4))

    cum_rows, sig_rows, step_rows, ratio_rows = [], [], [], []
    for counted, hit in ((n_f, own_f), (n_r, own_r)):
        for h in range(heads):
            cum_rows.append(-(rate_row[:, h : h + 1] * blend(counted, step_t, h)))
            sig_rows.append(blend(counted, sig_t, h))
            step_rows.append(blend(hit, step_t, h))
            ratio_rows.append(blend(hit, ratio_t, h))
    cum8 = jnp.concatenate(cum_rows, axis=0)
    both = split(jnp.concatenate([cum8] + sig_rows, axis=0))
    side = jnp.concatenate([both[0], both[1]], axis=0)
    side = jnp.concatenate([side, side], axis=1)
    columns = jnp.transpose(
        jnp.concatenate([cum8, jnp.zeros((128 - 2 * heads, own), F32)], axis=0)
    )
    for n in range(2 * heads):
        if n < heads:
            causal = iota((own, own), 0) >= iota((own, own), 1)
        else:
            causal = iota((own, own), 0) <= iota((own, own), 1)
        cum_c = jnp.broadcast_to(columns[:, n : n + 1], (own, 128))
        for half in range(own // 128):
            at = slice(half * 128, half * 128 + 128)
            decay_ref[n, :, at] = (
                jnp.where(causal[:, at], jnp.exp(cum_c - cum_rows[n][:, at]), 0.0)
                * step_rows[n][:, at]
            )
        part = slice((n % heads) * HEAD, (n % heads + 1) * HEAD)
        grow_ref[n // heads, :, part] = jnp.exp(cum_c)
    loads[14].wait()
    gain = hg_ref[...]
    dg_ref[...] = cot_ref[...].astype(F32) * (gain * loss_scale)

    if links is not None:
        links.pass_tokens(tok_ref)
        links.take_beside(tok_ref)
        earlier, later = links.near[0], links.near[1]
    else:
        earlier, later = (
            held[lax.rem(there, SIZES["z"]), there // SIZES["z"]]
            for there in (lax.rem(me + blocks - 1, blocks), lax.rem(me + 1, blocks))
        )
    earlier, later = earlier.astype(F32)[1:2], later.astype(F32)[0:1]
    earlier = jnp.where(me > 0, earlier, -1.0)
    later = jnp.where(me < blocks - 1, later, -1.0)
    line = jnp.concatenate([earlier, mine, later], axis=1)
    line = jnp.broadcast_to(line, (8, line.shape[1]))
    line_rc = complement(line)
    letters8 = iota((8, own), 0).astype(F32)
    f_hits, r_hits = [], []
    for k in range(CONV):
        d = CONV - 1 - k
        f_line = pltpu.roll(line, d, 1) if d else line
        r_line = pltpu.roll(line_rc, line.shape[1] - d, 1) if d else line_rc
        f_hits.append((f_line[:, 128 : 128 + own] == letters8)[0:4].astype(F32))
        r_hits.append((r_line[:, 128 : 128 + own] == letters8)[0:4].astype(F32))
    hits_t = [jnp.concatenate(f_hits, axis=0), jnp.concatenate(r_hits, axis=0)]
    slopes, c_parts, ct_parts, b_parts = [], [], [], []
    for strand in range(2):
        hits = jnp.concatenate([hits_t[strand]] * 3, axis=0).astype(BF16)
        summed = dot(hits, per_tap3[:, :place_cols], 0, 0)
        gate_ref[strand] = summed[:, width:]
        states = silu(summed[:, inner:width])
        slopes.append(silu_slope(summed[:, inner:width]))
        b_s = split(states[:, :HEAD])
        c_s = split(states[:, HEAD:])
        b_parts.append(b_s)
        c_parts.append(c_s)
        ct_parts.append(split(jnp.transpose(states[:, HEAD:])))
        scores = dot(lhs3(c_s), rhs3(b_s, 1), 1, 1)
        score_ref[strand] = scores
        for h in range(heads):
            part = slice(h * HEAD, (h + 1) * HEAD)
            x_h = silu(summed[:, part])
            x_s = split(x_h)
            xh_ref[strand, :, part] = x_s[0]
            xl_ref[strand, :, part] = x_s[1]
            mixing = split(scores * decay_ref[strand * heads + h])
            y_ref[strand, :, part] = dot(lhs3(mixing), rhs3(x_s)) + skip[h] * x_h

    if links is not None:
        links.take_tokens()
    for r in range(blocks):
        kmer_ref[2 * r : 2 * r + 2, :] = held[r % SIZES["z"], r // SIZES["z"]].astype(F32)
    tok = kmer_ref[...]
    comp = complement(tok)
    f_shift, r_shift = [tok], [comp]
    for _ in range(CONV - 1):
        f_shift.append(back_one(f_shift[-1], -1.0))
        r_shift.append(ahead_one(r_shift[-1], -1.0))

    row = iota(tok.shape, 0)
    position = row * 128 + iota(tok.shape, 1)
    before = row < 2 * me
    outside = before | (row >= 2 * me + 2)
    kmer_f = f_shift[1] + 4.0 * f_shift[2] + 16.0 * f_shift[3]
    kmer_r = r_shift[1] + 4.0 * r_shift[2] + 16.0 * r_shift[3]
    kmer = jnp.where(before, kmer_f, kmer_r)
    edge = (before & (position < CONV - 1)) | (position >= chunks * 128 - (CONV - 1))
    kmer_ref[...] = jnp.where(edge & outside, -1.0, kmer)
    mixed = jnp.where(outside, jnp.where(before, tok, comp), -1.0)
    last_ref[...] = mixed
    tri = (iota((128, 128), 0) <= iota((128, 128), 1)).astype(BF16)
    ones = jnp.ones((128, 128), BF16)
    strict = (iota((chunks, chunks), 1) < iota((chunks, chunks), 0)).astype(BF16)
    counts = []
    for a in range(4):
        hit = (mixed == a).astype(F32)
        hit16 = hit.astype(BF16)
        within = dot(hit16, tri)
        offset = dot(strict, dot(hit16, ones).astype(BF16))
        total_f = jnp.sum(jnp.where(before, hit, 0.0), keepdims=True)
        inclusive = within + offset - total_f
        counts.append(jnp.where(before, -inclusive, inclusive - hit))
    for h in range(heads):
        steps_sum = sum(counts[a] * step_t[a : a + 1, h : h + 1] for a in range(4))
        sig_sum = sum(counts[a] * sig_t[a : a + 1, h : h + 1] for a in range(4))
        exponent = -(rate_row[:, h : h + 1] * steps_sum)
        decay = jnp.where(outside, jnp.exp(exponent), 0.0)
        for q, value in enumerate((decay, decay * exponent, decay * sig_sum)):
            base = (q * heads + h) * chunks
            rows_ref[base : base + chunks, :] = value
    for q in range(3 * heads, 16):
        rows_ref[q * chunks : (q + 1) * chunks, :] = jnp.zeros((chunks, 128), F32)

    first_id = iota((64, 128), 0).astype(F32).astype(BF16)
    one16, zero16 = jnp.ones((64, 128), BF16), jnp.zeros((64, 128), BF16)
    nothing = jnp.zeros((32, 128), BF16)

    def load_rows(chunk):
        return rows_ref[pl.ds(chunk, 16, stride=chunks), :]

    acc_f = jnp.zeros((64, 128), F32)
    acc_r = jnp.zeros((64, 128), F32)
    for block in range(blocks):
        hits, weights = [], []
        for chunk in (2 * block, 2 * block + 1):
            w = jnp.concatenate(split(load_rows(chunk)), axis=0)
            final = jnp.broadcast_to(last_ref[chunk : chunk + 1, :], (32, 128)).astype(BF16)
            weights.append(
                jnp.concatenate([jnp.where(final == a, w, nothing) for a in range(4)], axis=0)
            )
            ids = jnp.broadcast_to(kmer_ref[chunk : chunk + 1, :], (64, 128)).astype(BF16)
            hits.append(jnp.where(ids == first_id, one16, zero16))
        found = dot(jnp.concatenate(hits, axis=1), jnp.concatenate(weights, axis=1), 1, 1)
        acc_f = acc_f + jnp.where(block < me, found, 0.0)
        acc_r = acc_r + jnp.where(block > me, found, 0.0)
    lane = iota((16, 128), 1)
    e_f = split(jnp.where(lane < CONV - 1, load_rows(0), 0.0))
    e_r = split(jnp.where(lane >= 128 - (CONV - 1), load_rows(chunks - 1), 0.0))
    pick_row = iota((16, 128), 0)
    pick = (lane == jnp.where(pick_row < 8, pick_row, pick_row + 112)).astype(BF16)

    def by_row(acc, ends):
        parts = [acc] + [pltpu.roll(acc, 128 - 32 * a, 1) for a in range(1, 4)]
        ends = jnp.concatenate([ends[0], ends[1], jnp.zeros((96, 128), BF16)], axis=0)
        joined = jnp.concatenate(parts + [dot(pick, ends, 1, 1)], axis=0)
        return joined + pltpu.roll(joined, 128 - 16, 1)

    joined = (by_row(acc_f, e_f), by_row(acc_r, e_r))

    end_hits = []
    for k in range(CONV):
        d = CONV - 1 - k
        ends = jnp.where(
            iota((1, 128), 1) < 64, f_shift[d][0:1, :], r_shift[d][chunks - 1 : chunks, :]
        )
        end_hits.append(
            (jnp.broadcast_to(ends, (4, 128)) == iota((4, 128), 0).astype(F32)).astype(F32)
        )
    end_hits = jnp.concatenate(end_hits, axis=0).astype(BF16)
    end_pick = dot(end_hits, pick, 1, 1)
    end3 = jnp.concatenate([end_pick] * 3, axis=0).astype(BF16)
    end_sum = dot(end3, per_tap3, 0, 0)
    kx = jnp.concatenate([kx, silu(end_sum[:, :inner])], axis=0)
    kb = jnp.concatenate([kb, silu(end_sum[:, inner : inner + HEAD])], axis=0)
    kb_slope = jnp.concatenate([kb_slope, silu_slope(end_sum[:, inner : inner + HEAD])], axis=0)
    k_tail = jnp.concatenate([kmer_tail, end_sum[:, place_cols:]], axis=0)
    table_rows = kx.shape[0]

    lanes = iota((1, 128), 1)
    lane_rate = jnp.zeros((1, 128), F32)
    for h in range(heads):
        lane_rate = jnp.where(lanes == 2 * heads + h, -rate_row[:, h : h + 1], lane_rate)
    lane_one = jnp.where((lanes >= heads) & (lanes < 2 * heads), 1.0, lane_rate)
    weights, ratios, kxw_parts = [], [], []
    for strand in range(2):
        source = joined[strand]
        w = k_tail[:, 0:128] * source
        e4, e8 = pltpu.roll(source, heads, 1), pltpu.roll(source, 2 * heads, 1)
        decay = jnp.where((lanes >= heads) & (lanes < 2 * heads), e4, e8)
        kept = (decay > 0.0) & (lanes >= heads) & (lanes < 3 * heads)
        ratio = jnp.where(
            kept, lane_one * source / jnp.where(kept, decay, 1.0) + k_tail[:, 256:384], 0.0
        )
        ratio = jnp.concatenate(
            [ratio, jnp.zeros((384 - table_rows, 128), F32)], axis=0
        )
        ratio = split(jnp.transpose(ratio)[0:16, :table_rows])
        ratios.append(jnp.concatenate([ratio[0], ratio[1]], axis=0))
        for h in range(heads):
            part = slice(h * HEAD, (h + 1) * HEAD)
            kxw_ref[strand, :, part] = kx[:, part] * jnp.broadcast_to(
                w[:, h : h + 1], (table_rows, HEAD)
            )
        kxw_parts.append(split(kxw_ref[strand]))
    kb_t = jnp.concatenate([kb, jnp.zeros((384 - table_rows, HEAD), F32)], axis=0)
    kb_t = split(jnp.transpose(kb_t)[:, :table_rows])

    d_kb = [jnp.zeros(kb.shape, F32)]
    rate_grads = [jnp.zeros((1, 128), F32)] * heads
    bias_grads = [jnp.zeros((1, 128), F32)] * heads
    tap_sums = [jnp.zeros((16, 2 * HEAD), F32)]
    starts, d_scores, d_starts = [], [None, None], [None, None]
    for strand in range(2):
        kxw = kxw_parts[strand]
        start = dot(kb_t[0], kxw[0]) + (dot(kb_t[0], kxw[1]) + dot(kb_t[1], kxw[0]))
        starts.append(split(start))
        car_ref[strand] = dot(lhs3(c_parts[strand]), rhs3(starts[strand]))

    def head_pass(strand, h):
        n = strand * heads + h
        part = slice(h * HEAD, (h + 1) * HEAD)
        grow = grow_ref[strand, :, part]
        from_start = grow * car_ref[strand, :, part]
        gate = gate_ref[strand, :, part]
        gated = (y_ref[strand, :, part] + from_start) * gate
        inv = lax.rsqrt(jnp.mean(gated * gated, axis=1, keepdims=True) + EPS)
        normal = gated * inv
        out = normal * gain[:, part]
        if strand == 0:
            y_ref[0, :, part] = out
        else:
            enc_ref[:, part] = (y_ref[0, :, part] + out).astype(BF16)
        d_normal = dg_ref[:, part]
        d_y = d_normal - normal * jnp.mean(normal * d_normal, axis=1, keepdims=True)
        d_y = (d_y * inv) * gate
        x_s = (xh_ref[strand, :, part], xl_ref[strand, :, part])
        mixed_grad = dot(lhs3(split(d_y)), rhs3(x_s, 1), 1, 1) * decay_ref[n]
        d_scores[strand] = mixed_grad if h == 0 else d_scores[strand] + mixed_grad
        weighted = mixed_grad * score_ref[strand]
        wsum = split(fold(weighted) + d_y * from_start)
        moved = dot(side, jnp.concatenate([wsum[0], wsum[1]], axis=0))
        col_sum = jnp.sum(weighted, axis=0, keepdims=True)
        grown = split(d_y * grow)
        gh_ref[strand, :, part] = grown[0]
        gl_ref[strand, :, part] = grown[1]
        rate = rate_row[:, h : h + 1]
        rows = 2 * heads
        rate_grads[h] = (
            rate_grads[h]
            + (moved[n : n + 1] + moved[2 * rows + n : 2 * rows + n + 1])
            - fold(col_sum * cum_rows[n])
        )
        bias_grads[h] = (
            bias_grads[h]
            + fold(col_sum * (rate * sig_rows[n] + ratio_rows[n]))
            - rate * (moved[rows + n : rows + n + 1] + moved[3 * rows + n : 3 * rows + n + 1])
        )

    def state_pass(strand):
        grown = (gh_ref[strand], gl_ref[strand])
        d_starts[strand] = split(dot(lhs3(ct_parts[strand]), rhs3(grown)))

    def table_pass(strand):
        kxw, d_start = kxw_parts[strand], d_starts[strand]
        d_kb[0] = d_kb[0] + dot(lhs3(kxw), rhs3(d_start, 1), 1, 1)
        met = split(dot(lhs3(split(kb)), rhs3(d_start)) * kxw_ref[strand])
        slope = dot(ratios[strand], met[0]) + dot(ratios[strand], met[1])
        slope = slope[0:16] + slope[16:32]
        for h in range(heads):
            part = slice(h * HEAD, (h + 1) * HEAD)
            rate_grads[h] = rate_grads[h] + slope[heads + h : heads + h + 1, part]
            bias_grads[h] = bias_grads[h] + slope[2 * heads + h : 2 * heads + h + 1, part]

    def local_pass(strand):
        d_scores_s = split(d_scores[strand])
        d_c = dot(lhs3(d_scores_s), rhs3(b_parts[strand])) + dot(lhs3((gh_ref[strand], gl_ref[strand])), rhs3(starts[strand], 1), 1, 1)
        d_b = dot(lhs3(split(jnp.transpose(d_scores[strand]))), rhs3(c_parts[strand]))
        d_sum = split(jnp.concatenate([d_b, d_c], axis=1) * slopes[strand])
        hits = hits_t[strand].astype(BF16)
        tap_sums[0] = tap_sums[0] + dot(
            jnp.concatenate([hits, hits], axis=1), jnp.concatenate([d_sum[0], d_sum[1]], axis=0)
        )

    for h in range(heads):
        head_pass(0, h)
    state_pass(0)
    for h in range(heads):
        head_pass(1, h)
        if h == 0:
            table_pass(0)
    local_pass(0)
    state_pass(1)
    table_pass(1)
    local_pass(1)
    d_kb, tap_sums = d_kb[0], tap_sums[0]
    d_kb = split(d_kb * kb_slope)
    b_sums = dot(kmer_hits[:, 0:16], d_kb[0][0:256], 0, 0)
    b_sums = b_sums + dot(kmer_hits[:, 0:16], d_kb[1][0:256], 0, 0)
    end_pick = end_pick.astype(BF16)
    b_sums = b_sums + dot(end_pick, d_kb[0][256:]) + dot(end_pick, d_kb[1][256:])
    tap_sums = tap_sums + jnp.concatenate([b_sums, jnp.zeros_like(b_sums)], axis=1)
    conv_rows = []
    for k in range(CONV):
        conv_rows.append(
            jnp.sum(tap_sums[4 * k : 4 * k + 4] * table_s, axis=0, keepdims=True)
        )
    sums = jnp.sum(jnp.concatenate(rate_grads + bias_grads, axis=0), axis=1, keepdims=True)
    lane8 = iota((8, 128), 1)
    row8 = iota((8, 128), 0)
    last = jnp.zeros((8, 128), F32)
    head_total = 8 * heads
    for h in range(heads):
        at = slot * heads + h
        last = jnp.where((row8 == 0) & (lane8 == at), sums[h : h + 1], last)
        last = jnp.where(
            (row8 == 0) & (lane8 == head_total + at), sums[heads + h : heads + h + 1], last
        )
    conv = jnp.concatenate(conv_rows, axis=0)
    value = jnp.concatenate([conv[:, :128], conv[:, 128:], last[0:1]], axis=0)
    if links is not None:
        value = links.reduce(value)
    pay_ref[...] = value
    if links is not None:
        links.drain()


def layer(args, place, loss_scale, everyone=None, interpret=False):
    (tokens, rc_map, embedding, norm_gain, w_values, w_gates, w_states, w_steps, conv_values,
     conv_states, step_bias, log_rate, skip_gain, head_gain, cotangent) = args
    own, inner = cotangent.shape
    blocks = SIZES["x"] * SIZES["z"]
    chunks = 2 * blocks
    hbm = pl.BlockSpec(memory_space=pl.ANY)
    inputs = [
        tokens, rc_map, step_bias, log_rate, skip_gain, embedding, norm_gain.reshape(1, -1),
        conv_values, conv_states, head_gain.reshape(1, -1), w_states, w_steps.T, w_values, w_gates,
        cotangent,
    ]
    count = len(inputs)
    stores = [
        (pltpu.SMEM if 1 <= n <= 4 else pltpu.VMEM)(a.shape, a.dtype) for n, a in enumerate(inputs)
    ]
    scratch = [
        pltpu.VMEM((chunks, 128), F32),
        pltpu.VMEM((chunks, 128), F32),
        pltpu.VMEM((16 * chunks, 128), F32),
        pltpu.VMEM((8, own, own), F32),
        pltpu.SemaphoreType.DMA((count,)),
        pltpu.VMEM((2, own, inner), BF16),
        pltpu.VMEM((2, own, inner), BF16),
        pltpu.VMEM((2, own, inner), F32),
        pltpu.VMEM((2, own, inner), F32),
        pltpu.VMEM((2, own, inner), F32),
        pltpu.VMEM((own, inner), F32),
        pltpu.VMEM((2, own, own), F32),
        pltpu.VMEM((2, own, inner), BF16),
        pltpu.VMEM((2, own, inner), BF16),
        pltpu.VMEM((2, own, inner), F32),
        pltpu.VMEM((2, 256 + 16, inner), F32),
    ]
    slots = SIZES["c"] + SIZES["x"] * SIZES["y"] + SIZES["z"]
    remote = [
        pltpu.VMEM((SIZES["z"], SIZES["x"], 2, 128), jnp.int32),
        pltpu.VMEM((2, 2, 128), jnp.int32),
        pltpu.VMEM((slots, 9, 128), F32),
        pltpu.VMEM((3, 9, 128), F32),
        pltpu.SemaphoreType.DMA((12,)),
        pltpu.SemaphoreType.DMA((14,)),
        pltpu.SemaphoreType.DMA((slots,)),
        pltpu.SemaphoreType.DMA((slots,)),
    ]
    shapes = (
        pltpu.VMEM((own, inner), BF16),
        pltpu.VMEM((9, 128), F32),
    )
    alone = everyone is not None

    def body(*refs):
        refs = list(refs)
        sources, refs = refs[:count], refs[count:]
        if alone:
            links, held, refs = None, refs[0], refs[1:]
            out, refs = refs[:2], refs[2:]
        else:
            out, refs = refs[:2], refs[2:]
            links, held, refs = Links(refs[:8]), refs[0], refs[8:]
        layer_kernel(
            place, links, sources, *out, held, refs[:count], *refs[count:], loss_scale=loss_scale
        )

    if alone:
        params = pltpu.CompilerParams(vmem_limit_bytes=60 * 1024 * 1024)
    else:
        params = pltpu.CompilerParams(
            vmem_limit_bytes=60 * 1024 * 1024, collective_id=0, has_side_effects=True
        )
    return pl.pallas_call(
        body,
        out_shape=shapes,
        in_specs=[hbm] * count + [VM] * alone,
        out_specs=(VM, VM),
        scratch_shapes=([] if alone else remote) + stores + scratch,
        compiler_params=params,
        interpret=interpret,
        name="layer",
    )(*inputs, *([everyone] if alone else []))


def emit_kernel(enc_ref, pay_ref, out_hbm, rate_ref, bias_ref, conv_ref, sem):
    leave = pltpu.make_async_copy(enc_ref, out_hbm, sem)
    leave.start()
    heads = rate_ref.shape[1]
    rate_ref[...] = pay_ref[8:9, 0:heads]
    bias_ref[...] = pay_ref[8:9, heads : 2 * heads]
    conv_ref[...] = jnp.concatenate([pay_ref[0:4, :], pay_ref[4:8, :]], axis=1)
    leave.wait()


def emit(encoded, pay, heads):
    return pl.pallas_call(
        emit_kernel,
        out_shape=(
            jax.ShapeDtypeStruct(encoded.shape, BF16),
            jax.ShapeDtypeStruct((1, heads), F32),
            jax.ShapeDtypeStruct((1, heads), F32),
            jax.ShapeDtypeStruct((4, 256), F32),
        ),
        in_specs=[VM] * 2,
        out_specs=(pl.BlockSpec(memory_space=pl.ANY), VM, VM, VM),
        scratch_shapes=[pltpu.SemaphoreType.DMA],
        name="emit",
    )(
        pltpu.with_memory_space_constraint(encoded, pltpu.VMEM),
        pltpu.with_memory_space_constraint(pay, pltpu.VMEM),
    )


def solution(mesh):
    count = mesh.shape["ctx"]

    def on_device(*args):
        own = args[-1].shape[0]
        loss_scale = 1.0 / math.sqrt(own * count * HEAD)

        def place():
            return lax.axis_index("ctx"), lax.axis_index("tp")

        heads = args[11].shape[0] * mesh.shape["tp"]
        encoded, pay = layer((args[0].reshape(2, 128),) + args[1:], place, loss_scale)
        encoded, rate, bias, conv = emit(encoded, pay, heads)
        return encoded, rate.reshape(-1), bias.reshape(-1), conv

    tp = P("tp")
    cols = P(None, "tp")
    in_specs = (
        P("ctx"), P(), P(), P(), cols, cols, P(), cols, cols, P(), tp, tp, tp, tp, P("ctx", "tp"),
    )
    return jax.shard_map(
        on_device, mesh=mesh, in_specs=in_specs,
        out_specs=(P("ctx", "tp"), P(), P(), P()), check_vma=False,
    )
```

```python
import math

import jax
import jax.numpy as jnp
from jax import lax
from jax.experimental import pallas as pl
from jax.experimental.pallas import tpu as pltpu
from jax.sharding import PartitionSpec as P

F32 = jnp.float32
BF16 = jnp.bfloat16
HEAD = 128
CONV = 4
EPS = 1e-05
MESH = pl.DeviceIdType.MESH
VM = pl.BlockSpec(memory_space=pltpu.VMEM)


def split(v):
    hi = v.astype(BF16)
    return hi, (v - hi.astype(F32)).astype(BF16)


def dot(a, b, ca=1, cb=0):
    return lax.dot_general(a, b, (((ca,), (cb,)), ((), ())), preferred_element_type=F32)


def lhs3(v):
    hi, lo = v
    return jnp.concatenate([hi, lo, hi], axis=1)


def rhs3(v, axis=0):
    hi, lo = v
    return jnp.concatenate([hi, hi, lo], axis=axis)


def silu(v):
    return v / (1.0 + jnp.exp(-v))


def silu_slope(v):
    s = 1.0 / (1.0 + jnp.exp(-v))
    return s + v * s * (1.0 - s)


def fold(v):
    return v[:, :128] + v[:, 128:] if v.shape[1] > 128 else v


def live(strand):
    if strand == 0:
        return ((slice(0, 128), slice(0, 128)), (slice(128, 256), slice(0, 256)))
    return ((slice(0, 128), slice(0, 256)), (slice(128, 256), slice(128, 256)))


def filled(halves, strand):
    zero = jnp.zeros((128, 128), halves[0].dtype)
    if strand == 0:
        return jnp.concatenate(
            [jnp.concatenate([halves[0], zero], axis=1), halves[1]], axis=0
        )
    return jnp.concatenate([halves[0], jnp.concatenate([zero, halves[1]], axis=1)], axis=0)


def iota(shape, dim):
    return lax.broadcasted_iota(jnp.int32, shape, dim)


def back_one(v, fill):
    rolled = pltpu.roll(v, 1, 1)
    wrapped = pltpu.roll(rolled, 1, 0)
    moved = jnp.where(iota(v.shape, 1) == 0, wrapped, rolled)
    first = (iota(v.shape, 0) == 0) & (iota(v.shape, 1) == 0)
    return jnp.where(first, fill, moved)


def ahead_one(v, fill):
    rows, lanes = v.shape
    rolled = pltpu.roll(v, lanes - 1, 1)
    wrapped = pltpu.roll(rolled, rows - 1, 0)
    moved = jnp.where(iota(v.shape, 1) == lanes - 1, wrapped, rolled)
    last = (iota(v.shape, 0) == rows - 1) & (iota(v.shape, 1) == lanes - 1)
    return jnp.where(last, fill, moved)


def softplus(v):
    return jnp.maximum(v, 0.0) + jnp.log1p(jnp.exp(-jnp.abs(v)))


SIZES = {"x": 4, "z": 8, "y": 4, "c": 2}


def offsets(axes):
    steps = [()]
    for axis in axes:
        steps = [step + (d,) for step in steps for d in range(SIZES[axis])]

    def hops(step):
        return sum(min(d, SIZES[axis] - d) for axis, d in zip(axes, step) if axis != "c")

    return sorted(steps[1:], key=lambda step: -hops(step))


class Links:
    def __init__(self, refs):
        (self.held, self.near, self.slots, self.sent, self.tok_send, self.tok_recv,
         self.sum_send, self.sum_recv) = refs
        ctx, tp = lax.axis_index("ctx"), lax.axis_index("tp")
        self.ctx = ctx
        self.here = {
            "x": ctx // SIZES["z"], "z": lax.rem(ctx, SIZES["z"]),
            "y": tp // SIZES["c"], "c": lax.rem(tp, SIZES["c"]),
        }
        self.drains = []

    def moved(self, axes, step):
        there = dict(self.here)
        for axis, d in zip(axes, step):
            if d:
                there[axis] = lax.rem(there[axis] + d, SIZES[axis])
        return there

    def device(self, there):
        return {
            "ctx": there["x"] * SIZES["z"] + there["z"], "tp": there["y"] * SIZES["c"] + there["c"]
        }

    def beside(self, d):
        count = SIZES["x"] * SIZES["z"]
        return {"ctx": lax.rem(self.ctx + d % count, count)}

    def greet(self):
        barrier = pltpu.get_barrier_semaphore()
        devices = [self.device(self.moved("z", step)) for step in offsets("z")]
        devices += [self.device(self.moved("x", step)) for step in offsets("x")]
        devices += [self.beside(1), self.beside(-1)]
        devices += [self.device(self.moved("xy", step)) for step in offsets("xy") if step[1]]
        devices += [self.device(self.moved("c", step)) for step in offsets("c")]
        for device in devices:
            pl.semaphore_signal(barrier, inc=1, device_id=device, device_id_type=MESH)
        self.greeted = len(devices)

    def met(self):
        pl.semaphore_wait(pltpu.get_barrier_semaphore(), self.greeted)

    def token_copy(self, source, target, number, arrives, device):
        return pltpu.make_async_remote_copy(
            src_ref=source, dst_ref=target, send_sem=self.tok_send.at[number],
            recv_sem=self.tok_recv.at[arrives], device_id=device, device_id_type=MESH,
        )

    def send(self, copy):
        copy.start()
        self.drains.append(copy)

    def send_tokens(self, tok_ref):
        x, z = self.here["x"], self.here["z"]
        own = self.held.at[z, x]
        for k, step in enumerate(offsets("x")):
            self.send(self.token_copy(tok_ref, own, k, x, self.device(self.moved("x", step))))
        for k, d in ((3, 1), (4, -1)):
            near = self.near.at[k - 3]
            self.send(self.token_copy(tok_ref, near, k, 9 + k, self.beside(d)))
        self.held[z, x] = tok_ref[...]

    def pass_tokens(self, tok_ref):
        x, z = self.here["x"], self.here["z"]
        for step in reversed(offsets("x")):
            there = self.moved("x", step)
            self.token_copy(
                tok_ref, self.held.at[z, there["x"]], 0, there["x"], self.device(there)
            ).wait_recv()
        row = self.held.at[z]
        for k, step in enumerate(offsets("z")):
            there = self.moved("z", step)
            self.send(self.token_copy(row, row, 5 + k, 4 + z, self.device(there)))

    def take_beside(self, tok_ref):
        for k, d in ((3, 1), (4, -1)):
            self.token_copy(tok_ref, self.near.at[k - 3], k, 9 + k, self.beside(d)).wait_recv()

    def take_tokens(self):
        for step in reversed(offsets("z")):
            there = self.moved("z", step)
            row = self.held.at[there["z"]]
            self.token_copy(row, row, 5, 4 + there["z"], self.device(there)).wait_recv()

    def reduce(self, value):
        base = 0
        for number, axes in enumerate(("c", "xy", "z")):
            self.sent[number] = value
            steps = offsets(axes)
            sending = []

            def slot(there):
                place = 0
                for axis in axes:
                    place = place * SIZES[axis] + there[axis]
                return base + place

            def copy(k, there, place):
                return pltpu.make_async_remote_copy(
                    src_ref=self.sent.at[number],
                    dst_ref=self.slots.at[place],
                    send_sem=self.sum_send.at[base + k],
                    recv_sem=self.sum_recv.at[place],
                    device_id=self.device(there),
                    device_id_type=MESH,
                )

            for k, step in enumerate(steps):
                sending.append(copy(k, self.moved(axes, step), slot(self.here)))
                sending[-1].start()
            self.drain()
            self.drains = sending
            self.slots[slot(self.here)] = value
            for step in reversed(steps):
                there = self.moved(axes, step)
                copy(0, there, slot(there)).wait_recv()
            value = self.slots[base]
            for i in range(1, len(steps) + 1):
                value = value + self.slots[base + i]
            base += len(steps) + 1
        return value

    def drain(self):
        for copy in self.drains:
            copy.wait_send()


def layer_kernel(
    place, links, sources, enc_ref, rate_ref, bias_ref, conv_ref, held, stores, kmer_ref, last_ref, rows_ref, decay_ref, load_sem,
    xh_ref, xl_ref, y_ref, gate_ref, grow_ref, dg_ref, score_ref, gh_ref, gl_ref, car_ref, kxw_ref,
    *, loss_scale,
):
    if links is not None:
        links.greet()
    loads = [
        pltpu.make_async_copy(source, store, load_sem.at[n])
        for n, (source, store) in enumerate(zip(sources, stores))
    ]
    for load in loads:
        load.start()
    (tok_ref, rc, bias, log_rate, skip, emb_ref, ng_ref, cv_ref, cs_ref, hg_ref, ws_ref, wst_ref,
     wv_ref, wg_ref, cot_ref) = stores
    me, slot = place()
    blocks = SIZES["x"] * SIZES["z"]
    chunks = 2 * blocks
    inner = cv_ref.shape[1]
    heads = inner // HEAD
    own = cot_ref.shape[0]
    width = inner + 2 * HEAD
    for load in loads[:10]:
        load.wait()
    e = emb_ref[...].astype(F32)
    scale = lax.rsqrt(jnp.mean(e * e, axis=1, keepdims=True) + EPS)
    normed = (e * scale * ng_ref[...]).astype(BF16)
    normed = jnp.concatenate([normed, jnp.zeros((12, e.shape[1]), BF16)], axis=0)
    loads[10].wait()
    table_s = dot(normed, ws_ref[...])[0:4]
    if links is not None:
        links.met()
        links.send_tokens(tok_ref)
    loads[11].wait()
    table_d = dot(normed, wst_ref[...], 1, 1)[0:4]
    loads[12].wait()
    table_v = dot(normed, wv_ref[...])[0:4]
    loads[13].wait()
    table_z = dot(normed, wg_ref[...])[0:4]
    lane_h = iota((1, heads), 1)
    bias_row = jnp.zeros((1, heads), F32)
    rate_row = jnp.zeros((1, heads), F32)
    for h in range(heads):
        bias_row = jnp.where(lane_h == h, bias[h], bias_row)
        rate_row = jnp.where(lane_h == h, log_rate[h], rate_row)
    rate_row = jnp.exp(rate_row)
    pre_step = table_d + bias_row
    step_t = softplus(pre_step)
    sig_t = 1.0 / (1.0 + jnp.exp(-pre_step))
    ratio_t = jnp.where(step_t > 0.0, sig_t / step_t, 1.0)
    gate_t = silu(table_z)
    table_vs = jnp.concatenate([table_v, table_s], axis=1)
    taps = jnp.concatenate([cv_ref[...], cs_ref[...]], axis=1)
    none2 = jnp.zeros((4, 2 * heads), F32)
    rest = jnp.zeros((4, 128 - 3 * heads), F32)
    tail = jnp.concatenate(
        [
            gate_t,
            step_t, step_t, -rate_row * step_t, rest,
            none2, sig_t, rest,
            none2, ratio_t, rest,
        ],
        axis=1,
    )
    parts = []
    for k in range(CONV):
        last = tail if k == CONV - 1 else jnp.zeros_like(tail)
        parts.append(jnp.concatenate([table_vs * taps[k : k + 1], last], axis=1))
    per_tap = jnp.concatenate(parts, axis=0)
    p_hi = per_tap.astype(BF16)
    p_rest = per_tap - p_hi.astype(F32)
    p_mid = p_rest.astype(BF16)
    p_low = (p_rest - p_mid.astype(F32)).astype(BF16)
    per_tap3 = jnp.concatenate([p_hi, p_mid, p_low], axis=0)
    place_cols = width + inner

    column = iota((256, 48), 1) % 16
    index, tap = iota((256, 48), 0), column // 4
    digit = lax.shift_right_logical(index & 63, jnp.maximum(2 * (2 - tap), 0)) & 3
    digit = jnp.where(tap == 3, lax.shift_right_logical(index, 6), digit)
    kmer_hits = (digit == column % 4).astype(F32).astype(BF16)
    kmer_sum = dot(kmer_hits, per_tap3[:, : inner + HEAD])
    kmer_tail = dot(kmer_hits, per_tap3[:, place_cols:])
    kx = silu(kmer_sum[:, :inner])
    kb = silu(kmer_sum[:, inner:])
    kb_slope = silu_slope(kmer_sum[:, inner:])

    tri_in = (iota((own, own), 0) <= iota((own, own), 1)).astype(BF16)
    tri_out = (iota((own, own), 0) >= iota((own, own), 1)).astype(BF16)
    pad4 = jnp.zeros((12, own), BF16)

    def complement(v):
        out = jnp.full(v.shape, -1.0, F32)
        for a in range(4):
            out = jnp.where(v == a, rc[a].astype(F32), out)
        return out

    pair = tok_ref[...].astype(F32)
    mine = jnp.concatenate([pair[0:1], pair[1:2]], axis=1)
    mine_rc = complement(mine)
    letters = iota((4, own), 0).astype(F32)
    own_f = (jnp.broadcast_to(mine, (4, own)) == letters).astype(F32)
    own_r = (jnp.broadcast_to(mine_rc, (4, own)) == letters).astype(F32)
    n_f = dot(jnp.concatenate([own_f.astype(BF16), pad4], axis=0), tri_in)
    n_r = dot(jnp.concatenate([own_r.astype(BF16), pad4], axis=0), tri_out)

    def blend(weights, table, h):
        return sum(weights[a : a + 1] * table[a : a + 1, h : h + 1] for a in range(4))

    cum_rows, sig_rows, step_rows, ratio_rows = [], [], [], []
    for counted, hit in ((n_f, own_f), (n_r, own_r)):
        for h in range(heads):
            cum_rows.append(-(rate_row[:, h : h + 1] * blend(counted, step_t, h)))
            sig_rows.append(blend(counted, sig_t, h))
            step_rows.append(blend(hit, step_t, h))
            ratio_rows.append(blend(hit, ratio_t, h))
    cum8 = jnp.concatenate(cum_rows, axis=0)
    both = split(jnp.concatenate([cum8] + sig_rows, axis=0))
    side = jnp.concatenate([both[0], both[1]], axis=0)
    side = jnp.concatenate([side, side], axis=1)
    columns = jnp.transpose(
        jnp.concatenate([cum8, jnp.zeros((128 - 2 * heads, own), F32)], axis=0)
    )
    square = (iota((128, 128), 0), iota((128, 128), 1))
    causal = (square[0] >= square[1], square[0] <= square[1])
    for n in range(2 * heads):
        cum_c = jnp.broadcast_to(columns[:, n : n + 1], (own, 128))
        for rows, _ in live(n // heads):
            for half in range(own // 128):
                cols = slice(half * 128, half * 128 + 128)
                if (cols.start > rows.start) if n < heads else (cols.start < rows.start):
                    continue
                grown = jnp.exp(cum_c[rows] - cum_rows[n][:, cols])
                if cols.start == rows.start:
                    grown = jnp.where(causal[n // heads], grown, 0.0)
                decay_ref[n, rows, cols] = grown * step_rows[n][:, cols]
        part = slice((n % heads) * HEAD, (n % heads + 1) * HEAD)
        grow_ref[n // heads, :, part] = jnp.exp(cum_c)
    loads[14].wait()
    gain = hg_ref[...]
    dg_ref[...] = cot_ref[...].astype(F32) * (gain * loss_scale)

    if links is not None:
        links.pass_tokens(tok_ref)
        links.take_beside(tok_ref)
        earlier, later = links.near[0], links.near[1]
    else:
        earlier, later = (
            held[lax.rem(there, SIZES["z"]), there // SIZES["z"]]
            for there in (lax.rem(me + blocks - 1, blocks), lax.rem(me + 1, blocks))
        )
    earlier, later = earlier.astype(F32)[1:2], later.astype(F32)[0:1]
    earlier = jnp.where(me > 0, earlier, -1.0)
    later = jnp.where(me < blocks - 1, later, -1.0)
    line = jnp.concatenate([earlier, mine, later], axis=1)
    line = jnp.broadcast_to(line, (8, line.shape[1]))
    line_rc = complement(line)
    letters8 = iota((8, own), 0).astype(F32)
    f_hits, r_hits = [], []
    for k in range(CONV):
        d = CONV - 1 - k
        f_line = pltpu.roll(line, d, 1) if d else line
        r_line = pltpu.roll(line_rc, line.shape[1] - d, 1) if d else line_rc
        f_hits.append((f_line[:, 128 : 128 + own] == letters8)[0:4].astype(F32))
        r_hits.append((r_line[:, 128 : 128 + own] == letters8)[0:4].astype(F32))
    hits_t = [jnp.concatenate(f_hits, axis=0), jnp.concatenate(r_hits, axis=0)]
    slopes, c_parts, ct_parts, b_parts = [], [], [], []
    for strand in range(2):
        hits = jnp.concatenate([hits_t[strand]] * 3, axis=0).astype(BF16)
        summed = dot(hits, per_tap3[:, :place_cols], 0, 0)
        gate_ref[strand] = summed[:, width:]
        states = silu(summed[:, inner:width])
        slopes.append(silu_slope(summed[:, inner:width]))
        b_s = split(states[:, :HEAD])
        c_s = split(states[:, HEAD:])
        b_parts.append(b_s)
        c_parts.append(c_s)
        ct_parts.append(split(jnp.transpose(states[:, HEAD:])))
        scores = dot(lhs3(c_s), rhs3(b_s, 1), 1, 1)
        score_ref[strand] = scores
        for h in range(heads):
            part = slice(h * HEAD, (h + 1) * HEAD)
            x_h = silu(summed[:, part])
            x_s = split(x_h)
            xh_ref[strand, :, part] = x_s[0]
            xl_ref[strand, :, part] = x_s[1]
            mixing = [
                split(scores[rows, cols] * decay_ref[strand * heads + h, rows, cols])
                for rows, cols in live(strand)
            ]
            mixing = [filled([half[k] for half in mixing], strand) for k in range(2)]
            y_ref[strand, :, part] = dot(lhs3(mixing), rhs3(x_s)) + skip[h] * x_h

    if links is not None:
        links.take_tokens()
    for r in range(blocks):
        kmer_ref[2 * r : 2 * r + 2, :] = held[r % SIZES["z"], r // SIZES["z"]].astype(F32)
    tok = kmer_ref[...]
    comp = complement(tok)
    f_shift, r_shift = [tok], [comp]
    for _ in range(CONV - 1):
        f_shift.append(back_one(f_shift[-1], -1.0))
        r_shift.append(ahead_one(r_shift[-1], -1.0))

    row = iota(tok.shape, 0)
    position = row * 128 + iota(tok.shape, 1)
    before = row < 2 * me
    outside = before | (row >= 2 * me + 2)
    kmer_f = f_shift[1] + 4.0 * f_shift[2] + 16.0 * f_shift[3]
    kmer_r = r_shift[1] + 4.0 * r_shift[2] + 16.0 * r_shift[3]
    kmer = jnp.where(before, kmer_f, kmer_r)
    edge = (before & (position < CONV - 1)) | (position >= chunks * 128 - (CONV - 1))
    kmer_ref[...] = jnp.where(edge & outside, -1.0, kmer)
    mixed = jnp.where(outside, jnp.where(before, tok, comp), -1.0)
    last_ref[...] = mixed
    tri = (iota((128, 128), 0) <= iota((128, 128), 1)).astype(BF16)
    ones = jnp.ones((128, 128), BF16)
    strict = (iota((chunks, chunks), 1) < iota((chunks, chunks), 0)).astype(BF16)
    counts = []
    for a in range(4):
        hit = (mixed == a).astype(F32)
        hit16 = hit.astype(BF16)
        within = dot(hit16, tri)
        offset = dot(strict, dot(hit16, ones).astype(BF16))
        total_f = jnp.sum(jnp.where(before, hit, 0.0), keepdims=True)
        inclusive = within + offset - total_f
        counts.append(jnp.where(before, -inclusive, inclusive - hit))
    for h in range(heads):
        steps_sum = sum(counts[a] * step_t[a : a + 1, h : h + 1] for a in range(4))
        sig_sum = sum(counts[a] * sig_t[a : a + 1, h : h + 1] for a in range(4))
        exponent = -(rate_row[:, h : h + 1] * steps_sum)
        decay = jnp.where(outside, jnp.exp(exponent), 0.0)
        for q, value in enumerate((decay, decay * exponent, decay * sig_sum)):
            base = (q * heads + h) * chunks
            rows_ref[base : base + chunks, :] = value
    for q in range(3 * heads, 16):
        rows_ref[q * chunks : (q + 1) * chunks, :] = jnp.zeros((chunks, 128), F32)

    first_id = iota((64, 128), 0).astype(F32).astype(BF16)
    one16, zero16 = jnp.ones((64, 128), BF16), jnp.zeros((64, 128), BF16)
    nothing = jnp.zeros((32, 128), BF16)

    def load_rows(chunk):
        return rows_ref[pl.ds(chunk, 16, stride=chunks), :]

    acc_f = jnp.zeros((64, 128), F32)
    acc_r = jnp.zeros((64, 128), F32)
    for block in range(blocks):
        hits, weights = [], []
        for chunk in (2 * block, 2 * block + 1):
            w = jnp.concatenate(split(load_rows(chunk)), axis=0)
            final = jnp.broadcast_to(last_ref[chunk : chunk + 1, :], (32, 128)).astype(BF16)
            weights.append(
                jnp.concatenate([jnp.where(final == a, w, nothing) for a in range(4)], axis=0)
            )
            ids = jnp.broadcast_to(kmer_ref[chunk : chunk + 1, :], (64, 128)).astype(BF16)
            hits.append(jnp.where(ids == first_id, one16, zero16))
        found = dot(jnp.concatenate(hits, axis=1), jnp.concatenate(weights, axis=1), 1, 1)
        acc_f = acc_f + jnp.where(block < me, found, 0.0)
        acc_r = acc_r + jnp.where(block > me, found, 0.0)
    lane = iota((16, 128), 1)
    e_f = split(jnp.where(lane < CONV - 1, load_rows(0), 0.0))
    e_r = split(jnp.where(lane >= 128 - (CONV - 1), load_rows(chunks - 1), 0.0))
    pick_row = iota((16, 128), 0)
    pick = (lane == jnp.where(pick_row < 8, pick_row, pick_row + 112)).astype(BF16)

    def by_row(acc, ends):
        parts = [acc] + [pltpu.roll(acc, 128 - 32 * a, 1) for a in range(1, 4)]
        ends = jnp.concatenate([ends[0], ends[1], jnp.zeros((96, 128), BF16)], axis=0)
        joined = jnp.concatenate(parts + [dot(pick, ends, 1, 1)], axis=0)
        return joined + pltpu.roll(joined, 128 - 16, 1)

    joined = (by_row(acc_f, e_f), by_row(acc_r, e_r))

    end_hits = []
    for k in range(CONV):
        d = CONV - 1 - k
        ends = jnp.where(
            iota((1, 128), 1) < 64, f_shift[d][0:1, :], r_shift[d][chunks - 1 : chunks, :]
        )
        end_hits.append(
            (jnp.broadcast_to(ends, (4, 128)) == iota((4, 128), 0).astype(F32)).astype(F32)
        )
    end_hits = jnp.concatenate(end_hits, axis=0).astype(BF16)
    end_pick = dot(end_hits, pick, 1, 1)
    end3 = jnp.concatenate([end_pick] * 3, axis=0).astype(BF16)
    end_sum = dot(end3, per_tap3, 0, 0)
    kx = jnp.concatenate([kx, silu(end_sum[:, :inner])], axis=0)
    kb = jnp.concatenate([kb, silu(end_sum[:, inner : inner + HEAD])], axis=0)
    kb_slope = jnp.concatenate([kb_slope, silu_slope(end_sum[:, inner : inner + HEAD])], axis=0)
    k_tail = jnp.concatenate([kmer_tail, end_sum[:, place_cols:]], axis=0)
    table_rows = kx.shape[0]

    lanes = iota((1, 128), 1)
    lane_rate = jnp.zeros((1, 128), F32)
    for h in range(heads):
        lane_rate = jnp.where(lanes == 2 * heads + h, -rate_row[:, h : h + 1], lane_rate)
    lane_one = jnp.where((lanes >= heads) & (lanes < 2 * heads), 1.0, lane_rate)
    weights, ratios, kxw_parts = [], [], []
    for strand in range(2):
        source = joined[strand]
        w = k_tail[:, 0:128] * source
        e4, e8 = pltpu.roll(source, heads, 1), pltpu.roll(source, 2 * heads, 1)
        decay = jnp.where((lanes >= heads) & (lanes < 2 * heads), e4, e8)
        kept = (decay > 0.0) & (lanes >= heads) & (lanes < 3 * heads)
        ratio = jnp.where(
            kept, lane_one * source / jnp.where(kept, decay, 1.0) + k_tail[:, 256:384], 0.0
        )
        ratio = jnp.concatenate(
            [ratio, jnp.zeros((384 - table_rows, 128), F32)], axis=0
        )
        ratio = split(jnp.transpose(ratio)[0:16, :table_rows])
        ratios.append(jnp.concatenate([ratio[0], ratio[1]], axis=0))
        for h in range(heads):
            part = slice(h * HEAD, (h + 1) * HEAD)
            kxw_ref[strand, :, part] = kx[:, part] * jnp.broadcast_to(
                w[:, h : h + 1], (table_rows, HEAD)
            )
        kxw_parts.append(split(kxw_ref[strand]))
    kb_t = jnp.concatenate([kb, jnp.zeros((384 - table_rows, HEAD), F32)], axis=0)
    kb_t = split(jnp.transpose(kb_t)[:, :table_rows])

    d_kb = [jnp.zeros(kb.shape, F32)]
    rate_grads = [jnp.zeros((1, 128), F32)] * heads
    bias_grads = [jnp.zeros((1, 128), F32)] * heads
    tap_sums = [jnp.zeros((16, 2 * HEAD), F32)]
    starts, d_scores, d_starts = [], [[None] * 2, [None] * 2], [None, None]
    for strand in range(2):
        kxw = kxw_parts[strand]
        start = dot(kb_t[0], kxw[0]) + (dot(kb_t[0], kxw[1]) + dot(kb_t[1], kxw[0]))
        starts.append(split(start))
        car_ref[strand] = dot(lhs3(c_parts[strand]), rhs3(starts[strand]))

    def head_pass(strand, h):
        n = strand * heads + h
        part = slice(h * HEAD, (h + 1) * HEAD)
        grow = grow_ref[strand, :, part]
        from_start = grow * car_ref[strand, :, part]
        gate = gate_ref[strand, :, part]
        gated = (y_ref[strand, :, part] + from_start) * gate
        inv = lax.rsqrt(jnp.mean(gated * gated, axis=1, keepdims=True) + EPS)
        normal = gated * inv
        out = normal * gain[:, part]
        if strand == 0:
            y_ref[0, :, part] = out
        else:
            enc_ref[:, part] = (y_ref[0, :, part] + out).astype(BF16)
        d_normal = dg_ref[:, part]
        d_y = d_normal - normal * jnp.mean(normal * d_normal, axis=1, keepdims=True)
        d_y = (d_y * inv) * gate
        x_s = (xh_ref[strand, :, part], xl_ref[strand, :, part])
        mixed_grad = dot(lhs3(split(d_y)), rhs3(x_s, 1), 1, 1)
        direct = d_y * from_start
        wsum, col_sums = [], []
        for half, (rows, cols) in enumerate(live(strand)):
            grad = mixed_grad[rows, cols] * decay_ref[n, rows, cols]
            d_scores[strand][half] = grad if h == 0 else d_scores[strand][half] + grad
            weighted = grad * score_ref[strand, rows, cols]
            wsum.append(split(fold(weighted) + direct[rows]))
            col_sums.append(jnp.sum(weighted, axis=0, keepdims=True))
        wsum = jnp.concatenate([wsum[0][0], wsum[1][0], wsum[0][1], wsum[1][1]], axis=0)
        moved = dot(side, wsum)
        if strand == 0:
            col_sum = col_sums[1] + jnp.concatenate(
                [col_sums[0], jnp.zeros((1, 128), F32)], axis=1
            )
        else:
            col_sum = col_sums[0] + jnp.concatenate(
                [jnp.zeros((1, 128), F32), col_sums[1]], axis=1
            )
        grown = split(d_y * grow)
        gh_ref[strand, :, part] = grown[0]
        gl_ref[strand, :, part] = grown[1]
        rate = rate_row[:, h : h + 1]
        rows = 2 * heads
        rate_grads[h] = (
            rate_grads[h]
            + (moved[n : n + 1] + moved[2 * rows + n : 2 * rows + n + 1])
            - fold(col_sum * cum_rows[n])
        )
        bias_grads[h] = (
            bias_grads[h]
            + fold(col_sum * (rate * sig_rows[n] + ratio_rows[n]))
            - rate * (moved[rows + n : rows + n + 1] + moved[3 * rows + n : 3 * rows + n + 1])
        )

    def state_pass(strand):
        grown = (gh_ref[strand], gl_ref[strand])
        d_starts[strand] = split(dot(lhs3(ct_parts[strand]), rhs3(grown)))

    def table_pass(strand):
        kxw, d_start = kxw_parts[strand], d_starts[strand]
        d_kb[0] = d_kb[0] + dot(lhs3(kxw), rhs3(d_start, 1), 1, 1)
        met = split(dot(lhs3(split(kb)), rhs3(d_start)) * kxw_ref[strand])
        slope = dot(ratios[strand], met[0]) + dot(ratios[strand], met[1])
        slope = slope[0:16] + slope[16:32]
        for h in range(heads):
            part = slice(h * HEAD, (h + 1) * HEAD)
            rate_grads[h] = rate_grads[h] + slope[heads + h : heads + h + 1, part]
            bias_grads[h] = bias_grads[h] + slope[2 * heads + h : 2 * heads + h + 1, part]

    def local_pass(strand):
        whole = filled(d_scores[strand], strand)
        d_scores_s = split(whole)
        d_c = dot(lhs3(d_scores_s), rhs3(b_parts[strand])) + dot(lhs3((gh_ref[strand], gl_ref[strand])), rhs3(starts[strand], 1), 1, 1)
        d_b = dot(lhs3(split(jnp.transpose(whole))), rhs3(c_parts[strand]))
        d_sum = split(jnp.concatenate([d_b, d_c], axis=1) * slopes[strand])
        hits = hits_t[strand].astype(BF16)
        tap_sums[0] = tap_sums[0] + dot(
            jnp.concatenate([hits, hits], axis=1), jnp.concatenate([d_sum[0], d_sum[1]], axis=0)
        )

    for h in range(heads):
        head_pass(0, h)
    state_pass(0)
    for h in range(heads):
        head_pass(1, h)
        if h == 0:
            table_pass(0)
    local_pass(0)
    state_pass(1)
    table_pass(1)
    local_pass(1)
    d_kb, tap_sums = d_kb[0], tap_sums[0]
    d_kb = split(d_kb * kb_slope)
    b_sums = dot(kmer_hits[:, 0:16], d_kb[0][0:256], 0, 0)
    b_sums = b_sums + dot(kmer_hits[:, 0:16], d_kb[1][0:256], 0, 0)
    end_pick = end_pick.astype(BF16)
    b_sums = b_sums + dot(end_pick, d_kb[0][256:]) + dot(end_pick, d_kb[1][256:])
    tap_sums = tap_sums + jnp.concatenate([b_sums, jnp.zeros_like(b_sums)], axis=1)
    conv_rows = []
    for k in range(CONV):
        conv_rows.append(
            jnp.sum(tap_sums[4 * k : 4 * k + 4] * table_s, axis=0, keepdims=True)
        )
    sums = jnp.sum(jnp.concatenate(rate_grads + bias_grads, axis=0), axis=1, keepdims=True)
    lane8 = iota((8, 128), 1)
    row8 = iota((8, 128), 0)
    last = jnp.zeros((8, 128), F32)
    head_total = 8 * heads
    for h in range(heads):
        at = slot * heads + h
        last = jnp.where((row8 == 0) & (lane8 == at), sums[h : h + 1], last)
        last = jnp.where(
            (row8 == 0) & (lane8 == head_total + at), sums[heads + h : heads + h + 1], last
        )
    conv = jnp.concatenate(conv_rows, axis=0)
    value = jnp.concatenate([conv[:, :128], conv[:, 128:], last[0:1]], axis=0)
    if links is not None:
        value = links.reduce(value)
    rate_ref[...] = value[8:9, 0:head_total]
    bias_ref[...] = value[8:9, head_total : 2 * head_total]
    conv_ref[...] = jnp.concatenate([value[0:4], value[4:8]], axis=1)
    if links is not None:
        links.drain()


def layer(args, place, loss_scale, everyone=None, interpret=False):
    (tokens, rc_map, embedding, norm_gain, w_values, w_gates, w_states, w_steps, conv_values,
     conv_states, step_bias, log_rate, skip_gain, head_gain, cotangent) = args
    own, inner = cotangent.shape
    all_heads = 8 * step_bias.shape[0]
    blocks = SIZES["x"] * SIZES["z"]
    chunks = 2 * blocks
    hbm = pl.BlockSpec(memory_space=pl.ANY)
    inputs = [
        tokens, rc_map, step_bias, log_rate, skip_gain, embedding, norm_gain.reshape(1, -1),
        conv_values, conv_states, head_gain.reshape(1, -1), w_states, w_steps.T, w_values, w_gates,
        cotangent,
    ]
    count = len(inputs)
    stores = [
        (pltpu.SMEM if 1 <= n <= 4 else pltpu.VMEM)(a.shape, a.dtype) for n, a in enumerate(inputs)
    ]
    scratch = [
        pltpu.VMEM((chunks, 128), F32),
        pltpu.VMEM((chunks, 128), F32),
        pltpu.VMEM((16 * chunks, 128), F32),
        pltpu.VMEM((8, own, own), F32),
        pltpu.SemaphoreType.DMA((count,)),
        pltpu.VMEM((2, own, inner), BF16),
        pltpu.VMEM((2, own, inner), BF16),
        pltpu.VMEM((2, own, inner), F32),
        pltpu.VMEM((2, own, inner), F32),
        pltpu.VMEM((2, own, inner), F32),
        pltpu.VMEM((own, inner), F32),
        pltpu.VMEM((2, own, own), F32),
        pltpu.VMEM((2, own, inner), BF16),
        pltpu.VMEM((2, own, inner), BF16),
        pltpu.VMEM((2, own, inner), F32),
        pltpu.VMEM((2, 256 + 16, inner), F32),
    ]
    slots = SIZES["c"] + SIZES["x"] * SIZES["y"] + SIZES["z"]
    remote = [
        pltpu.VMEM((SIZES["z"], SIZES["x"], 2, 128), jnp.int32),
        pltpu.VMEM((2, 2, 128), jnp.int32),
        pltpu.VMEM((slots, 9, 128), F32),
        pltpu.VMEM((3, 9, 128), F32),
        pltpu.SemaphoreType.DMA((12,)),
        pltpu.SemaphoreType.DMA((14,)),
        pltpu.SemaphoreType.DMA((slots,)),
        pltpu.SemaphoreType.DMA((slots,)),
    ]
    shapes = (
        pltpu.VMEM((own, inner), BF16),
        pltpu.VMEM((1, all_heads), F32),
        pltpu.VMEM((1, all_heads), F32),
        pltpu.VMEM((4, 256), F32),
    )
    alone = everyone is not None

    def body(*refs):
        refs = list(refs)
        sources, refs = refs[:count], refs[count:]
        if alone:
            links, held, refs = None, refs[0], refs[1:]
            out, refs = refs[:4], refs[4:]
        else:
            out, refs = refs[:4], refs[4:]
            links, held, refs = Links(refs[:8]), refs[0], refs[8:]
        layer_kernel(
            place, links, sources, *out, held, refs[:count], *refs[count:], loss_scale=loss_scale
        )

    if alone:
        params = pltpu.CompilerParams(vmem_limit_bytes=60 * 1024 * 1024)
    else:
        params = pltpu.CompilerParams(
            vmem_limit_bytes=60 * 1024 * 1024, collective_id=0, has_side_effects=True
        )
    return pl.pallas_call(
        body,
        out_shape=shapes,
        in_specs=[hbm] * count + [VM] * alone,
        out_specs=(VM,) * 4,
        scratch_shapes=([] if alone else remote) + stores + scratch,
        compiler_params=params,
        interpret=interpret,
        name="layer",
    )(*inputs, *([everyone] if alone else []))


def emit_kernel(*refs):
    count = len(refs) // 2
    copies = [
        pltpu.make_async_copy(refs[n], refs[count + n], refs[-1].at[n]) for n in range(count)
    ]
    for copy in copies:
        copy.start()
    for copy in copies:
        copy.wait()


def emit(results):
    hbm = pl.BlockSpec(memory_space=pl.ANY)
    return pl.pallas_call(
        emit_kernel,
        out_shape=tuple(jax.ShapeDtypeStruct(r.shape, r.dtype) for r in results),
        in_specs=[VM] * len(results),
        out_specs=(hbm,) * len(results),
        scratch_shapes=[pltpu.SemaphoreType.DMA((len(results),))],
        name="emit",
    )(*[pltpu.with_memory_space_constraint(r, pltpu.VMEM) for r in results])


def solution(mesh):
    count = mesh.shape["ctx"]

    def on_device(*args):
        own = args[-1].shape[0]
        loss_scale = 1.0 / math.sqrt(own * count * HEAD)

        def place():
            return lax.axis_index("ctx"), lax.axis_index("tp")

        results = layer((args[0].reshape(2, 128),) + args[1:], place, loss_scale)
        encoded, rate, bias, conv = emit(results)
        return encoded, rate.reshape(-1), bias.reshape(-1), conv

    tp = P("tp")
    cols = P(None, "tp")
    in_specs = (
        P("ctx"), P(), P(), P(), cols, cols, P(), cols, cols, P(), tp, tp, tp, tp, P("ctx", "tp"),
    )
    return jax.shard_map(
        on_device, mesh=mesh, in_specs=in_specs,
        out_specs=(P("ctx", "tp"), P(), P(), P()), check_vma=False,
    )
```

```python
import math

import jax
import jax.numpy as jnp
from jax import lax
from jax.experimental import pallas as pl
from jax.experimental.pallas import tpu as pltpu
from jax.sharding import PartitionSpec as P

F32 = jnp.float32
BF16 = jnp.bfloat16
HEAD = 128
CONV = 4
EPS = 1e-05
MESH = pl.DeviceIdType.MESH
VM = pl.BlockSpec(memory_space=pltpu.VMEM)


def split(v):
    hi = v.astype(BF16)
    return hi, (v - hi.astype(F32)).astype(BF16)


def dot(a, b, ca=1, cb=0):
    return lax.dot_general(a, b, (((ca,), (cb,)), ((), ())), preferred_element_type=F32)


def lhs3(v):
    hi, lo = v
    return jnp.concatenate([hi, lo, hi], axis=1)


def rhs3(v, axis=0):
    hi, lo = v
    return jnp.concatenate([hi, hi, lo], axis=axis)


def silu(v):
    return v / (1.0 + jnp.exp(-v))


def silu_slope(v):
    s = 1.0 / (1.0 + jnp.exp(-v))
    return s + v * s * (1.0 - s)


def fold(v):
    return v[:, :128] + v[:, 128:] if v.shape[1] > 128 else v


def live(strand):
    if strand == 0:
        return ((slice(0, 128), slice(0, 128)), (slice(128, 256), slice(0, 256)))
    return ((slice(0, 128), slice(0, 256)), (slice(128, 256), slice(128, 256)))


def filled(halves, strand):
    zero = jnp.zeros((128, 128), halves[0].dtype)
    if strand == 0:
        return jnp.concatenate(
            [jnp.concatenate([halves[0], zero], axis=1), halves[1]], axis=0
        )
    return jnp.concatenate([halves[0], jnp.concatenate([zero, halves[1]], axis=1)], axis=0)


def iota(shape, dim):
    return lax.broadcasted_iota(jnp.int32, shape, dim)


def back_one(v, fill):
    rolled = pltpu.roll(v, 1, 1)
    wrapped = pltpu.roll(rolled, 1, 0)
    moved = jnp.where(iota(v.shape, 1) == 0, wrapped, rolled)
    first = (iota(v.shape, 0) == 0) & (iota(v.shape, 1) == 0)
    return jnp.where(first, fill, moved)


def ahead_one(v, fill):
    rows, lanes = v.shape
    rolled = pltpu.roll(v, lanes - 1, 1)
    wrapped = pltpu.roll(rolled, rows - 1, 0)
    moved = jnp.where(iota(v.shape, 1) == lanes - 1, wrapped, rolled)
    last = (iota(v.shape, 0) == rows - 1) & (iota(v.shape, 1) == lanes - 1)
    return jnp.where(last, fill, moved)


def softplus(v):
    return jnp.maximum(v, 0.0) + jnp.log1p(jnp.exp(-jnp.abs(v)))


SIZES = {"x": 4, "z": 8, "y": 4, "c": 2}


def offsets(axes):
    steps = [()]
    for axis in axes:
        steps = [step + (d,) for step in steps for d in range(SIZES[axis])]

    def hops(step):
        return sum(min(d, SIZES[axis] - d) for axis, d in zip(axes, step) if axis != "c")

    return sorted(steps[1:], key=lambda step: -hops(step))


class Links:
    def __init__(self, refs):
        (self.held, self.near, self.slots, self.sent, self.tok_send, self.tok_recv,
         self.sum_send, self.sum_recv) = refs
        ctx, tp = lax.axis_index("ctx"), lax.axis_index("tp")
        self.ctx = ctx
        self.here = {
            "x": ctx // SIZES["z"], "z": lax.rem(ctx, SIZES["z"]),
            "y": tp // SIZES["c"], "c": lax.rem(tp, SIZES["c"]),
        }
        self.drains = []

    def moved(self, axes, step):
        there = dict(self.here)
        for axis, d in zip(axes, step):
            if d:
                there[axis] = lax.rem(there[axis] + d, SIZES[axis])
        return there

    def device(self, there):
        return {
            "ctx": there["x"] * SIZES["z"] + there["z"], "tp": there["y"] * SIZES["c"] + there["c"]
        }

    def beside(self, d):
        count = SIZES["x"] * SIZES["z"]
        return {"ctx": lax.rem(self.ctx + d % count, count)}

    def greet(self):
        barrier = pltpu.get_barrier_semaphore()
        devices = [self.device(self.moved("z", step)) for step in offsets("z")]
        devices += [self.device(self.moved("x", step)) for step in offsets("x")]
        devices += [self.beside(1), self.beside(-1)]
        devices += [self.device(self.moved("xy", step)) for step in offsets("xy") if step[1]]
        devices += [self.device(self.moved("zc", step)) for step in offsets("zc") if step[1]]
        for device in devices:
            pl.semaphore_signal(barrier, inc=1, device_id=device, device_id_type=MESH)
        self.greeted = len(devices)

    def met(self):
        pl.semaphore_wait(pltpu.get_barrier_semaphore(), self.greeted)

    def token_copy(self, source, target, number, arrives, device):
        return pltpu.make_async_remote_copy(
            src_ref=source, dst_ref=target, send_sem=self.tok_send.at[number],
            recv_sem=self.tok_recv.at[arrives], device_id=device, device_id_type=MESH,
        )

    def send(self, copy):
        copy.start()
        self.drains.append(copy)

    def send_tokens(self, tok_ref):
        x, z = self.here["x"], self.here["z"]
        own = self.held.at[z, x]
        for k, step in enumerate(offsets("x")):
            self.send(self.token_copy(tok_ref, own, k, x, self.device(self.moved("x", step))))
        for k, d in ((3, 1), (4, -1)):
            near = self.near.at[k - 3]
            self.send(self.token_copy(tok_ref, near, k, 9 + k, self.beside(d)))
        self.held[z, x] = tok_ref[...]

    def pass_tokens(self, tok_ref):
        x, z = self.here["x"], self.here["z"]
        for step in reversed(offsets("x")):
            there = self.moved("x", step)
            self.token_copy(
                tok_ref, self.held.at[z, there["x"]], 0, there["x"], self.device(there)
            ).wait_recv()
        row = self.held.at[z]
        for k, step in enumerate(offsets("z")):
            there = self.moved("z", step)
            self.send(self.token_copy(row, row, 5 + k, 4 + z, self.device(there)))

    def take_beside(self, tok_ref):
        for k, d in ((3, 1), (4, -1)):
            self.token_copy(tok_ref, self.near.at[k - 3], k, 9 + k, self.beside(d)).wait_recv()

    def take_tokens(self):
        for step in reversed(offsets("z")):
            there = self.moved("z", step)
            row = self.held.at[there["z"]]
            self.token_copy(row, row, 5, 4 + there["z"], self.device(there)).wait_recv()

    def reduce(self, value):
        base = 0
        for number, axes in enumerate(("zc", "xy")):
            self.sent[number] = value
            steps = offsets(axes)
            sending = []

            def slot(there):
                place = 0
                for axis in axes:
                    place = place * SIZES[axis] + there[axis]
                return base + place

            def copy(k, there, place):
                return pltpu.make_async_remote_copy(
                    src_ref=self.sent.at[number],
                    dst_ref=self.slots.at[place],
                    send_sem=self.sum_send.at[base + k],
                    recv_sem=self.sum_recv.at[place],
                    device_id=self.device(there),
                    device_id_type=MESH,
                )

            for k, step in enumerate(steps):
                sending.append(copy(k, self.moved(axes, step), slot(self.here)))
                sending[-1].start()
            self.drain()
            self.drains = sending
            self.slots[slot(self.here)] = value
            for step in reversed(steps):
                there = self.moved(axes, step)
                copy(0, there, slot(there)).wait_recv()
            value = self.slots[base]
            for i in range(1, len(steps) + 1):
                value = value + self.slots[base + i]
            base += len(steps) + 1
        return value

    def drain(self):
        for copy in self.drains:
            copy.wait_send()


def layer_kernel(
    place, links, sources, enc_ref, rate_ref, bias_ref, conv_ref, held, stores, kmer_ref, last_ref, rows_ref, decay_ref, load_sem,
    xh_ref, xl_ref, y_ref, gate_ref, grow_ref, dg_ref, score_ref, gh_ref, gl_ref, car_ref, kxw_ref,
    *, loss_scale,
):
    if links is not None:
        links.greet()
    loads = [
        pltpu.make_async_copy(source, store, load_sem.at[n])
        for n, (source, store) in enumerate(zip(sources, stores))
    ]
    for load in loads:
        load.start()
    (tok_ref, rc, bias, log_rate, skip, emb_ref, ng_ref, cv_ref, cs_ref, hg_ref, ws_ref, wst_ref,
     wv_ref, wg_ref, cot_ref) = stores
    me, slot = place()
    blocks = SIZES["x"] * SIZES["z"]
    chunks = 2 * blocks
    inner = cv_ref.shape[1]
    heads = inner // HEAD
    own = cot_ref.shape[0]
    width = inner + 2 * HEAD
    for load in loads[:10]:
        load.wait()
    e = emb_ref[...].astype(F32)
    scale = lax.rsqrt(jnp.mean(e * e, axis=1, keepdims=True) + EPS)
    normed = (e * scale * ng_ref[...]).astype(BF16)
    normed = jnp.concatenate([normed, jnp.zeros((12, e.shape[1]), BF16)], axis=0)
    loads[10].wait()
    table_s = dot(normed, ws_ref[...])[0:4]
    if links is not None:
        links.met()
        links.send_tokens(tok_ref)
    loads[11].wait()
    table_d = dot(normed, wst_ref[...], 1, 1)[0:4]
    loads[12].wait()
    table_v = dot(normed, wv_ref[...])[0:4]
    loads[13].wait()
    table_z = dot(normed, wg_ref[...])[0:4]
    lane_h = iota((1, heads), 1)
    bias_row = jnp.zeros((1, heads), F32)
    rate_row = jnp.zeros((1, heads), F32)
    for h in range(heads):
        bias_row = jnp.where(lane_h == h, bias[h], bias_row)
        rate_row = jnp.where(lane_h == h, log_rate[h], rate_row)
    rate_row = jnp.exp(rate_row)
    pre_step = table_d + bias_row
    step_t = softplus(pre_step)
    sig_t = 1.0 / (1.0 + jnp.exp(-pre_step))
    ratio_t = jnp.where(step_t > 0.0, sig_t / step_t, 1.0)
    gate_t = silu(table_z)
    table_vs = jnp.concatenate([table_v, table_s], axis=1)
    taps = jnp.concatenate([cv_ref[...], cs_ref[...]], axis=1)
    none2 = jnp.zeros((4, 2 * heads), F32)
    rest = jnp.zeros((4, 128 - 3 * heads), F32)
    tail = jnp.concatenate(
        [
            gate_t,
            step_t, step_t, -rate_row * step_t, rest,
            none2, sig_t, rest,
            none2, ratio_t, rest,
        ],
        axis=1,
    )
    parts = []
    for k in range(CONV):
        last = tail if k == CONV - 1 else jnp.zeros_like(tail)
        parts.append(jnp.concatenate([table_vs * taps[k : k + 1], last], axis=1))
    per_tap = jnp.concatenate(parts, axis=0)
    p_hi = per_tap.astype(BF16)
    p_rest = per_tap - p_hi.astype(F32)
    p_mid = p_rest.astype(BF16)
    p_low = (p_rest - p_mid.astype(F32)).astype(BF16)
    per_tap3 = jnp.concatenate([p_hi, p_mid, p_low], axis=0)
    place_cols = width + inner

    column = iota((256, 48), 1) % 16
    index, tap = iota((256, 48), 0), column // 4
    digit = lax.shift_right_logical(index & 63, jnp.maximum(2 * (2 - tap), 0)) & 3
    digit = jnp.where(tap == 3, lax.shift_right_logical(index, 6), digit)
    kmer_hits = (digit == column % 4).astype(F32).astype(BF16)
    kmer_sum = dot(kmer_hits, per_tap3[:, : inner + HEAD])
    kmer_tail = dot(kmer_hits, per_tap3[:, place_cols:])
    kx = silu(kmer_sum[:, :inner])
    kb = silu(kmer_sum[:, inner:])
    kb_slope = silu_slope(kmer_sum[:, inner:])

    tri_in = (iota((own, own), 0) <= iota((own, own), 1)).astype(BF16)
    tri_out = (iota((own, own), 0) >= iota((own, own), 1)).astype(BF16)
    pad4 = jnp.zeros((12, own), BF16)

    def complement(v):
        out = jnp.full(v.shape, -1.0, F32)
        for a in range(4):
            out = jnp.where(v == a, rc[a].astype(F32), out)
        return out

    pair = tok_ref[...].astype(F32)
    mine = jnp.concatenate([pair[0:1], pair[1:2]], axis=1)
    mine_rc = complement(mine)
    letters = iota((4, own), 0).astype(F32)
    own_f = (jnp.broadcast_to(mine, (4, own)) == letters).astype(F32)
    own_r = (jnp.broadcast_to(mine_rc, (4, own)) == letters).astype(F32)
    n_f = dot(jnp.concatenate([own_f.astype(BF16), pad4], axis=0), tri_in)
    n_r = dot(jnp.concatenate([own_r.astype(BF16), pad4], axis=0), tri_out)

    def blend(weights, table, h):
        return sum(weights[a : a + 1] * table[a : a + 1, h : h + 1] for a in range(4))

    cum_rows, sig_rows, step_rows, ratio_rows = [], [], [], []
    for counted, hit in ((n_f, own_f), (n_r, own_r)):
        for h in range(heads):
            cum_rows.append(-(rate_row[:, h : h + 1] * blend(counted, step_t, h)))
            sig_rows.append(blend(counted, sig_t, h))
            step_rows.append(blend(hit, step_t, h))
            ratio_rows.append(blend(hit, ratio_t, h))
    cum8 = jnp.concatenate(cum_rows, axis=0)
    both = split(jnp.concatenate([cum8] + sig_rows, axis=0))
    side = jnp.concatenate([both[0], both[1]], axis=0)
    side = jnp.concatenate([side, side], axis=1)
    columns = jnp.transpose(
        jnp.concatenate([cum8, jnp.zeros((128 - 2 * heads, own), F32)], axis=0)
    )
    square = (iota((128, 128), 0), iota((128, 128), 1))
    causal = (square[0] >= square[1], square[0] <= square[1])
    for n in range(2 * heads):
        cum_c = jnp.broadcast_to(columns[:, n : n + 1], (own, 128))
        for rows, _ in live(n // heads):
            for half in range(own // 128):
                cols = slice(half * 128, half * 128 + 128)
                if (cols.start > rows.start) if n < heads else (cols.start < rows.start):
                    continue
                grown = jnp.exp(cum_c[rows] - cum_rows[n][:, cols])
                if cols.start == rows.start:
                    grown = jnp.where(causal[n // heads], grown, 0.0)
                decay_ref[n, rows, cols] = grown * step_rows[n][:, cols]
        part = slice((n % heads) * HEAD, (n % heads + 1) * HEAD)
        grow_ref[n // heads, :, part] = jnp.exp(cum_c)
    loads[14].wait()
    gain = hg_ref[...]
    dg_ref[...] = cot_ref[...].astype(F32) * (gain * loss_scale)

    if links is not None:
        links.pass_tokens(tok_ref)
        links.take_beside(tok_ref)
        earlier, later = links.near[0], links.near[1]
    else:
        earlier, later = (
            held[lax.rem(there, SIZES["z"]), there // SIZES["z"]]
            for there in (lax.rem(me + blocks - 1, blocks), lax.rem(me + 1, blocks))
        )
    earlier, later = earlier.astype(F32)[1:2], later.astype(F32)[0:1]
    earlier = jnp.where(me > 0, earlier, -1.0)
    later = jnp.where(me < blocks - 1, later, -1.0)
    line = jnp.concatenate([earlier, mine, later], axis=1)
    line = jnp.broadcast_to(line, (8, line.shape[1]))
    line_rc = complement(line)
    letters8 = iota((8, own), 0).astype(F32)
    f_hits, r_hits = [], []
    for k in range(CONV):
        d = CONV - 1 - k
        f_line = pltpu.roll(line, d, 1) if d else line
        r_line = pltpu.roll(line_rc, line.shape[1] - d, 1) if d else line_rc
        f_hits.append((f_line[:, 128 : 128 + own] == letters8)[0:4].astype(F32))
        r_hits.append((r_line[:, 128 : 128 + own] == letters8)[0:4].astype(F32))
    hits_t = [jnp.concatenate(f_hits, axis=0), jnp.concatenate(r_hits, axis=0)]
    slopes, c_parts, ct_parts, b_parts = [], [], [], []
    for strand in range(2):
        hits = jnp.concatenate([hits_t[strand]] * 3, axis=0).astype(BF16)
        summed = dot(hits, per_tap3[:, :place_cols], 0, 0)
        gate_ref[strand] = summed[:, width:]
        states = silu(summed[:, inner:width])
        slopes.append(silu_slope(summed[:, inner:width]))
        b_s = split(states[:, :HEAD])
        c_s = split(states[:, HEAD:])
        b_parts.append(b_s)
        c_parts.append(c_s)
        ct_parts.append(split(jnp.transpose(states[:, HEAD:])))
        scores = dot(lhs3(c_s), rhs3(b_s, 1), 1, 1)
        score_ref[strand] = scores
        for h in range(heads):
            part = slice(h * HEAD, (h + 1) * HEAD)
            x_h = silu(summed[:, part])
            x_s = split(x_h)
            xh_ref[strand, :, part] = x_s[0]
            xl_ref[strand, :, part] = x_s[1]
            mixing = [
                split(scores[rows, cols] * decay_ref[strand * heads + h, rows, cols])
                for rows, cols in live(strand)
            ]
            mixing = [filled([half[k] for half in mixing], strand) for k in range(2)]
            y_ref[strand, :, part] = dot(lhs3(mixing), rhs3(x_s)) + skip[h] * x_h

    if links is not None:
        links.take_tokens()
    for r in range(blocks):
        kmer_ref[2 * r : 2 * r + 2, :] = held[r % SIZES["z"], r // SIZES["z"]].astype(F32)
    tok = kmer_ref[...]
    comp = complement(tok)
    f_shift, r_shift = [tok], [comp]
    for _ in range(CONV - 1):
        f_shift.append(back_one(f_shift[-1], -1.0))
        r_shift.append(ahead_one(r_shift[-1], -1.0))

    row = iota(tok.shape, 0)
    position = row * 128 + iota(tok.shape, 1)
    before = row < 2 * me
    outside = before | (row >= 2 * me + 2)
    kmer_f = f_shift[1] + 4.0 * f_shift[2] + 16.0 * f_shift[3]
    kmer_r = r_shift[1] + 4.0 * r_shift[2] + 16.0 * r_shift[3]
    kmer = jnp.where(before, kmer_f, kmer_r)
    edge = (before & (position < CONV - 1)) | (position >= chunks * 128 - (CONV - 1))
    kmer_ref[...] = jnp.where(edge & outside, -1.0, kmer)
    mixed = jnp.where(outside, jnp.where(before, tok, comp), -1.0)
    last_ref[...] = mixed
    tri = (iota((128, 128), 0) <= iota((128, 128), 1)).astype(BF16)
    ones = jnp.ones((128, 128), BF16)
    strict = (iota((chunks, chunks), 1) < iota((chunks, chunks), 0)).astype(BF16)
    counts = []
    for a in range(4):
        hit = (mixed == a).astype(F32)
        hit16 = hit.astype(BF16)
        within = dot(hit16, tri)
        offset = dot(strict, dot(hit16, ones).astype(BF16))
        total_f = jnp.sum(jnp.where(before, hit, 0.0), keepdims=True)
        inclusive = within + offset - total_f
        counts.append(jnp.where(before, -inclusive, inclusive - hit))
    for h in range(heads):
        steps_sum = sum(counts[a] * step_t[a : a + 1, h : h + 1] for a in range(4))
        sig_sum = sum(counts[a] * sig_t[a : a + 1, h : h + 1] for a in range(4))
        exponent = -(rate_row[:, h : h + 1] * steps_sum)
        decay = jnp.where(outside, jnp.exp(exponent), 0.0)
        for q, value in enumerate((decay, decay * exponent, decay * sig_sum)):
            base = (q * heads + h) * chunks
            rows_ref[base : base + chunks, :] = value
    for q in range(3 * heads, 16):
        rows_ref[q * chunks : (q + 1) * chunks, :] = jnp.zeros((chunks, 128), F32)

    first_id = iota((64, 128), 0).astype(F32).astype(BF16)
    one16, zero16 = jnp.ones((64, 128), BF16), jnp.zeros((64, 128), BF16)
    nothing = jnp.zeros((32, 128), BF16)

    def load_rows(chunk):
        return rows_ref[pl.ds(chunk, 16, stride=chunks), :]

    acc_f = jnp.zeros((64, 128), F32)
    acc_r = jnp.zeros((64, 128), F32)
    for block in range(blocks):
        hits, weights = [], []
        for chunk in (2 * block, 2 * block + 1):
            w = jnp.concatenate(split(load_rows(chunk)), axis=0)
            final = jnp.broadcast_to(last_ref[chunk : chunk + 1, :], (32, 128)).astype(BF16)
            weights.append(
                jnp.concatenate([jnp.where(final == a, w, nothing) for a in range(4)], axis=0)
            )
            ids = jnp.broadcast_to(kmer_ref[chunk : chunk + 1, :], (64, 128)).astype(BF16)
            hits.append(jnp.where(ids == first_id, one16, zero16))
        found = dot(jnp.concatenate(hits, axis=1), jnp.concatenate(weights, axis=1), 1, 1)
        acc_f = acc_f + jnp.where(block < me, found, 0.0)
        acc_r = acc_r + jnp.where(block > me, found, 0.0)
    lane = iota((16, 128), 1)
    e_f = split(jnp.where(lane < CONV - 1, load_rows(0), 0.0))
    e_r = split(jnp.where(lane >= 128 - (CONV - 1), load_rows(chunks - 1), 0.0))
    pick_row = iota((16, 128), 0)
    pick = (lane == jnp.where(pick_row < 8, pick_row, pick_row + 112)).astype(BF16)

    def by_row(acc, ends):
        parts = [acc] + [pltpu.roll(acc, 128 - 32 * a, 1) for a in range(1, 4)]
        ends = jnp.concatenate([ends[0], ends[1], jnp.zeros((96, 128), BF16)], axis=0)
        joined = jnp.concatenate(parts + [dot(pick, ends, 1, 1)], axis=0)
        return joined + pltpu.roll(joined, 128 - 16, 1)

    joined = (by_row(acc_f, e_f), by_row(acc_r, e_r))

    end_hits = []
    for k in range(CONV):
        d = CONV - 1 - k
        ends = jnp.where(
            iota((1, 128), 1) < 64, f_shift[d][0:1, :], r_shift[d][chunks - 1 : chunks, :]
        )
        end_hits.append(
            (jnp.broadcast_to(ends, (4, 128)) == iota((4, 128), 0).astype(F32)).astype(F32)
        )
    end_hits = jnp.concatenate(end_hits, axis=0).astype(BF16)
    end_pick = dot(end_hits, pick, 1, 1)
    end3 = jnp.concatenate([end_pick] * 3, axis=0).astype(BF16)
    end_sum = dot(end3, per_tap3, 0, 0)
    kx = jnp.concatenate([kx, silu(end_sum[:, :inner])], axis=0)
    kb = jnp.concatenate([kb, silu(end_sum[:, inner : inner + HEAD])], axis=0)
    kb_slope = jnp.concatenate([kb_slope, silu_slope(end_sum[:, inner : inner + HEAD])], axis=0)
    k_tail = jnp.concatenate([kmer_tail, end_sum[:, place_cols:]], axis=0)
    table_rows = kx.shape[0]

    lanes = iota((1, 128), 1)
    lane_rate = jnp.zeros((1, 128), F32)
    for h in range(heads):
        lane_rate = jnp.where(lanes == 2 * heads + h, -rate_row[:, h : h + 1], lane_rate)
    lane_one = jnp.where((lanes >= heads) & (lanes < 2 * heads), 1.0, lane_rate)
    weights, ratios, kxw_parts = [], [], []
    for strand in range(2):
        source = joined[strand]
        w = k_tail[:, 0:128] * source
        e4, e8 = pltpu.roll(source, heads, 1), pltpu.roll(source, 2 * heads, 1)
        decay = jnp.where((lanes >= heads) & (lanes < 2 * heads), e4, e8)
        kept = (decay > 0.0) & (lanes >= heads) & (lanes < 3 * heads)
        ratio = jnp.where(
            kept, lane_one * source / jnp.where(kept, decay, 1.0) + k_tail[:, 256:384], 0.0
        )
        ratio = jnp.concatenate(
            [ratio, jnp.zeros((384 - table_rows, 128), F32)], axis=0
        )
        ratio = split(jnp.transpose(ratio)[0:16, :table_rows])
        ratios.append(jnp.concatenate([ratio[0], ratio[1]], axis=0))
        for h in range(heads):
            part = slice(h * HEAD, (h + 1) * HEAD)
            kxw_ref[strand, :, part] = kx[:, part] * jnp.broadcast_to(
                w[:, h : h + 1], (table_rows, HEAD)
            )
        kxw_parts.append(split(kxw_ref[strand]))
    kb_t = jnp.concatenate([kb, jnp.zeros((384 - table_rows, HEAD), F32)], axis=0)
    kb_t = split(jnp.transpose(kb_t)[:, :table_rows])

    d_kb = [jnp.zeros(kb.shape, F32)]
    rate_grads = [jnp.zeros((1, 128), F32)] * heads
    bias_grads = [jnp.zeros((1, 128), F32)] * heads
    tap_sums = [jnp.zeros((16, 2 * HEAD), F32)]
    starts, d_scores, d_starts = [], [[None] * 2, [None] * 2], [None, None]
    for strand in range(2):
        kxw = kxw_parts[strand]
        start = dot(kb_t[0], kxw[0]) + (dot(kb_t[0], kxw[1]) + dot(kb_t[1], kxw[0]))
        starts.append(split(start))
        car_ref[strand] = dot(lhs3(c_parts[strand]), rhs3(starts[strand]))

    def head_pass(strand, h):
        n = strand * heads + h
        part = slice(h * HEAD, (h + 1) * HEAD)
        grow = grow_ref[strand, :, part]
        from_start = grow * car_ref[strand, :, part]
        gate = gate_ref[strand, :, part]
        gated = (y_ref[strand, :, part] + from_start) * gate
        inv = lax.rsqrt(jnp.mean(gated * gated, axis=1, keepdims=True) + EPS)
        normal = gated * inv
        out = normal * gain[:, part]
        if strand == 0:
            y_ref[0, :, part] = out
        else:
            enc_ref[:, part] = (y_ref[0, :, part] + out).astype(BF16)
        d_normal = dg_ref[:, part]
        d_y = d_normal - normal * jnp.mean(normal * d_normal, axis=1, keepdims=True)
        d_y = (d_y * inv) * gate
        x_s = (xh_ref[strand, :, part], xl_ref[strand, :, part])
        mixed_grad = dot(lhs3(split(d_y)), rhs3(x_s, 1), 1, 1)
        direct = d_y * from_start
        wsum, col_sums = [], []
        for half, (rows, cols) in enumerate(live(strand)):
            grad = mixed_grad[rows, cols] * decay_ref[n, rows, cols]
            d_scores[strand][half] = grad if h == 0 else d_scores[strand][half] + grad
            weighted = grad * score_ref[strand, rows, cols]
            wsum.append(split(fold(weighted) + direct[rows]))
            col_sums.append(jnp.sum(weighted, axis=0, keepdims=True))
        wsum = jnp.concatenate([wsum[0][0], wsum[1][0], wsum[0][1], wsum[1][1]], axis=0)
        moved = dot(side, wsum)
        if strand == 0:
            col_sum = col_sums[1] + jnp.concatenate(
                [col_sums[0], jnp.zeros((1, 128), F32)], axis=1
            )
        else:
            col_sum = col_sums[0] + jnp.concatenate(
                [jnp.zeros((1, 128), F32), col_sums[1]], axis=1
            )
        grown = split(d_y * grow)
        gh_ref[strand, :, part] = grown[0]
        gl_ref[strand, :, part] = grown[1]
        rate = rate_row[:, h : h + 1]
        rows = 2 * heads
        rate_grads[h] = (
            rate_grads[h]
            + (moved[n : n + 1] + moved[2 * rows + n : 2 * rows + n + 1])
            - fold(col_sum * cum_rows[n])
        )
        bias_grads[h] = (
            bias_grads[h]
            + fold(col_sum * (rate * sig_rows[n] + ratio_rows[n]))
            - rate * (moved[rows + n : rows + n + 1] + moved[3 * rows + n : 3 * rows + n + 1])
        )

    def state_pass(strand):
        grown = (gh_ref[strand], gl_ref[strand])
        d_starts[strand] = split(dot(lhs3(ct_parts[strand]), rhs3(grown)))

    def table_pass(strand):
        kxw, d_start = kxw_parts[strand], d_starts[strand]
        d_kb[0] = d_kb[0] + dot(lhs3(kxw), rhs3(d_start, 1), 1, 1)
        met = split(dot(lhs3(split(kb)), rhs3(d_start)) * kxw_ref[strand])
        slope = dot(ratios[strand], met[0]) + dot(ratios[strand], met[1])
        slope = slope[0:16] + slope[16:32]
        for h in range(heads):
            part = slice(h * HEAD, (h + 1) * HEAD)
            rate_grads[h] = rate_grads[h] + slope[heads + h : heads + h + 1, part]
            bias_grads[h] = bias_grads[h] + slope[2 * heads + h : 2 * heads + h + 1, part]

    def local_pass(strand):
        whole = filled(d_scores[strand], strand)
        d_scores_s = split(whole)
        d_c = dot(lhs3(d_scores_s), rhs3(b_parts[strand])) + dot(lhs3((gh_ref[strand], gl_ref[strand])), rhs3(starts[strand], 1), 1, 1)
        d_b = dot(lhs3(split(jnp.transpose(whole))), rhs3(c_parts[strand]))
        d_sum = split(jnp.concatenate([d_b, d_c], axis=1) * slopes[strand])
        hits = hits_t[strand].astype(BF16)
        tap_sums[0] = tap_sums[0] + dot(
            jnp.concatenate([hits, hits], axis=1), jnp.concatenate([d_sum[0], d_sum[1]], axis=0)
        )

    for h in range(heads):
        head_pass(0, h)
    state_pass(0)
    for h in range(heads):
        head_pass(1, h)
        if h == 0:
            table_pass(0)
    local_pass(0)
    state_pass(1)
    table_pass(1)
    local_pass(1)
    d_kb, tap_sums = d_kb[0], tap_sums[0]
    d_kb = split(d_kb * kb_slope)
    b_sums = dot(kmer_hits[:, 0:16], d_kb[0][0:256], 0, 0)
    b_sums = b_sums + dot(kmer_hits[:, 0:16], d_kb[1][0:256], 0, 0)
    end_pick = end_pick.astype(BF16)
    b_sums = b_sums + dot(end_pick, d_kb[0][256:]) + dot(end_pick, d_kb[1][256:])
    tap_sums = tap_sums + jnp.concatenate([b_sums, jnp.zeros_like(b_sums)], axis=1)
    conv_rows = []
    for k in range(CONV):
        conv_rows.append(
            jnp.sum(tap_sums[4 * k : 4 * k + 4] * table_s, axis=0, keepdims=True)
        )
    sums = jnp.sum(jnp.concatenate(rate_grads + bias_grads, axis=0), axis=1, keepdims=True)
    lane8 = iota((8, 128), 1)
    row8 = iota((8, 128), 0)
    last = jnp.zeros((8, 128), F32)
    head_total = 8 * heads
    for h in range(heads):
        at = slot * heads + h
        last = jnp.where((row8 == 0) & (lane8 == at), sums[h : h + 1], last)
        last = jnp.where(
            (row8 == 0) & (lane8 == head_total + at), sums[heads + h : heads + h + 1], last
        )
    conv = jnp.concatenate(conv_rows, axis=0)
    value = jnp.concatenate([conv[:, :128], conv[:, 128:], last[0:1]], axis=0)
    if links is not None:
        value = links.reduce(value)
    rate_ref[...] = value[8:9, 0:head_total]
    bias_ref[...] = value[8:9, head_total : 2 * head_total]
    conv_ref[...] = jnp.concatenate([value[0:4], value[4:8]], axis=1)
    if links is not None:
        links.drain()


def layer(args, place, loss_scale, everyone=None, interpret=False):
    (tokens, rc_map, embedding, norm_gain, w_values, w_gates, w_states, w_steps, conv_values,
     conv_states, step_bias, log_rate, skip_gain, head_gain, cotangent) = args
    own, inner = cotangent.shape
    all_heads = 8 * step_bias.shape[0]
    blocks = SIZES["x"] * SIZES["z"]
    chunks = 2 * blocks
    hbm = pl.BlockSpec(memory_space=pl.ANY)
    inputs = [
        tokens, rc_map, step_bias, log_rate, skip_gain, embedding, norm_gain.reshape(1, -1),
        conv_values, conv_states, head_gain.reshape(1, -1), w_states, w_steps.T, w_values, w_gates,
        cotangent,
    ]
    count = len(inputs)
    stores = [
        (pltpu.SMEM if 1 <= n <= 4 else pltpu.VMEM)(a.shape, a.dtype) for n, a in enumerate(inputs)
    ]
    scratch = [
        pltpu.VMEM((chunks, 128), F32),
        pltpu.VMEM((chunks, 128), F32),
        pltpu.VMEM((16 * chunks, 128), F32),
        pltpu.VMEM((8, own, own), F32),
        pltpu.SemaphoreType.DMA((count,)),
        pltpu.VMEM((2, own, inner), BF16),
        pltpu.VMEM((2, own, inner), BF16),
        pltpu.VMEM((2, own, inner), F32),
        pltpu.VMEM((2, own, inner), F32),
        pltpu.VMEM((2, own, inner), F32),
        pltpu.VMEM((own, inner), F32),
        pltpu.VMEM((2, own, own), F32),
        pltpu.VMEM((2, own, inner), BF16),
        pltpu.VMEM((2, own, inner), BF16),
        pltpu.VMEM((2, own, inner), F32),
        pltpu.VMEM((2, 256 + 16, inner), F32),
    ]
    slots = SIZES["z"] * SIZES["c"] + SIZES["x"] * SIZES["y"]
    remote = [
        pltpu.VMEM((SIZES["z"], SIZES["x"], 2, 128), jnp.int32),
        pltpu.VMEM((2, 2, 128), jnp.int32),
        pltpu.VMEM((slots, 9, 128), F32),
        pltpu.VMEM((2, 9, 128), F32),
        pltpu.SemaphoreType.DMA((12,)),
        pltpu.SemaphoreType.DMA((14,)),
        pltpu.SemaphoreType.DMA((slots,)),
        pltpu.SemaphoreType.DMA((slots,)),
    ]
    shapes = (
        pltpu.VMEM((own, inner), BF16),
        pltpu.VMEM((1, all_heads), F32),
        pltpu.VMEM((1, all_heads), F32),
        pltpu.VMEM((4, 256), F32),
    )
    alone = everyone is not None

    def body(*refs):
        refs = list(refs)
        sources, refs = refs[:count], refs[count:]
        if alone:
            links, held, refs = None, refs[0], refs[1:]
            out, refs = refs[:4], refs[4:]
        else:
            out, refs = refs[:4], refs[4:]
            links, held, refs = Links(refs[:8]), refs[0], refs[8:]
        layer_kernel(
            place, links, sources, *out, held, refs[:count], *refs[count:], loss_scale=loss_scale
        )

    if alone:
        params = pltpu.CompilerParams(vmem_limit_bytes=60 * 1024 * 1024)
    else:
        params = pltpu.CompilerParams(
            vmem_limit_bytes=60 * 1024 * 1024, collective_id=0, has_side_effects=True
        )
    return pl.pallas_call(
        body,
        out_shape=shapes,
        in_specs=[hbm] * count + [VM] * alone,
        out_specs=(VM,) * 4,
        scratch_shapes=([] if alone else remote) + stores + scratch,
        compiler_params=params,
        interpret=interpret,
        name="layer",
    )(*inputs, *([everyone] if alone else []))


def emit_kernel(*refs):
    count = len(refs) // 2
    copies = [
        pltpu.make_async_copy(refs[n], refs[count + n], refs[-1].at[n]) for n in range(count)
    ]
    for copy in copies:
        copy.start()
    for copy in copies:
        copy.wait()


def emit(results):
    hbm = pl.BlockSpec(memory_space=pl.ANY)
    return pl.pallas_call(
        emit_kernel,
        out_shape=tuple(jax.ShapeDtypeStruct(r.shape, r.dtype) for r in results),
        in_specs=[VM] * len(results),
        out_specs=(hbm,) * len(results),
        scratch_shapes=[pltpu.SemaphoreType.DMA((len(results),))],
        name="emit",
    )(*[pltpu.with_memory_space_constraint(r, pltpu.VMEM) for r in results])


def solution(mesh):
    count = mesh.shape["ctx"]

    def on_device(*args):
        own = args[-1].shape[0]
        loss_scale = 1.0 / math.sqrt(own * count * HEAD)

        def place():
            return lax.axis_index("ctx"), lax.axis_index("tp")

        results = layer((args[0].reshape(2, 128),) + args[1:], place, loss_scale)
        encoded, rate, bias, conv = emit(results)
        return encoded, rate.reshape(-1), bias.reshape(-1), conv

    tp = P("tp")
    cols = P(None, "tp")
    in_specs = (
        P("ctx"), P(), P(), P(), cols, cols, P(), cols, cols, P(), tp, tp, tp, tp, P("ctx", "tp"),
    )
    return jax.shard_map(
        on_device, mesh=mesh, in_specs=in_specs,
        out_specs=(P("ctx", "tp"), P(), P(), P()), check_vma=False,
    )
```

```python
import math

import jax
import jax.numpy as jnp
from jax import lax
from jax.experimental import pallas as pl
from jax.experimental.pallas import tpu as pltpu
from jax.sharding import PartitionSpec as P

F32 = jnp.float32
BF16 = jnp.bfloat16
HEAD = 128
CONV = 4
EPS = 1e-05
MESH = pl.DeviceIdType.MESH
VM = pl.BlockSpec(memory_space=pltpu.VMEM)


def split(v):
    hi = v.astype(BF16)
    return hi, (v - hi.astype(F32)).astype(BF16)


def dot(a, b, ca=1, cb=0):
    return lax.dot_general(a, b, (((ca,), (cb,)), ((), ())), preferred_element_type=F32)


def lhs3(v):
    hi, lo = v
    return jnp.concatenate([hi, lo, hi], axis=1)


def rhs3(v, axis=0):
    hi, lo = v
    return jnp.concatenate([hi, hi, lo], axis=axis)


def silu(v):
    return v / (1.0 + jnp.exp(-v))


def silu_slope(v):
    s = 1.0 / (1.0 + jnp.exp(-v))
    return s + v * s * (1.0 - s)


def fold(v):
    return v[:, :128] + v[:, 128:] if v.shape[1] > 128 else v


def live(strand):
    if strand == 0:
        return ((slice(0, 128), slice(0, 128)), (slice(128, 256), slice(0, 256)))
    return ((slice(0, 128), slice(0, 256)), (slice(128, 256), slice(128, 256)))


def filled(halves, strand):
    zero = jnp.zeros((128, 128), halves[0].dtype)
    if strand == 0:
        return jnp.concatenate(
            [jnp.concatenate([halves[0], zero], axis=1), halves[1]], axis=0
        )
    return jnp.concatenate([halves[0], jnp.concatenate([zero, halves[1]], axis=1)], axis=0)


def iota(shape, dim):
    return lax.broadcasted_iota(jnp.int32, shape, dim)


def back_one(v, fill):
    rolled = pltpu.roll(v, 1, 1)
    wrapped = pltpu.roll(rolled, 1, 0)
    moved = jnp.where(iota(v.shape, 1) == 0, wrapped, rolled)
    first = (iota(v.shape, 0) == 0) & (iota(v.shape, 1) == 0)
    return jnp.where(first, fill, moved)


def ahead_one(v, fill):
    rows, lanes = v.shape
    rolled = pltpu.roll(v, lanes - 1, 1)
    wrapped = pltpu.roll(rolled, rows - 1, 0)
    moved = jnp.where(iota(v.shape, 1) == lanes - 1, wrapped, rolled)
    last = (iota(v.shape, 0) == rows - 1) & (iota(v.shape, 1) == lanes - 1)
    return jnp.where(last, fill, moved)


def softplus(v):
    return jnp.maximum(v, 0.0) + jnp.log1p(jnp.exp(-jnp.abs(v)))


SIZES = {"x": 4, "z": 8, "y": 4, "c": 2}


def offsets(axes):
    steps = [()]
    for axis in axes:
        steps = [step + (d,) for step in steps for d in range(SIZES[axis])]

    def hops(step):
        return sum(min(d, SIZES[axis] - d) for axis, d in zip(axes, step) if axis != "c")

    return sorted(steps[1:], key=lambda step: -hops(step))


class Links:
    def __init__(self, refs):
        (self.held, self.near, self.slots, self.sent, self.tok_send, self.tok_recv,
         self.sum_send, self.sum_recv) = refs
        ctx, tp = lax.axis_index("ctx"), lax.axis_index("tp")
        self.ctx = ctx
        self.here = {
            "x": ctx // SIZES["z"], "z": lax.rem(ctx, SIZES["z"]),
            "y": tp // SIZES["c"], "c": lax.rem(tp, SIZES["c"]),
        }
        self.drains = []

    def moved(self, axes, step):
        there = dict(self.here)
        for axis, d in zip(axes, step):
            if d:
                there[axis] = lax.rem(there[axis] + d, SIZES[axis])
        return there

    def device(self, there):
        return {
            "ctx": there["x"] * SIZES["z"] + there["z"], "tp": there["y"] * SIZES["c"] + there["c"]
        }

    def beside(self, d):
        count = SIZES["x"] * SIZES["z"]
        return {"ctx": lax.rem(self.ctx + d % count, count)}

    def greet(self):
        barrier = pltpu.get_barrier_semaphore()
        devices = [self.device(self.moved("z", step)) for step in offsets("z")]
        devices += [self.device(self.moved("x", step)) for step in offsets("x")]
        devices += [self.beside(1), self.beside(-1)]
        devices += [self.device(self.moved("xy", step)) for step in offsets("xy") if step[1]]
        devices += [self.device(self.moved("c", step)) for step in offsets("c")]
        for device in devices:
            pl.semaphore_signal(barrier, inc=1, device_id=device, device_id_type=MESH)
        self.greeted = len(devices)

    def met(self):
        pl.semaphore_wait(pltpu.get_barrier_semaphore(), self.greeted)

    def token_copy(self, source, target, number, arrives, device):
        return pltpu.make_async_remote_copy(
            src_ref=source, dst_ref=target, send_sem=self.tok_send.at[number],
            recv_sem=self.tok_recv.at[arrives], device_id=device, device_id_type=MESH,
        )

    def send(self, copy):
        copy.start()
        self.drains.append(copy)

    def send_tokens(self, tok_ref):
        x, z = self.here["x"], self.here["z"]
        own = self.held.at[z, x]
        for k, step in enumerate(offsets("x")):
            self.send(self.token_copy(tok_ref, own, k, x, self.device(self.moved("x", step))))
        for k, d in ((3, 1), (4, -1)):
            near = self.near.at[k - 3]
            self.send(self.token_copy(tok_ref, near, k, 9 + k, self.beside(d)))
        self.held[z, x] = tok_ref[...]

    def pass_tokens(self, tok_ref):
        x, z = self.here["x"], self.here["z"]
        for step in reversed(offsets("x")):
            there = self.moved("x", step)
            self.token_copy(
                tok_ref, self.held.at[z, there["x"]], 0, there["x"], self.device(there)
            ).wait_recv()
        row = self.held.at[z]
        for k, step in enumerate(offsets("z")):
            there = self.moved("z", step)
            self.send(self.token_copy(row, row, 5 + k, 4 + z, self.device(there)))

    def take_beside(self, tok_ref):
        for k, d in ((3, 1), (4, -1)):
            self.token_copy(tok_ref, self.near.at[k - 3], k, 9 + k, self.beside(d)).wait_recv()

    def take_tokens(self):
        for step in reversed(offsets("z")):
            there = self.moved("z", step)
            row = self.held.at[there["z"]]
            self.token_copy(row, row, 5, 4 + there["z"], self.device(there)).wait_recv()

    def reduce(self, value):
        base = 0
        for number, axes in enumerate(("c", "xy", "z")):
            self.sent[number] = value
            steps = offsets(axes)
            sending = []

            def slot(there):
                place = 0
                for axis in axes:
                    place = place * SIZES[axis] + there[axis]
                return base + place

            def copy(k, there, place):
                return pltpu.make_async_remote_copy(
                    src_ref=self.sent.at[number],
                    dst_ref=self.slots.at[place],
                    send_sem=self.sum_send.at[base + k],
                    recv_sem=self.sum_recv.at[place],
                    device_id=self.device(there),
                    device_id_type=MESH,
                )

            for k, step in enumerate(steps):
                sending.append(copy(k, self.moved(axes, step), slot(self.here)))
                sending[-1].start()
            self.drain()
            self.drains = sending
            self.slots[slot(self.here)] = value
            for step in reversed(steps):
                there = self.moved(axes, step)
                copy(0, there, slot(there)).wait_recv()
            value = self.slots[base]
            for i in range(1, len(steps) + 1):
                value = value + self.slots[base + i]
            base += len(steps) + 1
        return value

    def drain(self):
        for copy in self.drains:
            copy.wait_send()


def layer_kernel(
    place, links, sources, enc_ref, rate_ref, bias_ref, conv_ref, held, stores, kmer_ref, last_ref, rows_ref, decay_ref, load_sem,
    xh_ref, xl_ref, y_ref, gate_ref, grow_ref, dg_ref, score_ref, gh_ref, gl_ref, car_ref, kxw_ref,
    *, loss_scale,
):
    if links is not None:
        links.greet()
    loads = [
        pltpu.make_async_copy(source, store, load_sem.at[n])
        for n, (source, store) in enumerate(zip(sources, stores))
    ]
    for load in loads:
        load.start()
    (tok_ref, rc, bias, log_rate, skip, emb_ref, ng_ref, cv_ref, cs_ref, hg_ref, ws_ref, wst_ref,
     wv_ref, wg_ref, cot_ref) = stores
    me, slot = place()
    blocks = SIZES["x"] * SIZES["z"]
    chunks = 2 * blocks
    inner = cv_ref.shape[1]
    heads = inner // HEAD
    own = cot_ref.shape[0]
    width = inner + 2 * HEAD
    for load in loads[:10]:
        load.wait()
    e = emb_ref[...].astype(F32)
    scale = lax.rsqrt(jnp.mean(e * e, axis=1, keepdims=True) + EPS)
    normed = (e * scale * ng_ref[...]).astype(BF16)
    normed = jnp.concatenate([normed, jnp.zeros((12, e.shape[1]), BF16)], axis=0)
    loads[10].wait()
    table_s = dot(normed, ws_ref[...])[0:4]
    if links is not None:
        links.met()
        links.send_tokens(tok_ref)
    loads[11].wait()
    table_d = dot(normed, wst_ref[...], 1, 1)[0:4]
    loads[12].wait()
    table_v = dot(normed, wv_ref[...])[0:4]
    loads[13].wait()
    table_z = dot(normed, wg_ref[...])[0:4]
    lane_h = iota((1, heads), 1)
    bias_row = jnp.zeros((1, heads), F32)
    rate_row = jnp.zeros((1, heads), F32)
    for h in range(heads):
        bias_row = jnp.where(lane_h == h, bias[h], bias_row)
        rate_row = jnp.where(lane_h == h, log_rate[h], rate_row)
    rate_row = jnp.exp(rate_row)
    pre_step = table_d + bias_row
    step_t = softplus(pre_step)
    sig_t = 1.0 / (1.0 + jnp.exp(-pre_step))
    ratio_t = jnp.where(step_t > 0.0, sig_t / step_t, 1.0)
    gate_t = silu(table_z)
    table_vs = jnp.concatenate([table_v, table_s], axis=1)
    taps = jnp.concatenate([cv_ref[...], cs_ref[...]], axis=1)
    none2 = jnp.zeros((4, 2 * heads), F32)
    rest = jnp.zeros((4, 128 - 3 * heads), F32)
    tail = jnp.concatenate(
        [
            gate_t,
            step_t, step_t, -rate_row * step_t, rest,
            none2, sig_t, rest,
            none2, ratio_t, rest,
        ],
        axis=1,
    )
    parts = []
    for k in range(CONV):
        last = tail if k == CONV - 1 else jnp.zeros_like(tail)
        parts.append(jnp.concatenate([table_vs * taps[k : k + 1], last], axis=1))
    per_tap = jnp.concatenate(parts, axis=0)
    p_hi = per_tap.astype(BF16)
    p_rest = per_tap - p_hi.astype(F32)
    p_mid = p_rest.astype(BF16)
    p_low = (p_rest - p_mid.astype(F32)).astype(BF16)
    per_tap3 = jnp.concatenate([p_hi, p_mid, p_low], axis=0)
    place_cols = width + inner

    column = iota((256, 48), 1) % 16
    index, tap = iota((256, 48), 0), column // 4
    digit = lax.shift_right_logical(index & 63, jnp.maximum(2 * (2 - tap), 0)) & 3
    digit = jnp.where(tap == 3, lax.shift_right_logical(index, 6), digit)
    kmer_hits = (digit == column % 4).astype(F32).astype(BF16)
    kmer_sum = dot(kmer_hits, per_tap3[:, : inner + HEAD])
    kmer_tail = dot(kmer_hits, per_tap3[:, place_cols:])
    kx = silu(kmer_sum[:, :inner])
    kb = silu(kmer_sum[:, inner:])
    kb_slope = silu_slope(kmer_sum[:, inner:])

    tri_in = (iota((own, own), 0) <= iota((own, own), 1)).astype(BF16)
    tri_out = (iota((own, own), 0) >= iota((own, own), 1)).astype(BF16)
    pad4 = jnp.zeros((12, own), BF16)

    def complement(v):
        out = jnp.full(v.shape, -1.0, F32)
        for a in range(4):
            out = jnp.where(v == a, rc[a].astype(F32), out)
        return out

    pair = tok_ref[...].astype(F32)
    mine = jnp.concatenate([pair[0:1], pair[1:2]], axis=1)
    mine_rc = complement(mine)
    letters = iota((4, own), 0).astype(F32)
    own_f = (jnp.broadcast_to(mine, (4, own)) == letters).astype(F32)
    own_r = (jnp.broadcast_to(mine_rc, (4, own)) == letters).astype(F32)
    n_f = dot(jnp.concatenate([own_f.astype(BF16), pad4], axis=0), tri_in)
    n_r = dot(jnp.concatenate([own_r.astype(BF16), pad4], axis=0), tri_out)

    def blend(weights, table, h):
        return sum(weights[a : a + 1] * table[a : a + 1, h : h + 1] for a in range(4))

    cum_rows, sig_rows, step_rows, ratio_rows = [], [], [], []
    for counted, hit in ((n_f, own_f), (n_r, own_r)):
        for h in range(heads):
            cum_rows.append(-(rate_row[:, h : h + 1] * blend(counted, step_t, h)))
            sig_rows.append(blend(counted, sig_t, h))
            step_rows.append(blend(hit, step_t, h))
            ratio_rows.append(blend(hit, ratio_t, h))
    cum8 = jnp.concatenate(cum_rows, axis=0)
    both = split(jnp.concatenate([cum8] + sig_rows, axis=0))
    side = jnp.concatenate([both[0], both[1]], axis=0)
    side = jnp.concatenate([side, side], axis=1)
    columns = jnp.transpose(
        jnp.concatenate([cum8, jnp.zeros((128 - 2 * heads, own), F32)], axis=0)
    )
    square = (iota((128, 128), 0), iota((128, 128), 1))
    causal = (square[0] >= square[1], square[0] <= square[1])
    for n in range(2 * heads):
        cum_c = jnp.broadcast_to(columns[:, n : n + 1], (own, 128))
        for rows, _ in live(n // heads):
            for half in range(own // 128):
                cols = slice(half * 128, half * 128 + 128)
                if (cols.start > rows.start) if n < heads else (cols.start < rows.start):
                    continue
                grown = jnp.exp(cum_c[rows] - cum_rows[n][:, cols])
                if cols.start == rows.start:
                    grown = jnp.where(causal[n // heads], grown, 0.0)
                decay_ref[n, rows, cols] = grown * step_rows[n][:, cols]
        part = slice((n % heads) * HEAD, (n % heads + 1) * HEAD)
        grow_ref[n // heads, :, part] = jnp.exp(cum_c)
    loads[14].wait()
    gain = hg_ref[...]
    dg_ref[...] = cot_ref[...].astype(F32) * (gain * loss_scale)

    if links is not None:
        links.pass_tokens(tok_ref)
        links.take_beside(tok_ref)
        earlier, later = links.near[0], links.near[1]
    else:
        earlier, later = (
            held[lax.rem(there, SIZES["z"]), there // SIZES["z"]]
            for there in (lax.rem(me + blocks - 1, blocks), lax.rem(me + 1, blocks))
        )
    earlier, later = earlier.astype(F32)[1:2], later.astype(F32)[0:1]
    earlier = jnp.where(me > 0, earlier, -1.0)
    later = jnp.where(me < blocks - 1, later, -1.0)
    line = jnp.concatenate([earlier, mine, later], axis=1)
    line = jnp.broadcast_to(line, (8, line.shape[1]))
    line_rc = complement(line)
    letters8 = iota((8, own), 0).astype(F32)
    f_hits, r_hits = [], []
    for k in range(CONV):
        d = CONV - 1 - k
        f_line = pltpu.roll(line, d, 1) if d else line
        r_line = pltpu.roll(line_rc, line.shape[1] - d, 1) if d else line_rc
        f_hits.append((f_line[:, 128 : 128 + own] == letters8)[0:4].astype(F32))
        r_hits.append((r_line[:, 128 : 128 + own] == letters8)[0:4].astype(F32))
    hits_t = [jnp.concatenate(f_hits, axis=0), jnp.concatenate(r_hits, axis=0)]
    slopes, c_parts, ct_parts, b_parts = [], [], [], []
    for strand in range(2):
        hits = jnp.concatenate([hits_t[strand]] * 3, axis=0).astype(BF16)
        summed = dot(hits, per_tap3[:, :place_cols], 0, 0)
        gate_ref[strand] = summed[:, width:]
        states = silu(summed[:, inner:width])
        slopes.append(silu_slope(summed[:, inner:width]))
        b_s = split(states[:, :HEAD])
        c_s = split(states[:, HEAD:])
        b_parts.append(b_s)
        c_parts.append(c_s)
        ct_parts.append(split(jnp.transpose(states[:, HEAD:])))
        scores = dot(lhs3(c_s), rhs3(b_s, 1), 1, 1)
        score_ref[strand] = scores
        for h in range(heads):
            part = slice(h * HEAD, (h + 1) * HEAD)
            x_h = silu(summed[:, part])
            x_s = split(x_h)
            xh_ref[strand, :, part] = x_s[0]
            xl_ref[strand, :, part] = x_s[1]
            mixing = [
                split(scores[rows, cols] * decay_ref[strand * heads + h, rows, cols])
                for rows, cols in live(strand)
            ]
            mixing = [filled([half[k] for half in mixing], strand) for k in range(2)]
            y_ref[strand, :, part] = dot(lhs3(mixing), rhs3(x_s)) + skip[h] * x_h

    if links is not None:
        links.take_tokens()
    for r in range(blocks):
        kmer_ref[2 * r : 2 * r + 2, :] = held[r % SIZES["z"], r // SIZES["z"]].astype(F32)
    tok = kmer_ref[...]
    comp = complement(tok)
    f_shift, r_shift = [tok], [comp]
    for _ in range(CONV - 1):
        f_shift.append(back_one(f_shift[-1], -1.0))
        r_shift.append(ahead_one(r_shift[-1], -1.0))

    row = iota(tok.shape, 0)
    position = row * 128 + iota(tok.shape, 1)
    before = row < 2 * me
    outside = before | (row >= 2 * me + 2)
    kmer_f = f_shift[1] + 4.0 * f_shift[2] + 16.0 * f_shift[3]
    kmer_r = r_shift[1] + 4.0 * r_shift[2] + 16.0 * r_shift[3]
    kmer = jnp.where(before, kmer_f, kmer_r)
    edge = (before & (position < CONV - 1)) | (position >= chunks * 128 - (CONV - 1))
    kmer_ref[...] = jnp.where(edge & outside, -1.0, kmer)
    mixed = jnp.where(outside, jnp.where(before, tok, comp), -1.0)
    last_ref[...] = mixed
    tri = (iota((128, 128), 0) <= iota((128, 128), 1)).astype(BF16)
    ones = jnp.ones((128, 128), BF16)
    strict = (iota((chunks, chunks), 1) < iota((chunks, chunks), 0)).astype(BF16)
    counts = []
    for a in range(4):
        hit = (mixed == a).astype(F32)
        hit16 = hit.astype(BF16)
        within = dot(hit16, tri)
        offset = dot(strict, dot(hit16, ones).astype(BF16))
        total_f = jnp.sum(jnp.where(before, hit, 0.0), keepdims=True)
        inclusive = within + offset - total_f
        counts.append(jnp.where(before, -inclusive, inclusive - hit))
    for h in range(heads):
        steps_sum = sum(counts[a] * step_t[a : a + 1, h : h + 1] for a in range(4))
        sig_sum = sum(counts[a] * sig_t[a : a + 1, h : h + 1] for a in range(4))
        exponent = -(rate_row[:, h : h + 1] * steps_sum)
        decay = jnp.where(outside, jnp.exp(exponent), 0.0)
        for q, value in enumerate((decay, decay * exponent, decay * sig_sum)):
            base = (q * heads + h) * chunks
            rows_ref[base : base + chunks, :] = value
    for q in range(3 * heads, 16):
        rows_ref[q * chunks : (q + 1) * chunks, :] = jnp.zeros((chunks, 128), F32)

    first_id = iota((64, 128), 0).astype(F32).astype(BF16)
    one16, zero16 = jnp.ones((64, 128), BF16), jnp.zeros((64, 128), BF16)
    nothing = jnp.zeros((32, 128), BF16)

    def load_rows(chunk):
        return rows_ref[pl.ds(chunk, 16, stride=chunks), :]

    acc_f = jnp.zeros((64, 128), F32)
    acc_r = jnp.zeros((64, 128), F32)
    for block in range(blocks):
        hits, weights = [], []
        for chunk in (2 * block, 2 * block + 1):
            w = jnp.concatenate(split(load_rows(chunk)), axis=0)
            final = jnp.broadcast_to(last_ref[chunk : chunk + 1, :], (32, 128)).astype(BF16)
            weights.append(
                jnp.concatenate([jnp.where(final == a, w, nothing) for a in range(4)], axis=0)
            )
            ids = jnp.broadcast_to(kmer_ref[chunk : chunk + 1, :], (64, 128)).astype(BF16)
            hits.append(jnp.where(ids == first_id, one16, zero16))
        found = dot(jnp.concatenate(hits, axis=1), jnp.concatenate(weights, axis=1), 1, 1)
        acc_r = acc_r + found
        acc_f = jnp.where(block == me, acc_r, acc_f)
        acc_r = jnp.where(block == me, 0.0, acc_r)
    lane = iota((16, 128), 1)
    e_f = split(jnp.where(lane < CONV - 1, load_rows(0), 0.0))
    e_r = split(jnp.where(lane >= 128 - (CONV - 1), load_rows(chunks - 1), 0.0))
    pick_row = iota((16, 128), 0)
    pick = (lane == jnp.where(pick_row < 8, pick_row, pick_row + 112)).astype(BF16)

    def by_row(acc, ends):
        parts = [acc] + [pltpu.roll(acc, 128 - 32 * a, 1) for a in range(1, 4)]
        ends = jnp.concatenate([ends[0], ends[1], jnp.zeros((96, 128), BF16)], axis=0)
        joined = jnp.concatenate(parts + [dot(pick, ends, 1, 1)], axis=0)
        return joined + pltpu.roll(joined, 128 - 16, 1)

    joined = (by_row(acc_f, e_f), by_row(acc_r, e_r))

    end_hits = []
    for k in range(CONV):
        d = CONV - 1 - k
        ends = jnp.where(
            iota((1, 128), 1) < 64, f_shift[d][0:1, :], r_shift[d][chunks - 1 : chunks, :]
        )
        end_hits.append(
            (jnp.broadcast_to(ends, (4, 128)) == iota((4, 128), 0).astype(F32)).astype(F32)
        )
    end_hits = jnp.concatenate(end_hits, axis=0).astype(BF16)
    end_pick = dot(end_hits, pick, 1, 1)
    end3 = jnp.concatenate([end_pick] * 3, axis=0).astype(BF16)
    end_sum = dot(end3, per_tap3, 0, 0)
    kx = jnp.concatenate([kx, silu(end_sum[:, :inner])], axis=0)
    kb = jnp.concatenate([kb, silu(end_sum[:, inner : inner + HEAD])], axis=0)
    kb_slope = jnp.concatenate([kb_slope, silu_slope(end_sum[:, inner : inner + HEAD])], axis=0)
    k_tail = jnp.concatenate([kmer_tail, end_sum[:, place_cols:]], axis=0)
    table_rows = kx.shape[0]

    lanes = iota((1, 128), 1)
    lane_rate = jnp.zeros((1, 128), F32)
    for h in range(heads):
        lane_rate = jnp.where(lanes == 2 * heads + h, -rate_row[:, h : h + 1], lane_rate)
    lane_one = jnp.where((lanes >= heads) & (lanes < 2 * heads), 1.0, lane_rate)
    weights, ratios, kxw_parts = [], [], []
    for strand in range(2):
        source = joined[strand]
        w = k_tail[:, 0:128] * source
        e4, e8 = pltpu.roll(source, heads, 1), pltpu.roll(source, 2 * heads, 1)
        decay = jnp.where((lanes >= heads) & (lanes < 2 * heads), e4, e8)
        kept = (decay > 0.0) & (lanes >= heads) & (lanes < 3 * heads)
        ratio = jnp.where(
            kept, lane_one * source / jnp.where(kept, decay, 1.0) + k_tail[:, 256:384], 0.0
        )
        ratio = jnp.concatenate(
            [ratio, jnp.zeros((384 - table_rows, 128), F32)], axis=0
        )
        ratio = split(jnp.transpose(ratio)[0:16, :table_rows])
        ratios.append(jnp.concatenate([ratio[0], ratio[1]], axis=0))
        for h in range(heads):
            part = slice(h * HEAD, (h + 1) * HEAD)
            kxw_ref[strand, :, part] = kx[:, part] * jnp.broadcast_to(
                w[:, h : h + 1], (table_rows, HEAD)
            )
        kxw_parts.append(split(kxw_ref[strand]))
    kb_t = jnp.concatenate([kb, jnp.zeros((384 - table_rows, HEAD), F32)], axis=0)
    kb_t = split(jnp.transpose(kb_t)[:, :table_rows])

    d_kb = [jnp.zeros(kb.shape, F32)]
    rate_grads = [jnp.zeros((1, 128), F32)] * heads
    bias_grads = [jnp.zeros((1, 128), F32)] * heads
    tap_sums = [jnp.zeros((16, 2 * HEAD), F32)]
    starts, d_scores, d_starts = [], [[None] * 2, [None] * 2], [None, None]
    for strand in range(2):
        kxw = kxw_parts[strand]
        start = dot(kb_t[0], kxw[0]) + (dot(kb_t[0], kxw[1]) + dot(kb_t[1], kxw[0]))
        starts.append(split(start))
        car_ref[strand] = dot(lhs3(c_parts[strand]), rhs3(starts[strand]))

    def head_pass(strand, h):
        n = strand * heads + h
        part = slice(h * HEAD, (h + 1) * HEAD)
        grow = grow_ref[strand, :, part]
        from_start = grow * car_ref[strand, :, part]
        gate = gate_ref[strand, :, part]
        gated = (y_ref[strand, :, part] + from_start) * gate
        inv = lax.rsqrt(jnp.mean(gated * gated, axis=1, keepdims=True) + EPS)
        normal = gated * inv
        out = normal * gain[:, part]
        if strand == 0:
            y_ref[0, :, part] = out
        else:
            enc_ref[:, part] = (y_ref[0, :, part] + out).astype(BF16)
        d_normal = dg_ref[:, part]
        d_y = d_normal - normal * jnp.mean(normal * d_normal, axis=1, keepdims=True)
        d_y = (d_y * inv) * gate
        x_s = (xh_ref[strand, :, part], xl_ref[strand, :, part])
        mixed_grad = dot(lhs3(split(d_y)), rhs3(x_s, 1), 1, 1)
        direct = d_y * from_start
        wsum, col_sums = [], []
        for half, (rows, cols) in enumerate(live(strand)):
            grad = mixed_grad[rows, cols] * decay_ref[n, rows, cols]
            d_scores[strand][half] = grad if h == 0 else d_scores[strand][half] + grad
            weighted = grad * score_ref[strand, rows, cols]
            wsum.append(split(fold(weighted) + direct[rows]))
            col_sums.append(jnp.sum(weighted, axis=0, keepdims=True))
        wsum = jnp.concatenate([wsum[0][0], wsum[1][0], wsum[0][1], wsum[1][1]], axis=0)
        moved = dot(side, wsum)
        if strand == 0:
            col_sum = col_sums[1] + jnp.concatenate(
                [col_sums[0], jnp.zeros((1, 128), F32)], axis=1
            )
        else:
            col_sum = col_sums[0] + jnp.concatenate(
                [jnp.zeros((1, 128), F32), col_sums[1]], axis=1
            )
        grown = split(d_y * grow)
        gh_ref[strand, :, part] = grown[0]
        gl_ref[strand, :, part] = grown[1]
        rate = rate_row[:, h : h + 1]
        rows = 2 * heads
        rate_grads[h] = (
            rate_grads[h]
            + (moved[n : n + 1] + moved[2 * rows + n : 2 * rows + n + 1])
            - fold(col_sum * cum_rows[n])
        )
        bias_grads[h] = (
            bias_grads[h]
            + fold(col_sum * (rate * sig_rows[n] + ratio_rows[n]))
            - rate * (moved[rows + n : rows + n + 1] + moved[3 * rows + n : 3 * rows + n + 1])
        )

    def state_pass(strand):
        grown = (gh_ref[strand], gl_ref[strand])
        d_starts[strand] = split(dot(lhs3(ct_parts[strand]), rhs3(grown)))

    def table_pass(strand):
        kxw, d_start = kxw_parts[strand], d_starts[strand]
        d_kb[0] = d_kb[0] + dot(lhs3(kxw), rhs3(d_start, 1), 1, 1)
        met = split(dot(lhs3(split(kb)), rhs3(d_start)) * kxw_ref[strand])
        slope = dot(ratios[strand], met[0]) + dot(ratios[strand], met[1])
        slope = slope[0:16] + slope[16:32]
        for h in range(heads):
            part = slice(h * HEAD, (h + 1) * HEAD)
            rate_grads[h] = rate_grads[h] + slope[heads + h : heads + h + 1, part]
            bias_grads[h] = bias_grads[h] + slope[2 * heads + h : 2 * heads + h + 1, part]

    def local_pass(strand):
        whole = filled(d_scores[strand], strand)
        d_scores_s = split(whole)
        d_c = dot(lhs3(d_scores_s), rhs3(b_parts[strand])) + dot(lhs3((gh_ref[strand], gl_ref[strand])), rhs3(starts[strand], 1), 1, 1)
        d_b = dot(lhs3(split(jnp.transpose(whole))), rhs3(c_parts[strand]))
        d_sum = split(jnp.concatenate([d_b, d_c], axis=1) * slopes[strand])
        hits = hits_t[strand].astype(BF16)
        tap_sums[0] = tap_sums[0] + dot(
            jnp.concatenate([hits, hits], axis=1), jnp.concatenate([d_sum[0], d_sum[1]], axis=0)
        )

    for h in range(heads):
        head_pass(0, h)
    state_pass(0)
    for h in range(heads):
        head_pass(1, h)
        if h == 0:
            table_pass(0)
    local_pass(0)
    state_pass(1)
    table_pass(1)
    local_pass(1)
    d_kb, tap_sums = d_kb[0], tap_sums[0]
    d_kb = split(d_kb * kb_slope)
    b_sums = dot(kmer_hits[:, 0:16], d_kb[0][0:256], 0, 0)
    b_sums = b_sums + dot(kmer_hits[:, 0:16], d_kb[1][0:256], 0, 0)
    end_pick = end_pick.astype(BF16)
    b_sums = b_sums + dot(end_pick, d_kb[0][256:]) + dot(end_pick, d_kb[1][256:])
    tap_sums = tap_sums + jnp.concatenate([b_sums, jnp.zeros_like(b_sums)], axis=1)
    conv_rows = []
    for k in range(CONV):
        conv_rows.append(
            jnp.sum(tap_sums[4 * k : 4 * k + 4] * table_s, axis=0, keepdims=True)
        )
    sums = jnp.sum(jnp.concatenate(rate_grads + bias_grads, axis=0), axis=1, keepdims=True)
    lane8 = iota((8, 128), 1)
    row8 = iota((8, 128), 0)
    last = jnp.zeros((8, 128), F32)
    head_total = 8 * heads
    for h in range(heads):
        at = slot * heads + h
        last = jnp.where((row8 == 0) & (lane8 == at), sums[h : h + 1], last)
        last = jnp.where(
            (row8 == 0) & (lane8 == head_total + at), sums[heads + h : heads + h + 1], last
        )
    conv = jnp.concatenate(conv_rows, axis=0)
    value = jnp.concatenate([conv[:, :128], conv[:, 128:], last[0:1]], axis=0)
    if links is not None:
        value = links.reduce(value)
    rate_ref[...] = value[8:9, 0:head_total]
    bias_ref[...] = value[8:9, head_total : 2 * head_total]
    conv_ref[...] = jnp.concatenate([value[0:4], value[4:8]], axis=1)
    if links is not None:
        links.drain()


def layer(args, place, loss_scale, everyone=None, interpret=False):
    (tokens, rc_map, embedding, norm_gain, w_values, w_gates, w_states, w_steps, conv_values,
     conv_states, step_bias, log_rate, skip_gain, head_gain, cotangent) = args
    own, inner = cotangent.shape
    all_heads = 8 * step_bias.shape[0]
    blocks = SIZES["x"] * SIZES["z"]
    chunks = 2 * blocks
    hbm = pl.BlockSpec(memory_space=pl.ANY)
    inputs = [
        tokens, rc_map, step_bias, log_rate, skip_gain, embedding, norm_gain.reshape(1, -1),
        conv_values, conv_states, head_gain.reshape(1, -1), w_states, w_steps.T, w_values, w_gates,
        cotangent,
    ]
    count = len(inputs)
    stores = [
        (pltpu.SMEM if 1 <= n <= 4 else pltpu.VMEM)(a.shape, a.dtype) for n, a in enumerate(inputs)
    ]
    scratch = [
        pltpu.VMEM((chunks, 128), F32),
        pltpu.VMEM((chunks, 128), F32),
        pltpu.VMEM((16 * chunks, 128), F32),
        pltpu.VMEM((8, own, own), F32),
        pltpu.SemaphoreType.DMA((count,)),
        pltpu.VMEM((2, own, inner), BF16),
        pltpu.VMEM((2, own, inner), BF16),
        pltpu.VMEM((2, own, inner), F32),
        pltpu.VMEM((2, own, inner), F32),
        pltpu.VMEM((2, own, inner), F32),
        pltpu.VMEM((own, inner), F32),
        pltpu.VMEM((2, own, own), F32),
        pltpu.VMEM((2, own, inner), BF16),
        pltpu.VMEM((2, own, inner), BF16),
        pltpu.VMEM((2, own, inner), F32),
        pltpu.VMEM((2, 256 + 16, inner), F32),
    ]
    slots = SIZES["c"] + SIZES["x"] * SIZES["y"] + SIZES["z"]
    remote = [
        pltpu.VMEM((SIZES["z"], SIZES["x"], 2, 128), jnp.int32),
        pltpu.VMEM((2, 2, 128), jnp.int32),
        pltpu.VMEM((slots, 9, 128), F32),
        pltpu.VMEM((3, 9, 128), F32),
        pltpu.SemaphoreType.DMA((12,)),
        pltpu.SemaphoreType.DMA((14,)),
        pltpu.SemaphoreType.DMA((slots,)),
        pltpu.SemaphoreType.DMA((slots,)),
    ]
    shapes = (
        pltpu.VMEM((own, inner), BF16),
        pltpu.VMEM((1, all_heads), F32),
        pltpu.VMEM((1, all_heads), F32),
        pltpu.VMEM((4, 256), F32),
    )
    alone = everyone is not None

    def body(*refs):
        refs = list(refs)
        sources, refs = refs[:count], refs[count:]
        if alone:
            links, held, refs = None, refs[0], refs[1:]
            out, refs = refs[:4], refs[4:]
        else:
            out, refs = refs[:4], refs[4:]
            links, held, refs = Links(refs[:8]), refs[0], refs[8:]
        layer_kernel(
            place, links, sources, *out, held, refs[:count], *refs[count:], loss_scale=loss_scale
        )

    if alone:
        params = pltpu.CompilerParams(vmem_limit_bytes=60 * 1024 * 1024)
    else:
        params = pltpu.CompilerParams(
            vmem_limit_bytes=60 * 1024 * 1024, collective_id=0, has_side_effects=True
        )
    return pl.pallas_call(
        body,
        out_shape=shapes,
        in_specs=[hbm] * count + [VM] * alone,
        out_specs=(VM,) * 4,
        scratch_shapes=([] if alone else remote) + stores + scratch,
        compiler_params=params,
        interpret=interpret,
        name="layer",
    )(*inputs, *([everyone] if alone else []))


def emit_kernel(*refs):
    count = len(refs) // 2
    rows = refs[0].shape[0] // 4
    pieces = [(refs[0].at[r : r + rows], refs[count].at[r : r + rows]) for r in range(0, 4 * rows, rows)]
    pieces += [(refs[n], refs[count + n]) for n in range(1, count)]
    copies = [
        pltpu.make_async_copy(source, target, refs[-1].at[n])
        for n, (source, target) in enumerate(pieces)
    ]
    for copy in copies:
        copy.start()
    for copy in copies:
        copy.wait()


def emit(results):
    hbm = pl.BlockSpec(memory_space=pl.ANY)
    return pl.pallas_call(
        emit_kernel,
        out_shape=tuple(jax.ShapeDtypeStruct(r.shape, r.dtype) for r in results),
        in_specs=[VM] * len(results),
        out_specs=(hbm,) * len(results),
        scratch_shapes=[pltpu.SemaphoreType.DMA((len(results) + 3,))],
        name="emit",
    )(*[pltpu.with_memory_space_constraint(r, pltpu.VMEM) for r in results])


def solution(mesh):
    count = mesh.shape["ctx"]

    def on_device(*args):
        own = args[-1].shape[0]
        loss_scale = 1.0 / math.sqrt(own * count * HEAD)

        def place():
            return lax.axis_index("ctx"), lax.axis_index("tp")

        results = layer((args[0].reshape(2, 128),) + args[1:], place, loss_scale)
        encoded, rate, bias, conv = emit(results)
        return encoded, rate.reshape(-1), bias.reshape(-1), conv

    tp = P("tp")
    cols = P(None, "tp")
    in_specs = (
        P("ctx"), P(), P(), P(), cols, cols, P(), cols, cols, P(), tp, tp, tp, tp, P("ctx", "tp"),
    )
    return jax.shard_map(
        on_device, mesh=mesh, in_specs=in_specs,
        out_specs=(P("ctx", "tp"), P(), P(), P()), check_vma=False,
    )
```

```python
import math

import jax
import jax.numpy as jnp
from jax import lax
from jax.experimental import pallas as pl
from jax.experimental.pallas import tpu as pltpu
from jax.sharding import PartitionSpec as P

F32 = jnp.float32
BF16 = jnp.bfloat16
HEAD = 128
CONV = 4
EPS = 1e-05
MESH = pl.DeviceIdType.MESH
VM = pl.BlockSpec(memory_space=pltpu.VMEM)


def split(v):
    hi = v.astype(BF16)
    return hi, (v - hi.astype(F32)).astype(BF16)


def dot(a, b, ca=1, cb=0):
    return lax.dot_general(a, b, (((ca,), (cb,)), ((), ())), preferred_element_type=F32)


def lhs3(v):
    hi, lo = v
    return jnp.concatenate([hi, lo, hi], axis=1)


def rhs3(v, axis=0):
    hi, lo = v
    return jnp.concatenate([hi, hi, lo], axis=axis)


def silu(v):
    return v / (1.0 + jnp.exp(-v))


def silu_slope(v):
    s = 1.0 / (1.0 + jnp.exp(-v))
    return s + v * s * (1.0 - s)


def fold(v):
    return v[:, :128] + v[:, 128:] if v.shape[1] > 128 else v


def live(strand):
    if strand == 0:
        return ((slice(0, 128), slice(0, 128)), (slice(128, 256), slice(0, 256)))
    return ((slice(0, 128), slice(0, 256)), (slice(128, 256), slice(128, 256)))


def filled(halves, strand):
    zero = jnp.zeros((128, 128), halves[0].dtype)
    if strand == 0:
        return jnp.concatenate(
            [jnp.concatenate([halves[0], zero], axis=1), halves[1]], axis=0
        )
    return jnp.concatenate([halves[0], jnp.concatenate([zero, halves[1]], axis=1)], axis=0)


def iota(shape, dim):
    return lax.broadcasted_iota(jnp.int32, shape, dim)


def back_one(v, fill):
    rolled = pltpu.roll(v, 1, 1)
    wrapped = pltpu.roll(rolled, 1, 0)
    moved = jnp.where(iota(v.shape, 1) == 0, wrapped, rolled)
    first = (iota(v.shape, 0) == 0) & (iota(v.shape, 1) == 0)
    return jnp.where(first, fill, moved)


def ahead_one(v, fill):
    rows, lanes = v.shape
    rolled = pltpu.roll(v, lanes - 1, 1)
    wrapped = pltpu.roll(rolled, rows - 1, 0)
    moved = jnp.where(iota(v.shape, 1) == lanes - 1, wrapped, rolled)
    last = (iota(v.shape, 0) == rows - 1) & (iota(v.shape, 1) == lanes - 1)
    return jnp.where(last, fill, moved)


def softplus(v):
    return jnp.maximum(v, 0.0) + jnp.log1p(jnp.exp(-jnp.abs(v)))


SIZES = {"x": 4, "z": 8, "y": 4, "c": 2}


def offsets(axes):
    steps = [()]
    for axis in axes:
        steps = [step + (d,) for step in steps for d in range(SIZES[axis])]

    def hops(step):
        return sum(min(d, SIZES[axis] - d) for axis, d in zip(axes, step) if axis != "c")

    return sorted(steps[1:], key=lambda step: -hops(step))


class Links:
    def __init__(self, refs):
        (self.held, self.near, self.slots, self.sent, self.tok_send, self.tok_recv,
         self.sum_send, self.sum_recv) = refs
        ctx, tp = lax.axis_index("ctx"), lax.axis_index("tp")
        self.ctx = ctx
        self.here = {
            "x": ctx // SIZES["z"], "z": lax.rem(ctx, SIZES["z"]),
            "y": tp // SIZES["c"], "c": lax.rem(tp, SIZES["c"]),
        }
        self.drains = []

    def moved(self, axes, step):
        there = dict(self.here)
        for axis, d in zip(axes, step):
            if d:
                there[axis] = lax.rem(there[axis] + d, SIZES[axis])
        return there

    def device(self, there):
        return {
            "ctx": there["x"] * SIZES["z"] + there["z"], "tp": there["y"] * SIZES["c"] + there["c"]
        }

    def beside(self, d):
        count = SIZES["x"] * SIZES["z"]
        return {"ctx": lax.rem(self.ctx + d % count, count)}

    def greet(self):
        barrier = pltpu.get_barrier_semaphore()
        devices = [self.device(self.moved("z", step)) for step in offsets("z")]
        devices += [self.device(self.moved("x", step)) for step in offsets("x")]
        devices += [self.beside(1), self.beside(-1)]
        devices += [self.device(self.moved("xy", step)) for step in offsets("xy") if step[1]]
        devices += [self.device(self.moved("c", step)) for step in offsets("c")]
        for device in devices:
            pl.semaphore_signal(barrier, inc=1, device_id=device, device_id_type=MESH)
        self.greeted = len(devices)

    def met(self):
        pl.semaphore_wait(pltpu.get_barrier_semaphore(), self.greeted)

    def token_copy(self, source, target, number, arrives, device):
        return pltpu.make_async_remote_copy(
            src_ref=source, dst_ref=target, send_sem=self.tok_send.at[number],
            recv_sem=self.tok_recv.at[arrives], device_id=device, device_id_type=MESH,
        )

    def send(self, copy):
        copy.start()
        self.drains.append(copy)

    def send_tokens(self, tok_ref):
        x, z = self.here["x"], self.here["z"]
        own = self.held.at[z, x]
        for k, step in enumerate(offsets("x")):
            self.send(self.token_copy(tok_ref, own, k, x, self.device(self.moved("x", step))))
        for k, d in ((3, 1), (4, -1)):
            near = self.near.at[k - 3]
            self.send(self.token_copy(tok_ref, near, k, 9 + k, self.beside(d)))
        self.held[z, x] = tok_ref[...]

    def pass_tokens(self, tok_ref):
        x, z = self.here["x"], self.here["z"]
        for step in reversed(offsets("x")):
            there = self.moved("x", step)
            self.token_copy(
                tok_ref, self.held.at[z, there["x"]], 0, there["x"], self.device(there)
            ).wait_recv()
        row = self.held.at[z]
        for k, step in enumerate(offsets("z")):
            there = self.moved("z", step)
            self.send(self.token_copy(row, row, 5 + k, 4 + z, self.device(there)))

    def take_beside(self, tok_ref):
        for k, d in ((3, 1), (4, -1)):
            self.token_copy(tok_ref, self.near.at[k - 3], k, 9 + k, self.beside(d)).wait_recv()

    def take_tokens(self):
        for step in reversed(offsets("z")):
            there = self.moved("z", step)
            row = self.held.at[there["z"]]
            self.token_copy(row, row, 5, 4 + there["z"], self.device(there)).wait_recv()

    def reduce(self, value):
        base = 0
        for number, axes in enumerate(("c", "xy", "z")):
            self.sent[number] = value
            steps = offsets(axes)
            sending = []

            def slot(there):
                place = 0
                for axis in axes:
                    place = place * SIZES[axis] + there[axis]
                return base + place

            def copy(k, there, place):
                return pltpu.make_async_remote_copy(
                    src_ref=self.sent.at[number],
                    dst_ref=self.slots.at[place],
                    send_sem=self.sum_send.at[base + k],
                    recv_sem=self.sum_recv.at[place],
                    device_id=self.device(there),
                    device_id_type=MESH,
                )

            for k, step in enumerate(steps):
                sending.append(copy(k, self.moved(axes, step), slot(self.here)))
                sending[-1].start()
            self.drain()
            self.drains = sending
            self.slots[slot(self.here)] = value
            for step in reversed(steps):
                there = self.moved(axes, step)
                copy(0, there, slot(there)).wait_recv()
            value = self.slots[base]
            for i in range(1, len(steps) + 1):
                value = value + self.slots[base + i]
            base += len(steps) + 1
        return value

    def drain(self):
        for copy in self.drains:
            copy.wait_send()


def layer_kernel(
    place, links, sources, enc_ref, rate_ref, bias_ref, conv_ref, held, stores, kmer_ref, last_ref, rows_ref, decay_ref, load_sem,
    xh_ref, xl_ref, y_ref, gate_ref, grow_ref, dg_ref, score_ref, gh_ref, gl_ref, car_ref, kxw_ref,
    *, loss_scale,
):
    if links is not None:
        links.greet()
    loads = [
        pltpu.make_async_copy(source, store, load_sem.at[n])
        for n, (source, store) in enumerate(zip(sources, stores))
    ]
    for load in loads:
        load.start()
    (tok_ref, rc, bias, log_rate, skip, emb_ref, ng_ref, cv_ref, cs_ref, hg_ref, ws_ref, wst_ref,
     wv_ref, wg_ref, cot_ref) = stores
    me, slot = place()
    blocks = SIZES["x"] * SIZES["z"]
    chunks = 2 * blocks
    inner = cv_ref.shape[1]
    heads = inner // HEAD
    own = cot_ref.shape[0]
    width = inner + 2 * HEAD
    for load in loads[:10]:
        load.wait()
    e = emb_ref[...].astype(F32)
    scale = lax.rsqrt(jnp.mean(e * e, axis=1, keepdims=True) + EPS)
    normed = (e * scale * ng_ref[...]).astype(BF16)
    normed = jnp.concatenate([normed, jnp.zeros((12, e.shape[1]), BF16)], axis=0)
    loads[10].wait()
    table_s = dot(normed, ws_ref[...])[0:4]
    if links is not None:
        links.met()
        links.send_tokens(tok_ref)
    loads[11].wait()
    table_d = dot(normed, wst_ref[...], 1, 1)[0:4]
    loads[12].wait()
    table_v = dot(normed, wv_ref[...])[0:4]
    loads[13].wait()
    table_z = dot(normed, wg_ref[...])[0:4]
    lane_h = iota((1, heads), 1)
    bias_row = jnp.zeros((1, heads), F32)
    rate_row = jnp.zeros((1, heads), F32)
    for h in range(heads):
        bias_row = jnp.where(lane_h == h, bias[h], bias_row)
        rate_row = jnp.where(lane_h == h, log_rate[h], rate_row)
    rate_row = jnp.exp(rate_row)
    pre_step = table_d + bias_row
    step_t = softplus(pre_step)
    sig_t = 1.0 / (1.0 + jnp.exp(-pre_step))
    ratio_t = jnp.where(step_t > 0.0, sig_t / step_t, 1.0)
    gate_t = silu(table_z)
    table_vs = jnp.concatenate([table_v, table_s], axis=1)
    taps = jnp.concatenate([cv_ref[...], cs_ref[...]], axis=1)
    none2 = jnp.zeros((4, 2 * heads), F32)
    rest = jnp.zeros((4, 128 - 3 * heads), F32)
    tail = jnp.concatenate(
        [
            gate_t,
            step_t, step_t, -rate_row * step_t, rest,
            none2, sig_t, rest,
            none2, ratio_t, rest,
        ],
        axis=1,
    )
    parts = []
    for k in range(CONV):
        last = tail if k == CONV - 1 else jnp.zeros_like(tail)
        parts.append(jnp.concatenate([table_vs * taps[k : k + 1], last], axis=1))
    per_tap = jnp.concatenate(parts, axis=0)
    p_hi = per_tap.astype(BF16)
    p_rest = per_tap - p_hi.astype(F32)
    p_mid = p_rest.astype(BF16)
    p_low = (p_rest - p_mid.astype(F32)).astype(BF16)
    per_tap3 = jnp.concatenate([p_hi, p_mid, p_low], axis=0)
    place_cols = width + inner

    column = iota((256, 48), 1) % 16
    index, tap = iota((256, 48), 0), column // 4
    digit = lax.shift_right_logical(index & 63, jnp.maximum(2 * (2 - tap), 0)) & 3
    digit = jnp.where(tap == 3, lax.shift_right_logical(index, 6), digit)
    kmer_hits = (digit == column % 4).astype(F32).astype(BF16)
    kmer_sum = dot(kmer_hits, per_tap3[:, : inner + HEAD])
    kmer_tail = dot(kmer_hits, per_tap3[:, place_cols:])
    kx = silu(kmer_sum[:, :inner])
    kb = silu(kmer_sum[:, inner:])
    kb_slope = silu_slope(kmer_sum[:, inner:])

    tri_in = (iota((own, own), 0) <= iota((own, own), 1)).astype(BF16)
    tri_out = (iota((own, own), 0) >= iota((own, own), 1)).astype(BF16)
    pad4 = jnp.zeros((12, own), BF16)

    def complement(v):
        out = jnp.full(v.shape, -1.0, F32)
        for a in range(4):
            out = jnp.where(v == a, rc[a].astype(F32), out)
        return out

    pair = tok_ref[...].astype(F32)
    mine = jnp.concatenate([pair[0:1], pair[1:2]], axis=1)
    mine_rc = complement(mine)
    letters = iota((4, own), 0).astype(F32)
    own_f = (jnp.broadcast_to(mine, (4, own)) == letters).astype(F32)
    own_r = (jnp.broadcast_to(mine_rc, (4, own)) == letters).astype(F32)
    n_f = dot(jnp.concatenate([own_f.astype(BF16), pad4], axis=0), tri_in)
    n_r = dot(jnp.concatenate([own_r.astype(BF16), pad4], axis=0), tri_out)

    def blend(weights, table, h):
        return sum(weights[a : a + 1] * table[a : a + 1, h : h + 1] for a in range(4))

    cum_rows, sig_rows, step_rows, ratio_rows = [], [], [], []
    for counted, hit in ((n_f, own_f), (n_r, own_r)):
        for h in range(heads):
            cum_rows.append(-(rate_row[:, h : h + 1] * blend(counted, step_t, h)))
            sig_rows.append(blend(counted, sig_t, h))
            step_rows.append(blend(hit, step_t, h))
            ratio_rows.append(blend(hit, ratio_t, h))
    cum8 = jnp.concatenate(cum_rows, axis=0)
    both = split(jnp.concatenate([cum8] + sig_rows, axis=0))
    side = jnp.concatenate([both[0], both[1]], axis=0)
    side = jnp.concatenate([side, side], axis=1)
    columns = jnp.transpose(
        jnp.concatenate([cum8, jnp.zeros((128 - 2 * heads, own), F32)], axis=0)
    )
    square = (iota((128, 128), 0), iota((128, 128), 1))
    causal = (square[0] >= square[1], square[0] <= square[1])
    if links is not None:
        links.pass_tokens(tok_ref)
    for n in range(2 * heads):
        cum_c = jnp.broadcast_to(columns[:, n : n + 1], (own, 128))
        for rows, _ in live(n // heads):
            for half in range(own // 128):
                cols = slice(half * 128, half * 128 + 128)
                if (cols.start > rows.start) if n < heads else (cols.start < rows.start):
                    continue
                grown = jnp.exp(cum_c[rows] - cum_rows[n][:, cols])
                if cols.start == rows.start:
                    grown = jnp.where(causal[n // heads], grown, 0.0)
                decay_ref[n, rows, cols] = grown * step_rows[n][:, cols]
        part = slice((n % heads) * HEAD, (n % heads + 1) * HEAD)
        grow_ref[n // heads, :, part] = jnp.exp(cum_c)
    loads[14].wait()
    gain = hg_ref[...]
    dg_ref[...] = cot_ref[...].astype(F32) * (gain * loss_scale)

    if links is not None:
        links.take_beside(tok_ref)
        earlier, later = links.near[0], links.near[1]
    else:
        earlier, later = (
            held[lax.rem(there, SIZES["z"]), there // SIZES["z"]]
            for there in (lax.rem(me + blocks - 1, blocks), lax.rem(me + 1, blocks))
        )
    earlier, later = earlier.astype(F32)[1:2], later.astype(F32)[0:1]
    earlier = jnp.where(me > 0, earlier, -1.0)
    later = jnp.where(me < blocks - 1, later, -1.0)
    line = jnp.concatenate([earlier, mine, later], axis=1)
    line = jnp.broadcast_to(line, (8, line.shape[1]))
    line_rc = complement(line)
    letters8 = iota((8, own), 0).astype(F32)
    f_hits, r_hits = [], []
    for k in range(CONV):
        d = CONV - 1 - k
        f_line = pltpu.roll(line, d, 1) if d else line
        r_line = pltpu.roll(line_rc, line.shape[1] - d, 1) if d else line_rc
        f_hits.append((f_line[:, 128 : 128 + own] == letters8)[0:4].astype(F32))
        r_hits.append((r_line[:, 128 : 128 + own] == letters8)[0:4].astype(F32))
    hits_t = [jnp.concatenate(f_hits, axis=0), jnp.concatenate(r_hits, axis=0)]
    slopes, c_parts, ct_parts, b_parts = [], [], [], []
    for strand in range(2):
        hits = jnp.concatenate([hits_t[strand]] * 3, axis=0).astype(BF16)
        summed = dot(hits, per_tap3[:, :place_cols], 0, 0)
        gate_ref[strand] = summed[:, width:]
        states = silu(summed[:, inner:width])
        slopes.append(silu_slope(summed[:, inner:width]))
        b_s = split(states[:, :HEAD])
        c_s = split(states[:, HEAD:])
        b_parts.append(b_s)
        c_parts.append(c_s)
        ct_parts.append(split(jnp.transpose(states[:, HEAD:])))
        scores = dot(lhs3(c_s), rhs3(b_s, 1), 1, 1)
        score_ref[strand] = scores
        for h in range(heads):
            part = slice(h * HEAD, (h + 1) * HEAD)
            x_h = silu(summed[:, part])
            x_s = split(x_h)
            xh_ref[strand, :, part] = x_s[0]
            xl_ref[strand, :, part] = x_s[1]
            mixing = [
                split(scores[rows, cols] * decay_ref[strand * heads + h, rows, cols])
                for rows, cols in live(strand)
            ]
            mixing = [filled([half[k] for half in mixing], strand) for k in range(2)]
            y_ref[strand, :, part] = dot(lhs3(mixing), rhs3(x_s)) + skip[h] * x_h

    if links is not None:
        links.take_tokens()
    for r in range(blocks):
        kmer_ref[2 * r : 2 * r + 2, :] = held[r % SIZES["z"], r // SIZES["z"]].astype(F32)
    tok = kmer_ref[...]
    comp = complement(tok)
    f_shift, r_shift = [tok], [comp]
    for _ in range(CONV - 1):
        f_shift.append(back_one(f_shift[-1], -1.0))
        r_shift.append(ahead_one(r_shift[-1], -1.0))

    row = iota(tok.shape, 0)
    position = row * 128 + iota(tok.shape, 1)
    before = row < 2 * me
    outside = before | (row >= 2 * me + 2)
    kmer_f = f_shift[1] + 4.0 * f_shift[2] + 16.0 * f_shift[3]
    kmer_r = r_shift[1] + 4.0 * r_shift[2] + 16.0 * r_shift[3]
    kmer = jnp.where(before, kmer_f, kmer_r)
    edge = (before & (position < CONV - 1)) | (position >= chunks * 128 - (CONV - 1))
    kmer_ref[...] = jnp.where(edge & outside, -1.0, kmer)
    mixed = jnp.where(outside, jnp.where(before, tok, comp), -1.0)
    last_ref[...] = mixed
    tri = (iota((128, 128), 0) <= iota((128, 128), 1)).astype(BF16)
    ones = jnp.ones((128, 128), BF16)
    strict = (iota((chunks, chunks), 1) < iota((chunks, chunks), 0)).astype(BF16)
    counts = []
    for a in range(4):
        hit = (mixed == a).astype(F32)
        hit16 = hit.astype(BF16)
        within = dot(hit16, tri)
        offset = dot(strict, dot(hit16, ones).astype(BF16))
        total_f = jnp.sum(jnp.where(before, hit, 0.0), keepdims=True)
        inclusive = within + offset - total_f
        counts.append(jnp.where(before, -inclusive, inclusive - hit))
    for h in range(heads):
        steps_sum = sum(counts[a] * step_t[a : a + 1, h : h + 1] for a in range(4))
        sig_sum = sum(counts[a] * sig_t[a : a + 1, h : h + 1] for a in range(4))
        exponent = -(rate_row[:, h : h + 1] * steps_sum)
        decay = jnp.where(outside, jnp.exp(exponent), 0.0)
        for q, value in enumerate((decay, decay * exponent, decay * sig_sum)):
            base = (q * heads + h) * chunks
            rows_ref[base : base + chunks, :] = value
    for q in range(3 * heads, 16):
        rows_ref[q * chunks : (q + 1) * chunks, :] = jnp.zeros((chunks, 128), F32)

    first_id = iota((64, 128), 0).astype(F32).astype(BF16)
    one16, zero16 = jnp.ones((64, 128), BF16), jnp.zeros((64, 128), BF16)
    nothing = jnp.zeros((32, 128), BF16)

    def load_rows(chunk):
        return rows_ref[pl.ds(chunk, 16, stride=chunks), :]

    acc_f = jnp.zeros((64, 128), F32)
    acc_r = jnp.zeros((64, 128), F32)
    for block in range(blocks):
        hits, weights = [], []
        for chunk in (2 * block, 2 * block + 1):
            w = jnp.concatenate(split(load_rows(chunk)), axis=0)
            final = jnp.broadcast_to(last_ref[chunk : chunk + 1, :], (32, 128)).astype(BF16)
            weights.append(
                jnp.concatenate([jnp.where(final == a, w, nothing) for a in range(4)], axis=0)
            )
            ids = jnp.broadcast_to(kmer_ref[chunk : chunk + 1, :], (64, 128)).astype(BF16)
            hits.append(jnp.where(ids == first_id, one16, zero16))
        found = dot(jnp.concatenate(hits, axis=1), jnp.concatenate(weights, axis=1), 1, 1)
        acc_r = acc_r + found
        acc_f = jnp.where(block == me, acc_r, acc_f)
        acc_r = jnp.where(block == me, 0.0, acc_r)
    lane = iota((16, 128), 1)
    e_f = split(jnp.where(lane < CONV - 1, load_rows(0), 0.0))
    e_r = split(jnp.where(lane >= 128 - (CONV - 1), load_rows(chunks - 1), 0.0))
    pick_row = iota((16, 128), 0)
    pick = (lane == jnp.where(pick_row < 8, pick_row, pick_row + 112)).astype(BF16)

    def by_row(acc, ends):
        parts = [acc] + [pltpu.roll(acc, 128 - 32 * a, 1) for a in range(1, 4)]
        ends = jnp.concatenate([ends[0], ends[1], jnp.zeros((96, 128), BF16)], axis=0)
        joined = jnp.concatenate(parts + [dot(pick, ends, 1, 1)], axis=0)
        return joined + pltpu.roll(joined, 128 - 16, 1)

    joined = (by_row(acc_f, e_f), by_row(acc_r, e_r))

    end_hits = []
    for k in range(CONV):
        d = CONV - 1 - k
        ends = jnp.where(
            iota((1, 128), 1) < 64, f_shift[d][0:1, :], r_shift[d][chunks - 1 : chunks, :]
        )
        end_hits.append(
            (jnp.broadcast_to(ends, (4, 128)) == iota((4, 128), 0).astype(F32)).astype(F32)
        )
    end_hits = jnp.concatenate(end_hits, axis=0).astype(BF16)
    end_pick = dot(end_hits, pick, 1, 1)
    end3 = jnp.concatenate([end_pick] * 3, axis=0).astype(BF16)
    end_sum = dot(end3, per_tap3, 0, 0)
    kx = jnp.concatenate([kx, silu(end_sum[:, :inner])], axis=0)
    kb = jnp.concatenate([kb, silu(end_sum[:, inner : inner + HEAD])], axis=0)
    kb_slope = jnp.concatenate([kb_slope, silu_slope(end_sum[:, inner : inner + HEAD])], axis=0)
    k_tail = jnp.concatenate([kmer_tail, end_sum[:, place_cols:]], axis=0)
    table_rows = kx.shape[0]

    lanes = iota((1, 128), 1)
    lane_rate = jnp.zeros((1, 128), F32)
    for h in range(heads):
        lane_rate = jnp.where(lanes == 2 * heads + h, -rate_row[:, h : h + 1], lane_rate)
    lane_one = jnp.where((lanes >= heads) & (lanes < 2 * heads), 1.0, lane_rate)
    weights, ratios, kxw_parts = [], [], []
    for strand in range(2):
        source = joined[strand]
        w = k_tail[:, 0:128] * source
        e4, e8 = pltpu.roll(source, heads, 1), pltpu.roll(source, 2 * heads, 1)
        decay = jnp.where((lanes >= heads) & (lanes < 2 * heads), e4, e8)
        kept = (decay > 0.0) & (lanes >= heads) & (lanes < 3 * heads)
        ratio = jnp.where(
            kept, lane_one * source / jnp.where(kept, decay, 1.0) + k_tail[:, 256:384], 0.0
        )
        ratio = jnp.concatenate(
            [ratio, jnp.zeros((384 - table_rows, 128), F32)], axis=0
        )
        ratio = split(jnp.transpose(ratio)[0:16, :table_rows])
        ratios.append(jnp.concatenate([ratio[0], ratio[1]], axis=0))
        for h in range(heads):
            part = slice(h * HEAD, (h + 1) * HEAD)
            kxw_ref[strand, :, part] = kx[:, part] * jnp.broadcast_to(
                w[:, h : h + 1], (table_rows, HEAD)
            )
        kxw_parts.append(split(kxw_ref[strand]))
    kb_t = jnp.concatenate([kb, jnp.zeros((384 - table_rows, HEAD), F32)], axis=0)
    kb_t = split(jnp.transpose(kb_t)[:, :table_rows])

    d_kb = [jnp.zeros(kb.shape, F32)]
    rate_grads = [jnp.zeros((1, 128), F32)] * heads
    bias_grads = [jnp.zeros((1, 128), F32)] * heads
    tap_sums = [jnp.zeros((16, 2 * HEAD), F32)]
    starts, d_scores, d_starts = [], [[None] * 2, [None] * 2], [None, None]
    for strand in range(2):
        kxw = kxw_parts[strand]
        start = dot(kb_t[0], kxw[0]) + (dot(kb_t[0], kxw[1]) + dot(kb_t[1], kxw[0]))
        starts.append(split(start))
        car_ref[strand] = dot(lhs3(c_parts[strand]), rhs3(starts[strand]))

    def head_pass(strand, h):
        n = strand * heads + h
        part = slice(h * HEAD, (h + 1) * HEAD)
        grow = grow_ref[strand, :, part]
        from_start = grow * car_ref[strand, :, part]
        gate = gate_ref[strand, :, part]
        gated = (y_ref[strand, :, part] + from_start) * gate
        inv = lax.rsqrt(jnp.mean(gated * gated, axis=1, keepdims=True) + EPS)
        normal = gated * inv
        out = normal * gain[:, part]
        if strand == 0:
            y_ref[0, :, part] = out
        else:
            enc_ref[:, part] = (y_ref[0, :, part] + out).astype(BF16)
        d_normal = dg_ref[:, part]
        d_y = d_normal - normal * jnp.mean(normal * d_normal, axis=1, keepdims=True)
        d_y = (d_y * inv) * gate
        x_s = (xh_ref[strand, :, part], xl_ref[strand, :, part])
        mixed_grad = dot(lhs3(split(d_y)), rhs3(x_s, 1), 1, 1)
        direct = d_y * from_start
        wsum, col_sums = [], []
        for half, (rows, cols) in enumerate(live(strand)):
            grad = mixed_grad[rows, cols] * decay_ref[n, rows, cols]
            d_scores[strand][half] = grad if h == 0 else d_scores[strand][half] + grad
            weighted = grad * score_ref[strand, rows, cols]
            wsum.append(split(fold(weighted) + direct[rows]))
            col_sums.append(jnp.sum(weighted, axis=0, keepdims=True))
        wsum = jnp.concatenate([wsum[0][0], wsum[1][0], wsum[0][1], wsum[1][1]], axis=0)
        moved = dot(side, wsum)
        if strand == 0:
            col_sum = col_sums[1] + jnp.concatenate(
                [col_sums[0], jnp.zeros((1, 128), F32)], axis=1
            )
        else:
            col_sum = col_sums[0] + jnp.concatenate(
                [jnp.zeros((1, 128), F32), col_sums[1]], axis=1
            )
        grown = split(d_y * grow)
        gh_ref[strand, :, part] = grown[0]
        gl_ref[strand, :, part] = grown[1]
        rate = rate_row[:, h : h + 1]
        rows = 2 * heads
        rate_grads[h] = (
            rate_grads[h]
            + (moved[n : n + 1] + moved[2 * rows + n : 2 * rows + n + 1])
            - fold(col_sum * cum_rows[n])
        )
        bias_grads[h] = (
            bias_grads[h]
            + fold(col_sum * (rate * sig_rows[n] + ratio_rows[n]))
            - rate * (moved[rows + n : rows + n + 1] + moved[3 * rows + n : 3 * rows + n + 1])
        )

    def state_pass(strand):
        grown = (gh_ref[strand], gl_ref[strand])
        d_starts[strand] = split(dot(lhs3(ct_parts[strand]), rhs3(grown)))

    def table_pass(strand):
        kxw, d_start = kxw_parts[strand], d_starts[strand]
        d_kb[0] = d_kb[0] + dot(lhs3(kxw), rhs3(d_start, 1), 1, 1)
        met = split(dot(lhs3(split(kb)), rhs3(d_start)) * kxw_ref[strand])
        slope = dot(ratios[strand], met[0]) + dot(ratios[strand], met[1])
        slope = slope[0:16] + slope[16:32]
        for h in range(heads):
            part = slice(h * HEAD, (h + 1) * HEAD)
            rate_grads[h] = rate_grads[h] + slope[heads + h : heads + h + 1, part]
            bias_grads[h] = bias_grads[h] + slope[2 * heads + h : 2 * heads + h + 1, part]

    def local_pass(strand):
        whole = filled(d_scores[strand], strand)
        d_scores_s = split(whole)
        d_c = dot(lhs3(d_scores_s), rhs3(b_parts[strand])) + dot(lhs3((gh_ref[strand], gl_ref[strand])), rhs3(starts[strand], 1), 1, 1)
        d_b = dot(lhs3(split(jnp.transpose(whole))), rhs3(c_parts[strand]))
        d_sum = split(jnp.concatenate([d_b, d_c], axis=1) * slopes[strand])
        hits = hits_t[strand].astype(BF16)
        tap_sums[0] = tap_sums[0] + dot(
            jnp.concatenate([hits, hits], axis=1), jnp.concatenate([d_sum[0], d_sum[1]], axis=0)
        )

    for h in range(heads):
        head_pass(0, h)
    state_pass(0)
    for h in range(heads):
        head_pass(1, h)
        if h == 0:
            table_pass(0)
    local_pass(0)
    state_pass(1)
    table_pass(1)
    local_pass(1)
    d_kb, tap_sums = d_kb[0], tap_sums[0]
    d_kb = split(d_kb * kb_slope)
    b_sums = dot(kmer_hits[:, 0:16], d_kb[0][0:256], 0, 0)
    b_sums = b_sums + dot(kmer_hits[:, 0:16], d_kb[1][0:256], 0, 0)
    end_pick = end_pick.astype(BF16)
    b_sums = b_sums + dot(end_pick, d_kb[0][256:]) + dot(end_pick, d_kb[1][256:])
    tap_sums = tap_sums + jnp.concatenate([b_sums, jnp.zeros_like(b_sums)], axis=1)
    conv_rows = []
    for k in range(CONV):
        conv_rows.append(
            jnp.sum(tap_sums[4 * k : 4 * k + 4] * table_s, axis=0, keepdims=True)
        )
    sums = jnp.sum(jnp.concatenate(rate_grads + bias_grads, axis=0), axis=1, keepdims=True)
    lane8 = iota((8, 128), 1)
    row8 = iota((8, 128), 0)
    last = jnp.zeros((8, 128), F32)
    head_total = 8 * heads
    for h in range(heads):
        at = slot * heads + h
        last = jnp.where((row8 == 0) & (lane8 == at), sums[h : h + 1], last)
        last = jnp.where(
            (row8 == 0) & (lane8 == head_total + at), sums[heads + h : heads + h + 1], last
        )
    conv = jnp.concatenate(conv_rows, axis=0)
    value = jnp.concatenate([conv[:, :128], conv[:, 128:], last[0:1]], axis=0)
    if links is not None:
        value = links.reduce(value)
    rate_ref[...] = value[8:9, 0:head_total]
    bias_ref[...] = value[8:9, head_total : 2 * head_total]
    conv_ref[...] = jnp.concatenate([value[0:4], value[4:8]], axis=1)
    if links is not None:
        links.drain()


def layer(args, place, loss_scale, everyone=None, interpret=False):
    (tokens, rc_map, embedding, norm_gain, w_values, w_gates, w_states, w_steps, conv_values,
     conv_states, step_bias, log_rate, skip_gain, head_gain, cotangent) = args
    own, inner = cotangent.shape
    all_heads = 8 * step_bias.shape[0]
    blocks = SIZES["x"] * SIZES["z"]
    chunks = 2 * blocks
    hbm = pl.BlockSpec(memory_space=pl.ANY)
    inputs = [
        tokens, rc_map, step_bias, log_rate, skip_gain, embedding, norm_gain.reshape(1, -1),
        conv_values, conv_states, head_gain.reshape(1, -1), w_states, w_steps.T, w_values, w_gates,
        cotangent,
    ]
    count = len(inputs)
    stores = [
        (pltpu.SMEM if 1 <= n <= 4 else pltpu.VMEM)(a.shape, a.dtype) for n, a in enumerate(inputs)
    ]
    scratch = [
        pltpu.VMEM((chunks, 128), F32),
        pltpu.VMEM((chunks, 128), F32),
        pltpu.VMEM((16 * chunks, 128), F32),
        pltpu.VMEM((8, own, own), F32),
        pltpu.SemaphoreType.DMA((count,)),
        pltpu.VMEM((2, own, inner), BF16),
        pltpu.VMEM((2, own, inner), BF16),
        pltpu.VMEM((2, own, inner), F32),
        pltpu.VMEM((2, own, inner), F32),
        pltpu.VMEM((2, own, inner), F32),
        pltpu.VMEM((own, inner), F32),
        pltpu.VMEM((2, own, own), F32),
        pltpu.VMEM((2, own, inner), BF16),
        pltpu.VMEM((2, own, inner), BF16),
        pltpu.VMEM((2, own, inner), F32),
        pltpu.VMEM((2, 256 + 16, inner), F32),
    ]
    slots = SIZES["c"] + SIZES["x"] * SIZES["y"] + SIZES["z"]
    remote = [
        pltpu.VMEM((SIZES["z"], SIZES["x"], 2, 128), jnp.int32),
        pltpu.VMEM((2, 2, 128), jnp.int32),
        pltpu.VMEM((slots, 9, 128), F32),
        pltpu.VMEM((3, 9, 128), F32),
        pltpu.SemaphoreType.DMA((12,)),
        pltpu.SemaphoreType.DMA((14,)),
        pltpu.SemaphoreType.DMA((slots,)),
        pltpu.SemaphoreType.DMA((slots,)),
    ]
    shapes = (
        pltpu.VMEM((own, inner), BF16),
        pltpu.VMEM((1, all_heads), F32),
        pltpu.VMEM((1, all_heads), F32),
        pltpu.VMEM((4, 256), F32),
    )
    alone = everyone is not None

    def body(*refs):
        refs = list(refs)
        sources, refs = refs[:count], refs[count:]
        if alone:
            links, held, refs = None, refs[0], refs[1:]
            out, refs = refs[:4], refs[4:]
        else:
            out, refs = refs[:4], refs[4:]
            links, held, refs = Links(refs[:8]), refs[0], refs[8:]
        layer_kernel(
            place, links, sources, *out, held, refs[:count], *refs[count:], loss_scale=loss_scale
        )

    if alone:
        params = pltpu.CompilerParams(vmem_limit_bytes=60 * 1024 * 1024)
    else:
        params = pltpu.CompilerParams(
            vmem_limit_bytes=60 * 1024 * 1024, collective_id=0, has_side_effects=True
        )
    return pl.pallas_call(
        body,
        out_shape=shapes,
        in_specs=[hbm] * count + [VM] * alone,
        out_specs=(VM,) * 4,
        scratch_shapes=([] if alone else remote) + stores + scratch,
        compiler_params=params,
        interpret=interpret,
        name="layer",
    )(*inputs, *([everyone] if alone else []))


def emit_kernel(*refs):
    count = len(refs) // 2
    rows = refs[0].shape[0] // 4
    pieces = [(refs[0].at[r : r + rows], refs[count].at[r : r + rows]) for r in range(0, 4 * rows, rows)]
    pieces += [(refs[n], refs[count + n]) for n in range(1, count)]
    copies = [
        pltpu.make_async_copy(source, target, refs[-1].at[n])
        for n, (source, target) in enumerate(pieces)
    ]
    for copy in copies:
        copy.start()
    for copy in copies:
        copy.wait()


def emit(results):
    hbm = pl.BlockSpec(memory_space=pl.ANY)
    return pl.pallas_call(
        emit_kernel,
        out_shape=tuple(jax.ShapeDtypeStruct(r.shape, r.dtype) for r in results),
        in_specs=[VM] * len(results),
        out_specs=(hbm,) * len(results),
        scratch_shapes=[pltpu.SemaphoreType.DMA((len(results) + 3,))],
        name="emit",
    )(*[pltpu.with_memory_space_constraint(r, pltpu.VMEM) for r in results])


def solution(mesh):
    count = mesh.shape["ctx"]

    def on_device(*args):
        own = args[-1].shape[0]
        loss_scale = 1.0 / math.sqrt(own * count * HEAD)

        def place():
            return lax.axis_index("ctx"), lax.axis_index("tp")

        results = layer((args[0].reshape(2, 128),) + args[1:], place, loss_scale)
        encoded, rate, bias, conv = emit(results)
        return encoded, rate.reshape(-1), bias.reshape(-1), conv

    tp = P("tp")
    cols = P(None, "tp")
    in_specs = (
        P("ctx"), P(), P(), P(), cols, cols, P(), cols, cols, P(), tp, tp, tp, tp, P("ctx", "tp"),
    )
    return jax.shard_map(
        on_device, mesh=mesh, in_specs=in_specs,
        out_specs=(P("ctx", "tp"), P(), P(), P()), check_vma=False,
    )
```
